256 devices in a mesh: batch: 8 (over x, core), hidden: 4 (over z_hi), solver: 8 (over z_lo, y).
Axes of the slice: x: 4, y: 4, z: 8 (z_hi: 4, z_lo: 2; z = z_hi * 2 + z_lo), core: 2. Of those that a mesh axis runs over, the one named last changes fastest.
Arguments:
- activations: bfloat16 [2048, 4096], P('batch', ('hidden', 'solver')), may hold values from -16 to 16, as said below
- cotangent: bfloat16 [8192, 2048], P(('hidden', 'solver'), 'batch'), may hold values from -0.13183594 to 0.13183594
- weight: bfloat16 [4096, 8192], P(('hidden', 'solver'), 'batch'), may hold values from -0.09375 to 0.09375
- left_old: float32 [4, 8, 1024, 1024], P('hidden', 'batch'), may hold values from -0.001953125 to 2.0019531, as said below
- right_old: float32 [4, 8, 1024, 1024], P('hidden', 'batch'), may hold values from -0.001953125 to 2.0019531, as said below
Outputs:
- first_out: bfloat16 [8192, 2048], P(('hidden', 'solver'), 'batch')
- new_left: float32 [4, 8, 1024, 1024], P('hidden', 'batch', 'solver')
- new_right: float32 [4, 8, 1024, 1024], P('hidden', 'batch', 'solver')
- direction: float32 [4096, 8192], P(('hidden', 'solver'), 'batch')
- second_out: bfloat16 [8192, 2048], P(('hidden', 'solver'), 'batch')
The draws below stay inside these ranges and needn't reach their ends.
Inputs may be any that keep to these rules, and one draw needn't show every extreme that they name: `activations`: in the hidden draw each feature carries its own scale. `left_old`: every block is symmetric, its diagonal is positive and larger than the sum of the magnitudes of the rest of its row. `right_old`: every block is symmetric, its diagonal is positive and larger than the sum of the magnitudes of the rest of its row.
All inputs are finite; a program needn't handle non-finite values. Where the reference program divides by a largest or mean magnitude, that divisor is 1e-20 or more.
Results may differ from the reference program's by a relative error of at most 0.017.
Values may be sent and summed in bfloat16 or wider, within the bound.
No kernel may reach another device: no remote copies, remote signals or barrier semaphores. Data moves between devices by JAX's collectives and lax.ppermute only.
A program may use at most 128 MiB of HBM per device.

```python
import jax
import jax.numpy as jnp
from jax import lax

DIN = 4096
DOUT = 8192
BLOCK = 1024
TOK_DEV = 256
TOKENS = 2048
NROW = 4
NCOL = 8
N_BATCH = 8


def draw_activations(key, part):
    values = jnp.clip(jax.random.normal(jax.random.fold_in(key, 11), (TOKENS, DIN), jnp.float32), -4.0, 4.0)
    return values.astype(jnp.bfloat16)


def factor_blocks(key):
    diagonal = jnp.exp(jax.random.uniform(jax.random.fold_in(key, 21), (NROW, NCOL, BLOCK), jnp.float32, jnp.log(0.5), jnp.log(2.0)))
    off_part = jnp.clip(jax.random.normal(jax.random.fold_in(key, 22), (NROW, NCOL, BLOCK, BLOCK), jnp.float32), -4.0, 4.0) * (0.5 / BLOCK)
    symmetric = 0.5 * (off_part + jnp.swapaxes(off_part, 2, 3))
    identity = jnp.eye(BLOCK, dtype=jnp.float32)
    return symmetric * (1.0 - identity) + diagonal[..., None] * identity


def draw_left_old(key, part):
    return factor_blocks(jax.random.fold_in(key, 1))


def draw_right_old(key, part):
    return factor_blocks(jax.random.fold_in(key, 2))


def block_scale(stream_key, shape, shards, least, high):
    factor_of, own = 1.0, jax.random.fold_in(stream_key, 6)
    for axis_at, shards_of in shards:
        heights = jnp.exp(jax.random.uniform(jax.random.fold_in(own, axis_at), (shards_of,), jnp.float32, least / len(shards), high / len(shards)))
        factor_of = factor_of * jnp.repeat(heights, shape[axis_at] // shards_of).reshape([-1 if axis == axis_at else 1 for axis in range(len(shape))])
    return factor_of


def normal_values(stream_key, extent, scale, most, split=(), kind=jnp.bfloat16):
    entries = jax.random.normal(stream_key, extent, jnp.float32) * scale
    if len(split) > 0:
        entries = block_scale(stream_key, extent, split, -0.22, 0.18) * entries
    return jnp.clip(entries, min=-most, max=most).astype(kind)


def setup_inputs(seed: int = 0) -> dict:
    splits = jax.random.split(jax.random.key(seed), 6)
    return {
        "activations": draw_activations(jax.random.fold_in(splits[5], 71), 0),
        "cotangent": normal_values(splits[1], (DOUT, TOKENS), (TOKENS ** -0.5), 0.13183594, ((0, 32), (1, 8))),
        "weight": normal_values(splits[2], (DIN, DOUT), DIN ** -0.5, 0.09375, ((0, 32), (1, 8))),
        "left_old": draw_left_old(jax.random.fold_in(splits[5], 71), 0),
        "right_old": draw_right_old(jax.random.fold_in(splits[5], 71), 0),
    }


STAT_DECAY = 0.8
LEARN_RATE = 0.005
EPSILON = 1e-06

def product(left_mat, right_mat):
    return jnp.dot(left_mat, right_mat, precision=lax.Precision.HIGHEST, preferred_element_type=jnp.float32)

def inverse_root(factor):
    identity = jnp.eye(BLOCK, dtype=jnp.float32)
    scaled = 2.5 / (jnp.max(lax.optimization_barrier(jnp.sum(jnp.abs(factor), axis=1))) + EPSILON)
    moment = scaled * factor
    newton_step = (5.0 * identity - moment) * 0.25
    power_term = product(product(product(product(newton_step, newton_step), newton_step), newton_step), moment)
    next_step = (5.0 * identity - power_term) * 0.25
    return scaled ** 0.25 * product(newton_step, next_step)

def forward(activations, weight):
    outputs = lax.dot_general(weight, activations, (((0,), (1,)), ((), ())), preferred_element_type=jnp.float32)
    return outputs.astype(jnp.bfloat16)

def per_block(inputs):
    grad_block, left_block, right_block = inputs
    gram_left = lax.dot_general(grad_block, grad_block, (((0,), (0,)), ((), ())), preferred_element_type=jnp.float32)
    gram_right = lax.dot_general(grad_block, grad_block, (((1,), (1,)), ((), ())), preferred_element_type=jnp.float32)
    left_new = STAT_DECAY * left_block + (1.0 - STAT_DECAY) / BLOCK * gram_left
    right_new = STAT_DECAY * right_block + (1.0 - STAT_DECAY) / BLOCK * gram_right
    grad_float = grad_block.astype(jnp.float32).T
    mixed_rows = product(inverse_root(left_new), grad_float)
    update = product(mixed_rows, inverse_root(right_new))
    spread = jnp.sqrt(jnp.mean(update * update) + EPSILON)
    return (left_new, right_new, update / spread)

def reference(activations, cotangent, weight, left_old, right_old):
    first_out = forward(activations, weight)

    def add_group(carry, group):
        acts = lax.dynamic_slice_in_dim(activations, (group * TOK_DEV).astype(jnp.int32), TOK_DEV, 0)
        cotan = lax.dynamic_slice_in_dim(cotangent, (group * TOK_DEV).astype(jnp.int32), TOK_DEV, 1)
        partial_grad = jnp.dot(cotan, acts, preferred_element_type=jnp.float32)
        return (carry + partial_grad.astype(jnp.bfloat16).astype(jnp.float32), None)
    grad_sum, _ = lax.scan(add_group, jnp.zeros((DOUT, DIN), jnp.float32), jnp.arange(N_BATCH, dtype=jnp.int32))
    grad = grad_sum.astype(jnp.bfloat16)
    blocks = grad.reshape(NCOL, BLOCK, NROW, BLOCK).transpose(2, 0, 1, 3).reshape(NROW * NCOL, BLOCK, BLOCK)
    lefts = left_old.reshape(NROW * NCOL, BLOCK, BLOCK)
    rights = right_old.reshape(NROW * NCOL, BLOCK, BLOCK)
    new_left, new_right, updates = lax.map(per_block, (blocks, lefts, rights))
    new_left = new_left.reshape(NROW, NCOL, BLOCK, BLOCK)
    new_right = new_right.reshape(NROW, NCOL, BLOCK, BLOCK)
    direction = updates.reshape(NROW, NCOL, BLOCK, BLOCK).transpose(0, 2, 1, 3).reshape(DIN, DOUT)
    new_weight = (weight.astype(jnp.float32) - LEARN_RATE * direction).astype(jnp.bfloat16)
    second_out = forward(activations, new_weight)
    return (first_out, new_left, new_right, direction, second_out)
```

```python
import functools

import jax
import jax.numpy as jnp
from jax import lax
from jax.experimental import pallas as pl
from jax.experimental.pallas import tpu as pltpu
from jax.sharding import Mesh
from jax.sharding import PartitionSpec as P

BLOCK = 1024
STAT_DECAY = 0.8
LEARN_RATE = 0.005
EPSILON = 1e-06

AXES = ("x", "c", "zh", "zl", "y")
BATCH = ("x", "c")
ZAX = ("zh", "zl")
SOLVER = ("zl", "y")
PLANE = ("x", "c", "y")
MIB = 1 << 20

SWAP = [
    ((b * 8 + z) * 4 + y, (z * 8 + b) * 4 + y) for b in range(8) for z in range(8) for y in range(4)
]


def copies_to(shard, axis, count):
    copies = jnp.broadcast_to(shard, (count, *shard.shape))
    return lax.all_to_all(copies, axis, split_axis=0, concat_axis=0, tiled=True)


def swap_batch_z(value):
    return lax.ppermute(value, AXES, SWAP)


def dot(a, b):
    return jnp.dot(a, b, preferred_element_type=jnp.float32)


def vmem_call(body, out_shape, scratch=(), smem_args=0, n_args=0, limit=32, name=None):
    in_specs = [pl.BlockSpec(memory_space=pltpu.SMEM)] * smem_args
    in_specs += [pl.BlockSpec(memory_space=pltpu.VMEM)] * n_args
    return pl.pallas_call(
        body,
        out_shape=out_shape,
        in_specs=in_specs,
        out_specs=jax.tree.map(lambda _: pl.BlockSpec(memory_space=pltpu.VMEM), out_shape),
        scratch_shapes=list(scratch),
        compiler_params=pltpu.CompilerParams(vmem_limit_bytes=limit * MIB),
        name=name,
    )


def acts_of(acts_ref, group):
    return jnp.concatenate([acts_ref[group, q] for q in range(4)], axis=1)


def grad_body(cot_ref, acts_ref, out_ref):
    total = dot(cot_ref[0], acts_of(acts_ref, 0))
    for group in range(1, 8):
        total = total + dot(cot_ref[group], acts_of(acts_ref, group))
    out_ref[...] = total.astype(jnp.bfloat16)


def grad_piece(cot_all, acts_all):
    return vmem_call(
        grad_body, jax.ShapeDtypeStruct((256, 512), jnp.bfloat16), n_args=2, name="grad_piece"
    )(cot_all, acts_all)


def forward_groups(weight_t, acts_ref, out_ref):
    for group in range(8):
        out_ref[group] = lax.dot_general(
            weight_t,
            acts_of(acts_ref, group),
            (((1,), (1,)), ((), ())),
            preferred_element_type=jnp.float32,
        ).astype(jnp.bfloat16)


def first_body(weight_ref, acts_ref, out_ref):
    weight = weight_ref[...].reshape(512, 256)
    forward_groups(weight.T, acts_ref, out_ref)


def second_body(squares_ref, weight_ref, update_ref, acts_ref, out_ref):
    mean = jnp.sum(squares_ref[...], axis=0)[:1, :1] / (BLOCK * BLOCK)
    rate = LEARN_RATE / jnp.sqrt(mean + EPSILON)
    weight = weight_ref[...].reshape(512, 256).astype(jnp.float32)
    update = update_ref[...].reshape(512, 256).astype(jnp.float32)
    new_weight = (weight - rate * update).astype(jnp.bfloat16)
    forward_groups(new_weight.T, acts_ref, out_ref)


PARTIAL = jax.ShapeDtypeStruct((8, 256, 256), jnp.bfloat16)


def first_partial(weight_cols, acts_all):
    return vmem_call(first_body, PARTIAL, n_args=2, name="first_partial")(weight_cols, acts_all)


def second_partial(squares, weight_cols, update_cols, acts_all):
    return vmem_call(second_body, PARTIAL, n_args=4, name="second_partial")(
        squares, weight_cols, update_cols, acts_all
    )


def statistics(lhs_ref, rhs_ref, old_ref, full_ref, off_ref):
    tile = 256
    sums = jnp.zeros((1, BLOCK), jnp.float32)
    diag = jnp.zeros((1, BLOCK), jnp.float32)
    for i in range(BLOCK // tile):
        rows = pl.ds(i * tile, tile)
        gram = dot(lhs_ref[rows, :], rhs_ref[...])
        new = STAT_DECAY * old_ref[rows, :] + (1.0 - STAT_DECAY) / BLOCK * gram
        full_ref[rows, :] = new
        sums = sums + jnp.sum(jnp.abs(new), axis=0, keepdims=True)
        row = lax.broadcasted_iota(jnp.int32, (tile, BLOCK), 0) + i * tile
        col = lax.broadcasted_iota(jnp.int32, (tile, BLOCK), 1)
        on_diag = row == col
        diag = diag + jnp.sum(jnp.where(on_diag, new, 0.0), axis=0, keepdims=True)
        off_ref[rows, :] = jnp.where(on_diag, 0.0, new).astype(jnp.bfloat16)
    scale = 2.5 / (jnp.max(sums, axis=1, keepdims=True) + EPSILON)
    return scale, diag


def times_factor(rows, off_ref, diag):
    return rows * diag + dot(rows.astype(jnp.bfloat16), off_ref[...])


def times_root(start, off_ref, diag, quarter):
    value = start
    for _ in range(4):
        value = 1.25 * value - quarter * times_factor(value, off_ref, diag)
    return 1.25 * start - quarter * times_factor(value, off_ref, diag)


def solver_body(
    place_ref,
    pieces_ref,
    left_old_ref,
    right_old_ref,
    new_left_ref,
    new_right_ref,
    update_ref,
    sent_ref,
    squares_ref,
    grad_ref,
    grad_t_ref,
    full_ref,
    off_left_ref,
    off_right_ref,
):
    first = pl.multiple_of(place_ref[0] * 128, 128)
    own = pl.ds(first, 128)
    for zl in range(2):
        for y in range(4):
            piece = pieces_ref[zl * 4 + y]
            grad_ref[pl.ds(y * 256, 256), pl.ds(zl * 512, 512)] = piece
            grad_t_ref[pl.ds(zl * 512, 512), pl.ds(y * 256, 256)] = piece.T
    scale_left, diag_left = statistics(grad_t_ref, grad_ref, left_old_ref, full_ref, off_left_ref)
    left_rows = full_ref[own, :]
    new_left_ref[...] = left_rows
    scale_right, diag_right = statistics(
        grad_ref, grad_t_ref, right_old_ref, full_ref, off_right_ref
    )
    new_right_ref[...] = full_ref[own, :]
    quarter_left = scale_left * 0.25
    quarter_right = scale_right * 0.25
    row = lax.broadcasted_iota(jnp.int32, (128, BLOCK), 0) + first
    col = lax.broadcasted_iota(jnp.int32, (128, BLOCK), 1)
    start = jnp.where(row == col, 1.25, 0.0) - quarter_left * left_rows
    root = jnp.sqrt(jnp.sqrt(scale_left)) * times_root(start, off_left_ref, diag_left, quarter_left)
    high = root.astype(jnp.bfloat16)
    low = (root - high.astype(jnp.float32)).astype(jnp.bfloat16)
    both = dot(jnp.concatenate([high, low], axis=0), grad_t_ref[...])
    mixed = both[:128] + both[128:]
    turned = 1.25 * mixed - quarter_right * times_factor(mixed, off_right_ref, diag_right)
    update = jnp.sqrt(jnp.sqrt(scale_right)) * times_root(
        turned, off_right_ref, diag_right, quarter_right
    )
    update_ref[...] = update
    for y in range(4):
        sent_ref[y] = update[:, y * 256 : (y + 1) * 256].astype(jnp.bfloat16)
    squares = jnp.sum(jnp.sum(update * update, axis=0, keepdims=True), axis=1, keepdims=True)
    squares_ref[...] = jnp.broadcast_to(squares, (8, 128))


def solve(place, pieces, left_old, right_old):
    shape = jax.ShapeDtypeStruct
    return vmem_call(
        solver_body,
        (
            shape((128, BLOCK), jnp.float32),
            shape((128, BLOCK), jnp.float32),
            shape((128, BLOCK), jnp.float32),
            shape((4, 128, 256), jnp.bfloat16),
            shape((8, 128), jnp.float32),
        ),
        scratch=[
            pltpu.VMEM((BLOCK, BLOCK), jnp.bfloat16),
            pltpu.VMEM((BLOCK, BLOCK), jnp.bfloat16),
            pltpu.VMEM((BLOCK, BLOCK), jnp.float32),
            pltpu.VMEM((BLOCK, BLOCK), jnp.bfloat16),
            pltpu.VMEM((BLOCK, BLOCK), jnp.bfloat16),
        ],
        smem_args=1,
        n_args=3,
        limit=40,
        name="solve",
    )(place, pieces, left_old, right_old)


def finish(partial):
    arrived = lax.all_to_all(partial, ZAX, split_axis=0, concat_axis=0, tiled=True)
    return swap_batch_z(arrived.astype(jnp.float32).sum(axis=0).astype(jnp.bfloat16))


def body(activations, cotangent, weight, left_old, right_old):
    cot_turned = swap_batch_z(cotangent)
    acts_all = copies_to(activations, PLANE, 32).reshape(8, 4, 256, 128)
    cot_all = copies_to(cot_turned, ZAX, 8)
    weight_parts = jnp.transpose(weight.reshape(128, 4, 256), (1, 0, 2))
    weight_cols = lax.all_to_all(weight_parts, "y", split_axis=0, concat_axis=0, tiled=True)
    piece = grad_piece(cot_all, acts_all)
    pieces = copies_to(piece, SOLVER, 8)
    first_out = finish(first_partial(weight_cols, acts_all))
    place = (lax.axis_index("zl") * 4 + lax.axis_index("y")).astype(jnp.int32).reshape(1)
    new_left, new_right, update, sent, squares = solve(
        place, pieces, left_old[0, 0], right_old[0, 0]
    )
    update_cols = lax.all_to_all(sent, "y", split_axis=0, concat_axis=0, tiled=True)
    squares_all = copies_to(squares, SOLVER, 8)
    second_out = finish(second_partial(squares_all, weight_cols, update_cols, acts_all))
    total = jnp.sum(squares_all[:, 0, 0])
    direction = update / jnp.sqrt(total / (BLOCK * BLOCK) + EPSILON)
    return (first_out, new_left[None, None], new_right[None, None], direction, second_out)


def solution(mesh):
    fine = Mesh(mesh.devices.reshape(4, 2, 4, 2, 4), AXES)
    rows = ("zh", "zl", "y")
    in_specs = (
        P(BATCH, rows),
        P(rows, BATCH),
        P(rows, BATCH),
        P("zh", BATCH, None, None),
        P("zh", BATCH, None, None),
    )
    out_specs = (
        P(rows, BATCH),
        P("zh", BATCH, SOLVER, None),
        P("zh", BATCH, SOLVER, None),
        P(rows, BATCH),
        P(rows, BATCH),
    )
    return jax.shard_map(body, mesh=fine, in_specs=in_specs, out_specs=out_specs, check_vma=False)
```

```python
import jax
import jax.numpy as jnp
from jax import lax
from jax.experimental import pallas as pl
from jax.experimental.pallas import tpu as pltpu
from jax.sharding import Mesh
from jax.sharding import PartitionSpec as P

BLOCK = 1024
STAT_DECAY = 0.8
LEARN_RATE = 0.005
EPSILON = 1e-06

AXES = ("x", "c", "zh", "zl", "y")
BATCH = ("x", "c")
ZAX = ("zh", "zl")
SOLVER = ("zl", "y")
MIB = 1 << 20
SHAPE = jax.ShapeDtypeStruct
BF16 = jnp.bfloat16
F32 = jnp.float32


def device(x, c, zh, zl, y):
    return (((x * 2 + c) * 4 + zh) * 2 + zl) * 4 + y


EVERY = [
    (x, c, zh, zl, y)
    for x in range(4)
    for c in range(2)
    for zh in range(4)
    for zl in range(2)
    for y in range(4)
]
SWAP = [(device(*d), device(d[2], d[3], d[0], d[1], d[4])) for d in EVERY]
HOME = [
    [(device(*d), device(d[2], d[3] ^ e, d[0], d[1], d[4])) for d in EVERY] for e in range(2)
]
FLIP = [(0, 1), (1, 0)]


def shift(by):
    return [(i, (i + by) % 4) for i in range(4)]


def copies_to(shard, axis, count):
    copies = jnp.broadcast_to(shard, (count, *shard.shape))
    return lax.all_to_all(copies, axis, split_axis=0, concat_axis=0, tiled=True)


def dot(a, b):
    return jnp.dot(a, b, preferred_element_type=F32)


def dot_minor(a, b):
    return lax.dot_general(a, b, (((1,), (1,)), ((), ())), preferred_element_type=F32)


def vmem_call(body, out_shape, n_args, scratch=(), limit=32, name=None):
    in_specs = [pl.BlockSpec(memory_space=pltpu.SMEM)]
    in_specs += [pl.BlockSpec(memory_space=pltpu.VMEM)] * n_args
    return pl.pallas_call(
        body,
        out_shape=out_shape,
        in_specs=in_specs,
        out_specs=jax.tree.map(lambda _: pl.BlockSpec(memory_space=pltpu.VMEM), out_shape),
        scratch_shapes=list(scratch),
        compiler_params=pltpu.CompilerParams(vmem_limit_bytes=limit * MIB),
        name=name,
    )


def wide(slab):
    return jnp.concatenate([slab[q] for q in range(4)], axis=1)


def grad_body(place, cot_ref, *refs):
    own, swapped, out_ref, packed_ref = refs[:4], refs[4:8], refs[8], refs[9]
    x, c = place[0], place[1]
    total = jnp.zeros((256, 512), F32)
    for d in range(4):
        at = ((x - d) & 3) * 2
        mine = own[d][...]
        packed_ref[d] = mine
        total = total + dot(cot_ref[at + c], wide(mine))
        total = total + dot(cot_ref[at + 1 - c], wide(swapped[d][...]))
    piece = total.astype(BF16)
    for s in range(8):
        out_ref[s] = piece


def grad_piece(place, cot_all, own, swapped):
    return vmem_call(
        grad_body,
        (SHAPE((8, 256, 512), BF16), SHAPE((4, 4, 256, 128), BF16)),
        n_args=9,
        name="grad_piece",
    )(place, cot_all, *own, *swapped)


def forward_groups(place, near_t, far_t, near_refs, far_refs, out_ref):
    x, c = place[0], place[1]
    near0, near1 = near_refs
    far0, far1 = far_refs
    for d in range(4):
        at = (x - d) & 3
        out_ref[at, c] = (
            dot_minor(near_t, wide(near0[d])) + dot_minor(far_t, wide(far0[d]))
        ).astype(BF16)
        out_ref[at, 1 - c] = (
            dot_minor(near_t, wide(near1[d][...])) + dot_minor(far_t, wide(far1[d]))
        ).astype(BF16)


def weight_of(place, mixed_ref, far_ref):
    start = pl.multiple_of(256 + place[3] * 128, 128)
    near = jnp.concatenate([mixed_ref[q, pl.ds(start, 128), :] for q in range(4)], axis=0)
    far = jnp.concatenate([far_ref[q] for q in range(4)], axis=0)
    return near, far


def first_body(place, mixed_ref, far_ref, near0, n0, n1, n2, n3, far0, far1, *refs):
    outs, work = refs[:4], refs[4]
    near, far = weight_of(place, mixed_ref, far_ref)
    forward_groups(place, near.T, far.T, (near0, (n0, n1, n2, n3)), (far0, far1), work)
    for e in range(4):
        outs[e][...] = work[(place[2] + e) & 3]


def second_body(
    place, update_ref, mixed_ref, far_ref, near0, n0, n1, n2, n3, far0, far1, out_ref, spread_ref
):
    near, far = weight_of(place, mixed_ref, far_ref)
    squares = jnp.zeros((16, 128), F32)
    for s in range(8):
        squares = squares + update_ref[s, 128:144, :].astype(F32)
    mean = jnp.sum(squares, axis=0, keepdims=True)[:, :1] / (BLOCK * BLOCK)
    spread = jnp.sqrt(mean + EPSILON)
    spread_ref[...] = jnp.broadcast_to(spread, (8, 128))
    rate = LEARN_RATE / spread
    zl = place[3]

    def changed(weight, first):
        update = jnp.concatenate([update_ref[first + q, :128, :] for q in range(4)], axis=0)
        return (weight.astype(F32) - rate * update.astype(F32)).astype(BF16).T

    near_t = changed(near, zl * 4)
    far_t = changed(far, (1 - zl) * 4)
    forward_groups(place, near_t, far_t, (near0, (n0, n1, n2, n3)), (far0, far1), out_ref)


def first_partial(place, weights, acts):
    part = SHAPE((2, 128, 256), BF16)
    return vmem_call(
        first_body,
        (part, part, part, part),
        n_args=9,
        scratch=[pltpu.VMEM((4, 2, 128, 256), BF16)],
        name="first_partial",
    )(place, *weights, *acts)


def second_partial(place, update_cols, weights, acts):
    return vmem_call(
        second_body,
        (SHAPE((4, 2, 128, 256), BF16), SHAPE((8, 128), F32)),
        n_args=10,
        name="second_partial",
    )(place, update_cols, *weights, *acts)


def add_body(place, *refs):
    parts, outs = refs[:-3], refs[-3:]
    zl, work = place[3], outs[2]
    if len(parts) == 1:
        parts = [parts[0].at[i] for i in range(4)]
    total = parts[0][...].astype(F32)
    for part in parts[1:]:
        total = total + part[...].astype(F32)
    work[...] = total.astype(BF16)
    outs[0][...] = work[zl]
    outs[1][...] = work[1 - zl]


def add_up(place, *parts):
    half = SHAPE((128, 256), BF16)
    return vmem_call(
        add_body,
        (half, half),
        n_args=len(parts),
        scratch=[pltpu.VMEM((2, 128, 256), BF16)],
        name="add_up",
    )(place, *parts)


def send_home(halves):
    straight = lax.ppermute(halves[0], AXES, HOME[0])
    crossed = lax.ppermute(halves[1], AXES, HOME[1])
    even = lax.axis_index("c") == 0
    return jnp.concatenate(
        [jnp.where(even, straight, crossed), jnp.where(even, crossed, straight)], axis=0
    )


def statistics(lhs_ref, rhs_ref, old_ref, full_ref, off_ref):
    tile = 256
    sums = jnp.zeros((1, BLOCK), F32)
    diag = jnp.zeros((1, BLOCK), F32)
    for i in range(BLOCK // tile):
        rows = pl.ds(i * tile, tile)
        gram = dot(lhs_ref[rows, :], rhs_ref[...])
        new = STAT_DECAY * old_ref[rows, :] + (1.0 - STAT_DECAY) / BLOCK * gram
        full_ref[rows, :] = new
        sums = sums + jnp.sum(jnp.abs(new), axis=0, keepdims=True)
        row = lax.broadcasted_iota(jnp.int32, (tile, BLOCK), 0) + i * tile
        col = lax.broadcasted_iota(jnp.int32, (tile, BLOCK), 1)
        on_diag = row == col
        diag = diag + jnp.sum(jnp.where(on_diag, new, 0.0), axis=0, keepdims=True)
        off_ref[rows, :] = jnp.where(on_diag, 0.0, new).astype(BF16)
    scale = 2.5 / (jnp.max(sums, axis=1, keepdims=True) + EPSILON)
    return scale, diag


def times_factor(rows, off_ref, diag):
    return rows * diag + dot(rows.astype(BF16), off_ref[...])


def times_root(start, off_ref, diag, quarter):
    value = start
    for _ in range(4):
        value = 1.25 * value - quarter * times_factor(value, off_ref, diag)
    return 1.25 * start - quarter * times_factor(value, off_ref, diag)


def solver_body(
    place,
    pieces_ref,
    left_old_ref,
    right_old_ref,
    new_left_ref,
    new_right_ref,
    update_ref,
    sent_ref,
    grad_ref,
    grad_t_ref,
    full_ref,
    off_left_ref,
    off_right_ref,
):
    first = pl.multiple_of((place[3] * 4 + place[4]) * 128, 128)
    own = pl.ds(first, 128)
    for zl in range(2):
        for y in range(4):
            piece = pieces_ref[zl * 4 + y]
            grad_ref[pl.ds(y * 256, 256), pl.ds(zl * 512, 512)] = piece
            grad_t_ref[pl.ds(zl * 512, 512), pl.ds(y * 256, 256)] = piece.T
    scale_left, diag_left = statistics(grad_t_ref, grad_ref, left_old_ref, full_ref, off_left_ref)
    left_rows = full_ref[own, :]
    new_left_ref[...] = left_rows
    scale_right, diag_right = statistics(
        grad_ref, grad_t_ref, right_old_ref, full_ref, off_right_ref
    )
    new_right_ref[...] = full_ref[own, :]
    quarter_left = scale_left * 0.25
    quarter_right = scale_right * 0.25
    row = lax.broadcasted_iota(jnp.int32, (128, BLOCK), 0) + first
    col = lax.broadcasted_iota(jnp.int32, (128, BLOCK), 1)
    start = jnp.where(row == col, 1.25, 0.0) - quarter_left * left_rows
    root = jnp.sqrt(jnp.sqrt(scale_left)) * times_root(start, off_left_ref, diag_left, quarter_left)
    high = root.astype(BF16)
    low = (root - high.astype(F32)).astype(BF16)
    both = dot(jnp.concatenate([high, low], axis=0), grad_t_ref[...])
    mixed = both[:128] + both[128:]
    turned = 1.25 * mixed - quarter_right * times_factor(mixed, off_right_ref, diag_right)
    update = jnp.sqrt(jnp.sqrt(scale_right)) * times_root(
        turned, off_right_ref, diag_right, quarter_right
    )
    update_ref[...] = update
    squares = jnp.sum(jnp.sum(update * update, axis=0, keepdims=True), axis=1, keepdims=True)
    high = squares.astype(BF16).astype(F32)
    middle = (squares - high).astype(BF16).astype(F32)
    low = squares - high - middle
    row = lax.broadcasted_iota(jnp.int32, (16, 128), 0)
    tail = jnp.where(row == 0, high, jnp.where(row == 1, middle, jnp.where(row == 2, low, 0.0)))
    tail = tail.astype(BF16)
    for zl in range(2):
        for y in range(4):
            at = y * 256 + zl * 128
            sent_ref[zl * 4 + y, :128, :] = update[:, at : at + 128].astype(BF16)
            sent_ref[zl * 4 + y, 128:, :] = tail


def solve(place, pieces, left_old, right_old):
    square = (BLOCK, BLOCK)
    return vmem_call(
        solver_body,
        (
            SHAPE((128, BLOCK), F32),
            SHAPE((128, BLOCK), F32),
            SHAPE((128, BLOCK), F32),
            SHAPE((8, 144, 128), BF16),
        ),
        n_args=3,
        scratch=[pltpu.VMEM(square, kind) for kind in (BF16, BF16, F32, BF16, BF16)],
        limit=40,
        name="solve",
    )(place, pieces, left_old, right_old)


def body(activations, cotangent, weight, left_old, right_old):
    place = jnp.stack([lax.axis_index(a).astype(jnp.int32) for a in AXES])
    cot_turned = lax.ppermute(cotangent, AXES, SWAP)
    acts_copies = jnp.broadcast_to(activations, (4, 256, 128))
    weight_parts = jnp.transpose(weight.reshape(128, 4, 2, 128), (1, 2, 0, 3)).reshape(4, 256, 128)
    mixed = lax.all_to_all(
        jnp.concatenate([acts_copies, weight_parts], axis=1), "y", 0, 0, tiled=True
    )
    own = [mixed[:, :256]]
    own += [lax.ppermute(own[0], "x", shift(d)) for d in range(1, 4)]
    swapped = [lax.ppermute(slab, "c", FLIP) for slab in own]
    leaving = lax.dynamic_slice_in_dim(mixed, 256 + (1 - lax.axis_index("zl")) * 128, 128, 1)
    weight_far = lax.ppermute(leaving, "zl", FLIP)
    cot_all = copies_to(cot_turned, ZAX, 8)
    copies, packed = grad_piece(place, cot_all, own, swapped)
    far = lax.ppermute(packed, "zl", FLIP)
    far_swapped = lax.ppermute(far, "c", FLIP)
    weights = (mixed, weight_far)
    acts = (packed, *swapped, far, far_swapped)

    pieces = lax.all_to_all(copies, SOLVER, 0, 0, tiled=True)
    new_left, new_right, update, sent = solve(place, pieces, left_old[0, 0], right_old[0, 0])
    update_cols = lax.all_to_all(sent, SOLVER, 0, 0, tiled=True)

    parts = first_partial(place, weights, acts)
    parts = [parts[0]] + [lax.ppermute(parts[e], "zh", shift(e)) for e in range(1, 4)]
    first_out = send_home(add_up(place, *parts))

    second, spread = second_partial(place, update_cols, weights, acts)
    arrived = lax.all_to_all(second, "zh", 0, 0, tiled=True)
    second_out = send_home(add_up(place, arrived))
    direction = update / spread[0, 0]
    return (first_out, new_left[None, None], new_right[None, None], direction, second_out)


def solution(mesh):
    fine = Mesh(mesh.devices.reshape(4, 2, 4, 2, 4), AXES)
    rows = ("zh", "zl", "y")
    in_specs = (
        P(BATCH, rows),
        P(rows, BATCH),
        P(rows, BATCH),
        P("zh", BATCH, None, None),
        P("zh", BATCH, None, None),
    )
    out_specs = (
        P(rows, BATCH),
        P("zh", BATCH, SOLVER, None),
        P("zh", BATCH, SOLVER, None),
        P(rows, BATCH),
        P(rows, BATCH),
    )
    return jax.shard_map(body, mesh=fine, in_specs=in_specs, out_specs=out_specs, check_vma=False)
```

```python
import jax
import jax.numpy as jnp
from jax import lax
from jax.experimental import pallas as pl
from jax.experimental.pallas import tpu as pltpu
from jax.sharding import Mesh
from jax.sharding import PartitionSpec as P

BLOCK = 1024
STAT_DECAY = 0.8
LEARN_RATE = 0.005
EPSILON = 1e-06

AXES = ("x", "c", "zh", "zl", "y")
BATCH = ("x", "c")
ZAX = ("zh", "zl")
SOLVER = ("zl", "y")
MIB = 1 << 20
SHAPE = jax.ShapeDtypeStruct
BF16 = jnp.bfloat16
F32 = jnp.float32


def device(x, c, zh, zl, y):
    return (((x * 2 + c) * 4 + zh) * 2 + zl) * 4 + y


EVERY = [
    (x, c, zh, zl, y)
    for x in range(4)
    for c in range(2)
    for zh in range(4)
    for zl in range(2)
    for y in range(4)
]
SWAP = [(device(*d), device(d[2], d[3], d[0], d[1], d[4])) for d in EVERY]
FLIP = [(0, 1), (1, 0)]


def shift(by):
    return [(i, (i + by) % 4) for i in range(4)]


def copies_to(shard, axis, count):
    copies = jnp.broadcast_to(shard, (count, *shard.shape))
    return lax.all_to_all(copies, axis, split_axis=0, concat_axis=0, tiled=True)


def dot(a, b):
    return jnp.dot(a, b, preferred_element_type=F32)


def dot_minor(a, b):
    return lax.dot_general(a, b, (((1,), (1,)), ((), ())), preferred_element_type=F32)


VMEM = pl.BlockSpec(memory_space=pltpu.VMEM)
HBM = pl.BlockSpec(memory_space=pltpu.HBM)


def call(body, in_specs, out_specs, out_shape, scratch=(), limit=24, name=None):
    return pl.pallas_call(
        body,
        out_shape=out_shape,
        in_specs=[pl.BlockSpec(memory_space=pltpu.SMEM), *in_specs],
        out_specs=out_specs,
        scratch_shapes=list(scratch),
        compiler_params=pltpu.CompilerParams(vmem_limit_bytes=limit * MIB),
        name=name,
    )


def wide(slab):
    return jnp.concatenate([slab[q] for q in range(4)], axis=1)


def order_body(place, *refs):
    for d in range(4):
        refs[4][(place[4] - d) & 3] = refs[d][...]


def in_order(place, parts):
    shape = SHAPE((4, *parts[0].shape), BF16)
    return call(order_body, [VMEM] * 4, VMEM, shape, limit=8, name="in_order")(place, *parts)


def columns_body(place, weight_ref, *refs):
    outs, work = refs[:4], refs[4]
    for q in range(4):
        work[q] = weight_ref[:, q * 256 : (q + 1) * 256]
    for d in range(4):
        outs[d][...] = work[(place[4] + d) & 3]


def columns(place, weight):
    part = SHAPE((128, 256), BF16)
    return call(
        columns_body,
        [VMEM],
        [VMEM] * 4,
        [part] * 4,
        scratch=[pltpu.VMEM((4, 128, 256), BF16)],
        limit=8,
        name="columns",
    )(place, weight)


def grad_body(place, cot_ref, *refs):
    own, swapped = refs[:4], refs[4:8]
    copies_ref, near_ref, away_ref, piece_ref, near_buf, away_buf, sems = refs[8:]
    x, c, zl = place[0], place[1], place[3]
    total = jnp.zeros((256, 512), F32)
    for d in range(4):
        at = (x - d) & 3
        mine, theirs = own[d][...], swapped[d][...]
        near_buf[at] = jnp.where(c == zl, mine, theirs)
        away_buf[at] = jnp.where(c == zl, theirs, mine)
        total = total + dot(cot_ref[at * 2 + c], wide(mine))
        total = total + dot(cot_ref[at * 2 + 1 - c], wide(theirs))
    piece_ref[...] = total.astype(BF16)
    sends = [
        pltpu.make_async_copy(piece_ref, copies_ref.at[s], sems.at[s]) for s in range(8)
    ]
    sends.append(pltpu.make_async_copy(near_buf, near_ref, sems.at[8]))
    sends.append(pltpu.make_async_copy(away_buf.at[pl.ds(c * 2, 2)], away_ref, sems.at[9]))
    for send in sends:
        send.start()
    for send in sends:
        send.wait()


def grad_piece(place, cot_all, own, swapped):
    return call(
        grad_body,
        [VMEM] * 9,
        [HBM] * 3,
        [
            pltpu.HBM((8, 256, 512), BF16),
            pltpu.HBM((4, 4, 256, 128), BF16),
            pltpu.HBM((2, 4, 256, 128), BF16),
        ],
        scratch=[
            pltpu.VMEM((256, 512), BF16),
            pltpu.VMEM((4, 4, 256, 128), BF16),
            pltpu.VMEM((4, 4, 256, 128), BF16),
            pltpu.SemaphoreType.DMA((10,)),
        ],
        limit=10,
        name="grad_piece",
    )(place, cot_all, *own, *swapped)


def forward_groups(place, near_t, far_t, near_ref, far_refs, out_ref):
    c = place[1]
    for i in range(2):
        for j in range(2):
            at = (c * 2 if i == 0 else 2 - c * 2) + j
            total = dot_minor(near_t, wide(near_ref.at[at]))
            total = total + dot_minor(far_t, wide(far_refs[i].at[j]))
            out_ref[at] = total.astype(BF16)


def first_body(place, near_w, far_w, near_ref, far0, far1, *refs):
    outs, work = refs[:4], refs[4]
    near_t = near_w[...].reshape(512, 256).T
    far_t = far_w[...].reshape(512, 256).T
    forward_groups(place, near_t, far_t, near_ref, (far0, far1), work)
    for e in range(4):
        outs[e][...] = work[(place[2] + e) & 3]


def second_body(place, update_ref, near_w, far_w, near_ref, far0, far1, out_ref, spread_ref):
    squares = jnp.zeros((16, 128), F32)
    for s in range(8):
        squares = squares + update_ref[s, 128:144, :128].astype(F32)
    mean = jnp.sum(squares, axis=0, keepdims=True)[:, :1] / (BLOCK * BLOCK)
    spread = jnp.sqrt(mean + EPSILON)
    spread_ref[...] = jnp.broadcast_to(spread, (8, 128))
    rate = LEARN_RATE / spread
    zl = place[3]

    def changed(weight, first):
        update = jnp.concatenate([update_ref[first + q, :128, :] for q in range(4)], axis=0)
        weight = weight[...].reshape(512, 256)
        return (weight.astype(F32) - rate * update.astype(F32)).astype(BF16).T

    near_t = changed(near_w, zl * 4)
    far_t = changed(far_w, 4 - zl * 4)
    forward_groups(place, near_t, far_t, near_ref, (far0, far1), out_ref)


def first_partial(place, weights, acts):
    part = SHAPE((256, 256), BF16)
    return call(
        first_body,
        [VMEM] * 5,
        [VMEM] * 4,
        [part] * 4,
        scratch=[pltpu.VMEM((4, 256, 256), BF16)],
        limit=12,
        name="first_partial",
    )(place, *weights, *acts)


def second_partial(place, update_cols, weights, acts):
    return call(
        second_body,
        [VMEM] * 6,
        [VMEM] * 2,
        [SHAPE((4, 256, 256), BF16), SHAPE((8, 128), F32)],
        limit=12,
        name="second_partial",
    )(place, update_cols, *weights, *acts)


def add_body(place, *refs):
    parts = refs[:-1]
    if len(parts) == 1:
        parts = [parts[0].at[i] for i in range(4)]
    total = parts[0][...].astype(F32)
    for part in parts[1:]:
        total = total + part[...].astype(F32)
    refs[-1][...] = total.astype(BF16)


def add_up(place, *parts):
    return call(
        add_body, [VMEM] * len(parts), VMEM, SHAPE((256, 256), BF16), limit=8, name="add_up"
    )(place, *parts)


def statistics(lhs_ref, rhs_ref, old_ref, full_ref, off_ref):
    tile = 256
    sums = jnp.zeros((1, BLOCK), F32)
    diag = jnp.zeros((1, BLOCK), F32)
    for i in range(BLOCK // tile):
        rows = pl.ds(i * tile, tile)
        gram = dot(lhs_ref[rows, :], rhs_ref[...])
        new = STAT_DECAY * old_ref[rows, :] + (1.0 - STAT_DECAY) / BLOCK * gram
        full_ref[rows, :] = new
        sums = sums + jnp.sum(jnp.abs(new), axis=0, keepdims=True)
        row = lax.broadcasted_iota(jnp.int32, (tile, BLOCK), 0) + i * tile
        col = lax.broadcasted_iota(jnp.int32, (tile, BLOCK), 1)
        on_diag = row == col
        diag = diag + jnp.sum(jnp.where(on_diag, new, 0.0), axis=0, keepdims=True)
        off_ref[rows, :] = jnp.where(on_diag, 0.0, new).astype(BF16)
    scale = 2.5 / (jnp.max(sums, axis=1, keepdims=True) + EPSILON)
    return scale, diag


def times_factor(rows, off_ref, diag):
    return rows * diag + dot(rows.astype(BF16), off_ref[...])


def times_root(start, off_ref, diag, quarter):
    value = start
    for _ in range(4):
        value = 1.25 * value - quarter * times_factor(value, off_ref, diag)
    return 1.25 * start - quarter * times_factor(value, off_ref, diag)


def solver_body(
    place,
    pieces_ref,
    left_old_ref,
    right_old_ref,
    new_left_ref,
    new_right_ref,
    update_ref,
    sent_ref,
    left_buf,
    right_buf,
    grad_ref,
    grad_t_ref,
    full_ref,
    off_left_ref,
    off_right_ref,
    rows_buf,
    update_buf,
    sent_buf,
    sems,
):
    load_left = pltpu.make_async_copy(left_old_ref, left_buf, sems.at[0])
    load_right = pltpu.make_async_copy(right_old_ref, right_buf, sems.at[1])
    load_left.start()
    load_right.start()
    first = pl.multiple_of((place[3] * 4 + place[4]) * 128, 128)
    own = pl.ds(first, 128)
    for zl in range(2):
        for y in range(4):
            piece = pieces_ref[zl * 4 + y]
            grad_ref[pl.ds(y * 256, 256), pl.ds(zl * 512, 512)] = piece
            grad_t_ref[pl.ds(zl * 512, 512), pl.ds(y * 256, 256)] = piece.T
    load_left.wait()
    scale_left, diag_left = statistics(grad_t_ref, grad_ref, left_buf, full_ref, off_left_ref)
    left_rows = full_ref[own, :]
    rows_buf[...] = left_rows
    store_left = pltpu.make_async_copy(rows_buf, new_left_ref, sems.at[2])
    store_left.start()
    load_right.wait()
    scale_right, diag_right = statistics(
        grad_ref, grad_t_ref, right_buf, full_ref, off_right_ref
    )
    store_right = pltpu.make_async_copy(full_ref.at[own, :], new_right_ref, sems.at[3])
    store_right.start()
    quarter_left = scale_left * 0.25
    quarter_right = scale_right * 0.25
    row = lax.broadcasted_iota(jnp.int32, (128, BLOCK), 0) + first
    col = lax.broadcasted_iota(jnp.int32, (128, BLOCK), 1)
    start = jnp.where(row == col, 1.25, 0.0) - quarter_left * left_rows
    root = jnp.sqrt(jnp.sqrt(scale_left)) * times_root(start, off_left_ref, diag_left, quarter_left)
    high = root.astype(BF16)
    low = (root - high.astype(F32)).astype(BF16)
    both = dot(jnp.concatenate([high, low], axis=0), grad_t_ref[...])
    mixed = both[:128] + both[128:]
    turned = 1.25 * mixed - quarter_right * times_factor(mixed, off_right_ref, diag_right)
    update = jnp.sqrt(jnp.sqrt(scale_right)) * times_root(
        turned, off_right_ref, diag_right, quarter_right
    )
    squares = jnp.sum(jnp.sum(update * update, axis=0, keepdims=True), axis=1, keepdims=True)
    high = squares.astype(BF16).astype(F32)
    middle = (squares - high).astype(BF16).astype(F32)
    low = squares - high - middle
    row = lax.broadcasted_iota(jnp.int32, (16, 256), 0)
    tail = jnp.where(row == 0, high, jnp.where(row == 1, middle, jnp.where(row == 2, low, 0.0)))
    tail = tail.astype(BF16)
    for y in range(4):
        sent_buf[y, :128, :] = update[:, y * 256 : (y + 1) * 256].astype(BF16)
        sent_buf[y, 128:, :] = tail
    stores = [
        pltpu.make_async_copy(sent_buf, sent_ref.at[pl.ds(zl * 4, 4)], sems.at[4 + zl])
        for zl in range(2)
    ]
    for store in stores:
        store.start()
    update_buf[...] = update
    stores.append(pltpu.make_async_copy(update_buf, update_ref, sems.at[6]))
    stores[-1].start()
    for store in [store_left, store_right, *stores]:
        store.wait()


def solve(place, pieces, left_old, right_old):
    square = (BLOCK, BLOCK)
    rows = pltpu.HBM((128, BLOCK), F32)
    return call(
        solver_body,
        [VMEM, HBM, HBM],
        [HBM] * 4,
        [rows, rows, rows, pltpu.HBM((8, 144, 256), BF16)],
        scratch=[
            *[pltpu.VMEM(square, kind) for kind in (F32, F32, BF16, BF16, F32, BF16, BF16)],
            pltpu.VMEM((128, BLOCK), F32),
            pltpu.VMEM((128, BLOCK), F32),
            pltpu.VMEM((4, 144, 256), BF16),
            pltpu.SemaphoreType.DMA((7,)),
        ],
        limit=30,
        name="solve",
    )(place, pieces, left_old, right_old)


def body(activations, cotangent, weight, left_old, right_old):
    place = jnp.stack([lax.axis_index(a).astype(jnp.int32) for a in AXES])
    cot_turned = lax.ppermute(cotangent, AXES, SWAP)
    slab = in_order(
        place, [activations] + [lax.ppermute(activations, "y", shift(d)) for d in range(1, 4)]
    )
    cot_all = copies_to(cot_turned, ZAX, 8)
    own = [slab] + [lax.ppermute(slab, "x", shift(d)) for d in range(1, 4)]
    swapped = [lax.ppermute(part, "c", FLIP) for part in own]
    weight, _ = lax.optimization_barrier((weight, slab))
    cols = columns(place, weight)
    near_w = in_order(
        place, [cols[0]] + [lax.ppermute(cols[d], "y", shift(d)) for d in range(1, 4)]
    )
    far_w = lax.ppermute(near_w, "zl", FLIP)
    copies, near, away = grad_piece(place, cot_all, own, swapped)
    pieces = lax.all_to_all(copies, SOLVER, 0, 0, tiled=True)
    pieces, away, near_w, far_w = lax.optimization_barrier((pieces, away, near_w, far_w))
    far = lax.ppermute(away, "zl", FLIP)
    left_old = pltpu.with_memory_space_constraint(left_old[0, 0], pltpu.HBM)
    right_old = pltpu.with_memory_space_constraint(right_old[0, 0], pltpu.HBM)
    new_left, new_right, update, sent = solve(place, pieces, left_old, right_old)
    update_cols = lax.all_to_all(sent, SOLVER, 0, 0, tiled=True)
    far, sent = lax.optimization_barrier((far, sent))
    far_swapped = lax.ppermute(far, "c", FLIP)
    weights = (near_w, far_w)
    acts = (near, far, far_swapped)

    parts = first_partial(place, weights, acts)
    update_cols, _ = lax.optimization_barrier((update_cols, parts[0]))
    parts = [parts[0]] + [lax.ppermute(parts[e], "zh", shift(e)) for e in range(1, 4)]
    first_out = lax.ppermute(add_up(place, *parts), AXES, SWAP)

    second, spread = second_partial(place, update_cols, weights, acts)
    arrived = lax.all_to_all(second, "zh", 0, 0, tiled=True)
    second_out = lax.ppermute(add_up(place, arrived), AXES, SWAP)
    direction = update / spread[0, 0]
    return (first_out, new_left[None, None], new_right[None, None], direction, second_out)


def solution(mesh):
    fine = Mesh(mesh.devices.reshape(4, 2, 4, 2, 4), AXES)
    rows = ("zh", "zl", "y")
    in_specs = (
        P(BATCH, rows),
        P(rows, BATCH),
        P(rows, BATCH),
        P("zh", BATCH, None, None),
        P("zh", BATCH, None, None),
    )
    out_specs = (
        P(rows, BATCH),
        P("zh", BATCH, SOLVER, None),
        P("zh", BATCH, SOLVER, None),
        P(rows, BATCH),
        P(rows, BATCH),
    )
    return jax.shard_map(body, mesh=fine, in_specs=in_specs, out_specs=out_specs, check_vma=False)
```

```python
import jax
import jax.numpy as jnp
from jax import lax
from jax.experimental import pallas as pl
from jax.experimental.pallas import tpu as pltpu
from jax.sharding import Mesh
from jax.sharding import PartitionSpec as P

BLOCK = 1024
STAT_DECAY = 0.8
LEARN_RATE = 0.005
EPSILON = 1e-06

AXES = ("x", "c", "zh", "zl", "y")
BATCH = ("x", "c")
ZAX = ("zh", "zl")
SOLVER = ("zl", "y")
MIB = 1 << 20
SHAPE = jax.ShapeDtypeStruct
BF16 = jnp.bfloat16
F32 = jnp.float32


def device(x, c, zh, zl, y):
    return (((x * 2 + c) * 4 + zh) * 2 + zl) * 4 + y


EVERY = [
    (x, c, zh, zl, y)
    for x in range(4)
    for c in range(2)
    for zh in range(4)
    for zl in range(2)
    for y in range(4)
]
SWAP = [(device(*d), device(d[2], d[3], d[0], d[1], d[4])) for d in EVERY]
FLIP = [(0, 1), (1, 0)]


def shift(by):
    return [(i, (i + by) % 4) for i in range(4)]


def copies_to(shard, axis, count):
    copies = jnp.broadcast_to(shard, (count, *shard.shape))
    return lax.all_to_all(copies, axis, split_axis=0, concat_axis=0, tiled=True)


def dot(a, b):
    return jnp.dot(a, b, preferred_element_type=F32)


def dot_minor(a, b):
    return lax.dot_general(a, b, (((1,), (1,)), ((), ())), preferred_element_type=F32)


VMEM = pl.BlockSpec(memory_space=pltpu.VMEM)
HBM = pl.BlockSpec(memory_space=pltpu.HBM)


def call(body, in_specs, out_specs, out_shape, scratch=(), limit=24, name=None):
    return pl.pallas_call(
        body,
        out_shape=out_shape,
        in_specs=[pl.BlockSpec(memory_space=pltpu.SMEM), *in_specs],
        out_specs=out_specs,
        scratch_shapes=list(scratch),
        compiler_params=pltpu.CompilerParams(vmem_limit_bytes=limit * MIB),
        name=name,
    )


def wide(slab):
    return jnp.concatenate([slab[q] for q in range(4)], axis=1)


def order_body(place, *refs):
    for d in range(4):
        refs[4][(place[4] - d) & 3] = refs[d][...]


def in_order(place, parts):
    shape = SHAPE((4, *parts[0].shape), BF16)
    return call(order_body, [VMEM] * 4, VMEM, shape, limit=8, name="in_order")(place, *parts)


def columns_body(place, weight_ref, *refs):
    outs, work = refs[:4], refs[4]
    for q in range(4):
        work[q] = weight_ref[:, q * 256 : (q + 1) * 256]
    for d in range(4):
        outs[d][...] = work[(place[4] + d) & 3]


def columns(place, weight):
    part = SHAPE((128, 256), BF16)
    return call(
        columns_body,
        [VMEM],
        [VMEM] * 4,
        [part] * 4,
        scratch=[pltpu.VMEM((4, 128, 256), BF16)],
        limit=8,
        name="columns",
    )(place, weight)


def grad_body(place, cot_ref, *refs):
    own, swapped = refs[:4], refs[4:8]
    copies_ref, near_ref, away_ref, piece_ref, near_buf, away_buf, sems = refs[8:]
    x, c, zl = place[0], place[1], place[3]
    total = jnp.zeros((256, 512), F32)
    for d in range(4):
        at = (x - d) & 3
        mine, theirs = own[d][...], swapped[d][...]
        near_buf[at] = jnp.where(c == zl, mine, theirs)
        away_buf[at] = jnp.where(c == zl, theirs, mine)
    sends = [
        pltpu.make_async_copy(near_buf, near_ref, sems.at[8]),
        pltpu.make_async_copy(away_buf.at[pl.ds(c * 2, 2)], away_ref, sems.at[9]),
    ]
    for send in sends:
        send.start()
    for d in range(4):
        at = (x - d) & 3
        total = total + dot(cot_ref[at * 2 + c], wide(own[d]))
        total = total + dot(cot_ref[at * 2 + 1 - c], wide(swapped[d]))
    piece_ref[...] = total.astype(BF16)
    for s in range(8):
        send = pltpu.make_async_copy(piece_ref, copies_ref.at[s], sems.at[s])
        send.start()
        sends.append(send)
    for send in sends:
        send.wait()


def grad_piece(place, cot_all, own, swapped):
    return call(
        grad_body,
        [VMEM] * 9,
        [HBM] * 3,
        [
            pltpu.HBM((8, 256, 512), BF16),
            pltpu.HBM((4, 4, 256, 128), BF16),
            pltpu.HBM((2, 4, 256, 128), BF16),
        ],
        scratch=[
            pltpu.VMEM((256, 512), BF16),
            pltpu.VMEM((4, 4, 256, 128), BF16),
            pltpu.VMEM((4, 4, 256, 128), BF16),
            pltpu.SemaphoreType.DMA((10,)),
        ],
        limit=10,
        name="grad_piece",
    )(place, cot_all, *own, *swapped)


def forward_groups(place, near_t, far_t, near_ref, far_refs, out_ref):
    c = place[1]
    for i in range(2):
        for j in range(2):
            at = (c * 2 if i == 0 else 2 - c * 2) + j
            total = dot_minor(near_t, wide(near_ref.at[at]))
            total = total + dot_minor(far_t, wide(far_refs[i].at[j]))
            out_ref[at] = total.astype(BF16)


def first_body(place, near_w, far_w, near_ref, far0, far1, *refs):
    outs, work = refs[:4], refs[4]
    near_t = near_w[...].reshape(512, 256).T
    far_t = far_w[...].reshape(512, 256).T
    forward_groups(place, near_t, far_t, near_ref, (far0, far1), work)
    for e in range(4):
        outs[e][...] = work[(place[2] + e) & 3]


def second_body(place, update_ref, near_w, far_w, near_ref, far0, far1, out_ref, spread_ref):
    squares = jnp.zeros((16, 128), F32)
    for s in range(8):
        squares = squares + update_ref[s, 128:144, :128].astype(F32)
    mean = jnp.sum(squares, axis=0, keepdims=True)[:, :1] / (BLOCK * BLOCK)
    spread = jnp.sqrt(mean + EPSILON)
    spread_ref[...] = jnp.broadcast_to(spread, (8, 128))
    rate = LEARN_RATE / spread
    zl = place[3]

    def changed(weight, first):
        update = jnp.concatenate([update_ref[first + q, :128, :] for q in range(4)], axis=0)
        weight = weight[...].reshape(512, 256)
        return (weight.astype(F32) - rate * update.astype(F32)).astype(BF16).T

    near_t = changed(near_w, zl * 4)
    far_t = changed(far_w, 4 - zl * 4)
    forward_groups(place, near_t, far_t, near_ref, (far0, far1), out_ref)


def first_partial(place, weights, acts):
    part = SHAPE((256, 256), BF16)
    return call(
        first_body,
        [VMEM] * 5,
        [VMEM] * 4,
        [part] * 4,
        scratch=[pltpu.VMEM((4, 256, 256), BF16)],
        limit=12,
        name="first_partial",
    )(place, *weights, *acts)


def second_partial(place, update_cols, weights, acts):
    return call(
        second_body,
        [VMEM] * 6,
        [VMEM] * 2,
        [SHAPE((4, 256, 256), BF16), SHAPE((8, 128), F32)],
        limit=12,
        name="second_partial",
    )(place, update_cols, *weights, *acts)


def add_body(place, *refs):
    parts = refs[:-1]
    if len(parts) == 1:
        parts = [parts[0].at[i] for i in range(4)]
    total = parts[0][...].astype(F32)
    for part in parts[1:]:
        total = total + part[...].astype(F32)
    refs[-1][...] = total.astype(BF16)


def add_up(place, *parts):
    return call(
        add_body, [VMEM] * len(parts), VMEM, SHAPE((256, 256), BF16), limit=8, name="add_up"
    )(place, *parts)


def statistics(lhs_ref, rhs_ref, old_ref, full_ref, off_ref):
    tile = 256
    sums = jnp.zeros((1, BLOCK), F32)
    diag = jnp.zeros((1, BLOCK), F32)
    for i in range(BLOCK // tile):
        rows = pl.ds(i * tile, tile)
        gram = dot(lhs_ref[rows, :], rhs_ref[...])
        new = STAT_DECAY * old_ref[rows, :] + (1.0 - STAT_DECAY) / BLOCK * gram
        full_ref[rows, :] = new
        sums = sums + jnp.sum(jnp.abs(new), axis=0, keepdims=True)
        row = lax.broadcasted_iota(jnp.int32, (tile, BLOCK), 0) + i * tile
        col = lax.broadcasted_iota(jnp.int32, (tile, BLOCK), 1)
        on_diag = row == col
        diag = diag + jnp.sum(jnp.where(on_diag, new, 0.0), axis=0, keepdims=True)
        off_ref[rows, :] = jnp.where(on_diag, 0.0, new).astype(BF16)
    scale = 2.5 / (jnp.max(sums, axis=1, keepdims=True) + EPSILON)
    return scale, diag


def times_factor(rows, off_ref, diag):
    return rows * diag + dot(rows.astype(BF16), off_ref[...])


def times_root(start, off_ref, diag, quarter):
    value = start
    for _ in range(4):
        value = 1.25 * value - quarter * times_factor(value, off_ref, diag)
    return 1.25 * start - quarter * times_factor(value, off_ref, diag)


def solver_body(
    place,
    pieces_ref,
    left_old_ref,
    right_old_ref,
    new_left_ref,
    new_right_ref,
    update_ref,
    sent_ref,
    left_buf,
    right_buf,
    grad_ref,
    grad_t_ref,
    full_ref,
    off_left_ref,
    off_right_ref,
    rows_buf,
    update_buf,
    sent_buf,
    sems,
):
    load_left = pltpu.make_async_copy(left_old_ref, left_buf, sems.at[0])
    load_right = pltpu.make_async_copy(right_old_ref, right_buf, sems.at[1])
    load_left.start()
    load_right.start()
    first = pl.multiple_of((place[3] * 4 + place[4]) * 128, 128)
    own = pl.ds(first, 128)
    for zl in range(2):
        for y in range(4):
            piece = pieces_ref[zl * 4 + y]
            grad_ref[pl.ds(y * 256, 256), pl.ds(zl * 512, 512)] = piece
            grad_t_ref[pl.ds(zl * 512, 512), pl.ds(y * 256, 256)] = piece.T
    load_left.wait()
    scale_left, diag_left = statistics(grad_t_ref, grad_ref, left_buf, full_ref, off_left_ref)
    left_rows = full_ref[own, :]
    rows_buf[...] = left_rows
    store_left = pltpu.make_async_copy(rows_buf, new_left_ref, sems.at[2])
    store_left.start()
    load_right.wait()
    scale_right, diag_right = statistics(
        grad_ref, grad_t_ref, right_buf, full_ref, off_right_ref
    )
    store_right = pltpu.make_async_copy(full_ref.at[own, :], new_right_ref, sems.at[3])
    store_right.start()
    quarter_left = scale_left * 0.25
    quarter_right = scale_right * 0.25
    row = lax.broadcasted_iota(jnp.int32, (128, BLOCK), 0) + first
    col = lax.broadcasted_iota(jnp.int32, (128, BLOCK), 1)
    start = jnp.where(row == col, 1.25, 0.0) - quarter_left * left_rows
    root = jnp.sqrt(jnp.sqrt(scale_left)) * times_root(start, off_left_ref, diag_left, quarter_left)
    high = root.astype(BF16)
    low = (root - high.astype(F32)).astype(BF16)
    both = dot(jnp.concatenate([high, low], axis=0), grad_t_ref[...])
    mixed = both[:128] + both[128:]
    turned = 1.25 * mixed - quarter_right * times_factor(mixed, off_right_ref, diag_right)
    update = jnp.sqrt(jnp.sqrt(scale_right)) * times_root(
        turned, off_right_ref, diag_right, quarter_right
    )
    squares = jnp.sum(jnp.sum(update * update, axis=0, keepdims=True), axis=1, keepdims=True)
    high = squares.astype(BF16).astype(F32)
    middle = (squares - high).astype(BF16).astype(F32)
    low = squares - high - middle
    row = lax.broadcasted_iota(jnp.int32, (16, 256), 0)
    tail = jnp.where(row == 0, high, jnp.where(row == 1, middle, jnp.where(row == 2, low, 0.0)))
    tail = tail.astype(BF16)
    for y in range(4):
        sent_buf[y, :128, :] = update[:, y * 256 : (y + 1) * 256].astype(BF16)
        sent_buf[y, 128:, :] = tail
    stores = [
        pltpu.make_async_copy(sent_buf, sent_ref.at[pl.ds(zl * 4, 4)], sems.at[4 + zl])
        for zl in range(2)
    ]
    for store in stores:
        store.start()
    update_buf[...] = update
    stores.append(pltpu.make_async_copy(update_buf, update_ref, sems.at[6]))
    stores[-1].start()
    for store in [store_left, store_right, *stores]:
        store.wait()


def solve(place, pieces, left_old, right_old):
    square = (BLOCK, BLOCK)
    rows = pltpu.HBM((128, BLOCK), F32)
    return call(
        solver_body,
        [VMEM, HBM, HBM],
        [HBM] * 4,
        [rows, rows, rows, pltpu.HBM((8, 144, 256), BF16)],
        scratch=[
            *[pltpu.VMEM(square, kind) for kind in (F32, F32, BF16, BF16, F32, BF16, BF16)],
            pltpu.VMEM((128, BLOCK), F32),
            pltpu.VMEM((128, BLOCK), F32),
            pltpu.VMEM((4, 144, 256), BF16),
            pltpu.SemaphoreType.DMA((7,)),
        ],
        limit=30,
        name="solve",
    )(place, pieces, left_old, right_old)


def body(activations, cotangent, weight, left_old, right_old):
    place = jnp.stack([lax.axis_index(a).astype(jnp.int32) for a in AXES])
    cot_turned = lax.ppermute(cotangent, AXES, SWAP)
    crossed = [lax.ppermute(activations, "y", shift(d)) for d in range(1, 4)]
    cot_turned, *crossed = lax.optimization_barrier((cot_turned, *crossed))
    cot_all = copies_to(cot_turned, ZAX, 8)
    slab = in_order(place, [activations, *crossed])
    own = [slab] + [lax.ppermute(slab, "x", shift(d)) for d in range(1, 4)]
    swapped = [lax.ppermute(part, "c", FLIP) for part in own]
    weight, _ = lax.optimization_barrier((weight, slab))
    cols = columns(place, weight)
    near_w = in_order(
        place, [cols[0]] + [lax.ppermute(cols[d], "y", shift(d)) for d in range(1, 4)]
    )
    cot_all, near_w = lax.optimization_barrier((cot_all, near_w))
    copies, near, away = grad_piece(place, cot_all, own, swapped)

    pieces = lax.all_to_all(copies, SOLVER, 0, 0, tiled=True)
    pieces, away, leaving_w = lax.optimization_barrier((pieces, away, near_w))
    far = lax.ppermute(away, "zl", FLIP)
    far_w = lax.ppermute(leaving_w, "zl", FLIP)
    left_old = pltpu.with_memory_space_constraint(left_old[0, 0], pltpu.HBM)
    right_old = pltpu.with_memory_space_constraint(right_old[0, 0], pltpu.HBM)
    new_left, new_right, update, sent = solve(place, pieces, left_old, right_old)
    update_cols = lax.all_to_all(sent, SOLVER, 0, 0, tiled=True)
    far, far_w, sent = lax.optimization_barrier((far, far_w, sent))
    far_swapped = lax.ppermute(far, "c", FLIP)
    weights = (near_w, far_w)
    acts = (near, far, far_swapped)

    parts = first_partial(place, weights, acts)
    parts = [parts[0]] + [lax.ppermute(parts[e], "zh", shift(e)) for e in range(1, 4)]
    update_cols, *parts = lax.optimization_barrier((update_cols, *parts))
    second, spread = second_partial(place, update_cols, weights, acts)
    arrived = lax.all_to_all(second, "zh", 0, 0, tiled=True)
    first_out = lax.ppermute(add_up(place, *parts), AXES, SWAP)
    second_out = lax.ppermute(add_up(place, arrived), AXES, SWAP)
    direction = update / spread[0, 0]
    return (first_out, new_left[None, None], new_right[None, None], direction, second_out)


def solution(mesh):
    fine = Mesh(mesh.devices.reshape(4, 2, 4, 2, 4), AXES)
    rows = ("zh", "zl", "y")
    in_specs = (
        P(BATCH, rows),
        P(rows, BATCH),
        P(rows, BATCH),
        P("zh", BATCH, None, None),
        P("zh", BATCH, None, None),
    )
    out_specs = (
        P(rows, BATCH),
        P("zh", BATCH, SOLVER, None),
        P("zh", BATCH, SOLVER, None),
        P(rows, BATCH),
        P(rows, BATCH),
    )
    return jax.shard_map(body, mesh=fine, in_specs=in_specs, out_specs=out_specs, check_vma=False)
```

```python
import jax
import jax.numpy as jnp
from jax import lax
from jax.experimental import pallas as pl
from jax.experimental.pallas import tpu as pltpu
from jax.sharding import Mesh
from jax.sharding import PartitionSpec as P

BLOCK = 1024
STAT_DECAY = 0.8
LEARN_RATE = 0.005
EPSILON = 1e-06

AXES = ("x", "c", "zh", "zl", "y")
BATCH = ("x", "c")
ZAX = ("zh", "zl")
SOLVER = ("zl", "y")
MIB = 1 << 20
SHAPE = jax.ShapeDtypeStruct
BF16 = jnp.bfloat16
F32 = jnp.float32


def device(x, c, zh, zl, y):
    return (((x * 2 + c) * 4 + zh) * 2 + zl) * 4 + y


EVERY = [
    (x, c, zh, zl, y)
    for x in range(4)
    for c in range(2)
    for zh in range(4)
    for zl in range(2)
    for y in range(4)
]
SWAP = [(device(*d), device(d[2], d[3], d[0], d[1], d[4])) for d in EVERY]
FLIP = [(0, 1), (1, 0)]


def shift(by):
    return [(i, (i + by) % 4) for i in range(4)]


def copies_to(shard, axis, count):
    copies = jnp.broadcast_to(shard, (count, *shard.shape))
    return lax.all_to_all(copies, axis, split_axis=0, concat_axis=0, tiled=True)


def dot(a, b):
    return jnp.dot(a, b, preferred_element_type=F32)


def dot_minor(a, b):
    return lax.dot_general(a, b, (((1,), (1,)), ((), ())), preferred_element_type=F32)


VMEM = pl.BlockSpec(memory_space=pltpu.VMEM)
HBM = pl.BlockSpec(memory_space=pltpu.HBM)


def call(body, in_specs, out_specs, out_shape, scratch=(), limit=24, name=None):
    return pl.pallas_call(
        body,
        out_shape=out_shape,
        in_specs=[pl.BlockSpec(memory_space=pltpu.SMEM), *in_specs],
        out_specs=out_specs,
        scratch_shapes=list(scratch),
        compiler_params=pltpu.CompilerParams(vmem_limit_bytes=limit * MIB),
        name=name,
    )


def wide(slab):
    return jnp.concatenate([slab[q] for q in range(4)], axis=1)


def pack_body(place, acts_ref, weight_ref, *refs):
    outs, work = refs[:4], refs[4]
    for q in range(4):
        for half in range(2):
            at = q * 256 + half * 128
            work[q, half * 128 : (half + 1) * 128, :] = weight_ref[:, at : at + 128]
    acts = acts_ref[...]
    for d in range(4):
        outs[d][:256, :] = acts
        outs[d][256:, :] = work[(place[4] + d) & 3]


def pack(place, acts, weight):
    part = SHAPE((512, 128), BF16)
    return call(
        pack_body,
        [VMEM] * 2,
        [VMEM] * 4,
        [part] * 4,
        scratch=[pltpu.VMEM((4, 256, 128), BF16)],
        limit=8,
        name="pack",
    )(place, acts, weight)


def unpack_body(place, *refs):
    for d in range(4):
        at = (place[4] - d) & 3
        refs[4][at] = refs[d][:256, :]
        refs[5][at] = refs[d][256:, :]


def unpack(place, parts):
    shape = SHAPE((4, 256, 128), BF16)
    return call(unpack_body, [VMEM] * 4, [VMEM] * 2, [shape] * 2, limit=8, name="unpack")(
        place, *parts
    )


def weight_of(parts):
    rows = [jnp.concatenate([parts[q, :128, :], parts[q, 128:, :]], axis=1) for q in range(4)]
    return jnp.concatenate(rows, axis=0)


def grad_body(place, cot_ref, weight_ref, *refs):
    own, swapped = refs[:4], refs[4:8]
    piece_ref, near_ref, away_ref, near_buf, away_buf, sems = refs[8:]
    x, c, zl = place[0], place[1], place[3]
    for d in range(4):
        at = (x - d) & 3
        mine, theirs = own[d][...], swapped[d][...]
        near_buf[at] = jnp.where(c == zl, mine, theirs)
        away_buf[at] = jnp.where(c == zl, theirs, mine)
    sends = [
        pltpu.make_async_copy(near_buf, near_ref, sems.at[0]),
        pltpu.make_async_copy(
            away_buf.at[pl.ds(c * 2, 2)], away_ref.at[pl.ds(0, 2)], sems.at[1]
        ),
        pltpu.make_async_copy(weight_ref, away_ref.at[2], sems.at[2]),
    ]
    for send in sends:
        send.start()
    total = jnp.zeros((256, 512), F32)
    for d in range(4):
        at = (x - d) & 3
        total = total + dot(cot_ref[at * 2 + c], wide(own[d]))
        total = total + dot(cot_ref[at * 2 + 1 - c], wide(swapped[d]))
    piece_ref[...] = total.astype(BF16)
    for send in sends:
        send.wait()


def grad_piece(place, cot_all, near_w, own, swapped):
    return call(
        grad_body,
        [VMEM] * 10,
        [VMEM, HBM, HBM],
        [
            SHAPE((256, 512), BF16),
            pltpu.HBM((4, 4, 256, 128), BF16),
            pltpu.HBM((3, 4, 256, 128), BF16),
        ],
        scratch=[
            pltpu.VMEM((4, 4, 256, 128), BF16),
            pltpu.VMEM((4, 4, 256, 128), BF16),
            pltpu.SemaphoreType.DMA((3,)),
        ],
        limit=10,
        name="grad_piece",
    )(place, cot_all, near_w, *own, *swapped)


def first_body(place, weight_ref, *refs):
    own, swapped = refs[:4], refs[4:8]
    out_ref, work, sems = refs[8:]
    weight_t = weight_of(weight_ref).T
    sends = []
    for d in range(4):
        at = ((place[0] - d) & 3) * 2
        for i, (slab, group) in enumerate(
            ((own[d], at + place[1]), (swapped[d], at + 1 - place[1]))
        ):
            work[d * 2 + i] = dot_minor(weight_t, wide(slab)).astype(BF16)
            sends.append(
                pltpu.make_async_copy(work.at[d * 2 + i], out_ref.at[group], sems.at[d * 2 + i])
            )
            sends[-1].start()
    for send in sends:
        send.wait()


def first_partial(place, near_w, own, swapped):
    return call(
        first_body,
        [VMEM] * 9,
        HBM,
        pltpu.HBM((8, 256, 256), BF16),
        scratch=[pltpu.VMEM((8, 256, 256), BF16), pltpu.SemaphoreType.DMA((8,))],
        limit=12,
        name="first_partial",
    )(place, near_w, *own, *swapped)


def second_body(
    place, update_ref, near_w, near_ref, far_ref, swap_ref, out_ref, spread_ref, work, sems
):
    squares = jnp.zeros((16, 128), F32)
    for s in range(8):
        squares = squares + update_ref[s, 128:144, :128].astype(F32)
    mean = jnp.sum(squares, axis=0, keepdims=True)[:, :1] / (BLOCK * BLOCK)
    spread = jnp.sqrt(mean + EPSILON)
    spread_ref[...] = jnp.broadcast_to(spread, (8, 128))
    rate = LEARN_RATE / spread
    c, zl = place[1], place[3]

    def changed(weight, first):
        update = jnp.concatenate([update_ref[first + q, :128, :] for q in range(4)], axis=0)
        return (weight_of(weight).astype(F32) - rate * update.astype(F32)).astype(BF16).T

    near_t = changed(near_w, zl * 4)
    far_t = changed(far_ref.at[2], 4 - zl * 4)
    sends = []
    for i in range(2):
        for j in range(2):
            at = (c * 2 if i == 0 else 2 - c * 2) + j
            total = dot_minor(near_t, wide(near_ref.at[at]))
            total = total + dot_minor(far_t, wide((far_ref, swap_ref)[i].at[j]))
            work[i * 2 + j] = total.astype(BF16)
            sends.append(
                pltpu.make_async_copy(work.at[i * 2 + j], out_ref.at[at], sems.at[i * 2 + j])
            )
            sends[-1].start()
    for send in sends:
        send.wait()


def second_partial(place, update_cols, near_w, near, far, far_swapped):
    return call(
        second_body,
        [VMEM] * 5,
        [HBM, VMEM],
        [pltpu.HBM((4, 256, 256), BF16), SHAPE((8, 128), F32)],
        scratch=[pltpu.VMEM((4, 256, 256), BF16), pltpu.SemaphoreType.DMA((4,))],
        limit=12,
        name="second_partial",
    )(place, update_cols, near_w, near, far, far_swapped)


def add_body(place, parts_ref, out_ref):
    total = parts_ref[0].astype(F32)
    for i in range(1, parts_ref.shape[0]):
        total = total + parts_ref[i].astype(F32)
    out_ref[...] = total.astype(BF16)


def add_up(place, parts):
    return call(add_body, [VMEM], VMEM, SHAPE((256, 256), BF16), limit=8, name="add_up")(
        place, parts
    )


def statistics(lhs_ref, rhs_ref, old_ref, full_ref, off_ref):
    tile = 256
    sums = jnp.zeros((1, BLOCK), F32)
    diag = jnp.zeros((1, BLOCK), F32)
    for i in range(BLOCK // tile):
        rows = pl.ds(i * tile, tile)
        gram = dot(lhs_ref[rows, :], rhs_ref[...])
        new = STAT_DECAY * old_ref[rows, :] + (1.0 - STAT_DECAY) / BLOCK * gram
        full_ref[rows, :] = new
        sums = sums + jnp.sum(jnp.abs(new), axis=0, keepdims=True)
        row = lax.broadcasted_iota(jnp.int32, (tile, BLOCK), 0) + i * tile
        col = lax.broadcasted_iota(jnp.int32, (tile, BLOCK), 1)
        on_diag = row == col
        diag = diag + jnp.sum(jnp.where(on_diag, new, 0.0), axis=0, keepdims=True)
        off_ref[rows, :] = jnp.where(on_diag, 0.0, new).astype(BF16)
    scale = 2.5 / (jnp.max(sums, axis=1, keepdims=True) + EPSILON)
    return scale, diag


def times_factor(rows, off_ref, diag):
    return rows * diag + dot(rows.astype(BF16), off_ref[...])


def times_root(start, off_ref, diag, quarter):
    value = start
    for _ in range(4):
        value = 1.25 * value - quarter * times_factor(value, off_ref, diag)
    return 1.25 * start - quarter * times_factor(value, off_ref, diag)


def solver_body(
    place,
    near0,
    near1,
    near2,
    near3,
    far0,
    far1,
    far2,
    far3,
    left_old_ref,
    right_old_ref,
    new_left_ref,
    new_right_ref,
    update_ref,
    sent_ref,
    pieces_ref,
    left_buf,
    right_buf,
    grad_ref,
    grad_t_ref,
    full_ref,
    off_left_ref,
    off_right_ref,
    rows_buf,
    update_buf,
    sent_buf,
    sems,
):
    load_left = pltpu.make_async_copy(left_old_ref, left_buf, sems.at[0])
    load_right = pltpu.make_async_copy(right_old_ref, right_buf, sems.at[1])
    load_left.start()
    load_right.start()
    first = pl.multiple_of((place[3] * 4 + place[4]) * 128, 128)
    own = pl.ds(first, 128)
    for d, (near, far) in enumerate(((near0, far0), (near1, far1), (near2, far2), (near3, far3))):
        at = (place[4] - d) & 3
        pieces_ref[place[3] * 4 + at] = near[...]
        pieces_ref[4 - place[3] * 4 + at] = far[...]
    for zl in range(2):
        for y in range(4):
            piece = pieces_ref[zl * 4 + y]
            grad_ref[pl.ds(y * 256, 256), pl.ds(zl * 512, 512)] = piece
            grad_t_ref[pl.ds(zl * 512, 512), pl.ds(y * 256, 256)] = piece.T
    load_left.wait()
    scale_left, diag_left = statistics(grad_t_ref, grad_ref, left_buf, full_ref, off_left_ref)
    left_rows = full_ref[own, :]
    rows_buf[...] = left_rows
    store_left = pltpu.make_async_copy(rows_buf, new_left_ref, sems.at[2])
    store_left.start()
    load_right.wait()
    scale_right, diag_right = statistics(
        grad_ref, grad_t_ref, right_buf, full_ref, off_right_ref
    )
    store_right = pltpu.make_async_copy(full_ref.at[own, :], new_right_ref, sems.at[3])
    store_right.start()
    quarter_left = scale_left * 0.25
    quarter_right = scale_right * 0.25
    row = lax.broadcasted_iota(jnp.int32, (128, BLOCK), 0) + first
    col = lax.broadcasted_iota(jnp.int32, (128, BLOCK), 1)
    start = jnp.where(row == col, 1.25, 0.0) - quarter_left * left_rows
    root = jnp.sqrt(jnp.sqrt(scale_left)) * times_root(start, off_left_ref, diag_left, quarter_left)
    high = root.astype(BF16)
    low = (root - high.astype(F32)).astype(BF16)
    both = dot(jnp.concatenate([high, low], axis=0), grad_t_ref[...])
    mixed = both[:128] + both[128:]
    turned = 1.25 * mixed - quarter_right * times_factor(mixed, off_right_ref, diag_right)
    update = jnp.sqrt(jnp.sqrt(scale_right)) * times_root(
        turned, off_right_ref, diag_right, quarter_right
    )
    squares = jnp.sum(jnp.sum(update * update, axis=0, keepdims=True), axis=1, keepdims=True)
    high = squares.astype(BF16).astype(F32)
    middle = (squares - high).astype(BF16).astype(F32)
    low = squares - high - middle
    row = lax.broadcasted_iota(jnp.int32, (16, 256), 0)
    tail = jnp.where(row == 0, high, jnp.where(row == 1, middle, jnp.where(row == 2, low, 0.0)))
    tail = tail.astype(BF16)
    for y in range(4):
        sent_buf[y, :128, :] = update[:, y * 256 : (y + 1) * 256].astype(BF16)
        sent_buf[y, 128:, :] = tail
    stores = [
        pltpu.make_async_copy(sent_buf, sent_ref.at[pl.ds(zl * 4, 4)], sems.at[4 + zl])
        for zl in range(2)
    ]
    for store in stores:
        store.start()
    update_buf[...] = update
    stores.append(pltpu.make_async_copy(update_buf, update_ref, sems.at[6]))
    stores[-1].start()
    for store in [store_left, store_right, *stores]:
        store.wait()


def solve(place, pieces, left_old, right_old):
    square = (BLOCK, BLOCK)
    rows = pltpu.HBM((128, BLOCK), F32)
    return call(
        solver_body,
        [*[VMEM] * 8, HBM, HBM],
        [HBM] * 4,
        [rows, rows, rows, pltpu.HBM((8, 144, 256), BF16)],
        scratch=[
            pltpu.VMEM((8, 256, 512), BF16),
            *[pltpu.VMEM(square, kind) for kind in (F32, F32, BF16, BF16, F32, BF16, BF16)],
            pltpu.VMEM((128, BLOCK), F32),
            pltpu.VMEM((128, BLOCK), F32),
            pltpu.VMEM((4, 144, 256), BF16),
            pltpu.SemaphoreType.DMA((7,)),
        ],
        limit=27,
        name="solve",
    )(place, *pieces, left_old, right_old)


def body(activations, cotangent, weight, left_old, right_old):
    place = jnp.stack([lax.axis_index(a).astype(jnp.int32) for a in AXES])
    cot_turned = lax.ppermute(cotangent, AXES, SWAP)
    packed = pack(place, activations, weight)
    crossed = [lax.ppermute(packed[d], "y", shift(d)) for d in range(1, 4)]
    cot_turned, *crossed = lax.optimization_barrier((cot_turned, *crossed))
    cot_all = copies_to(cot_turned, ZAX, 8)
    slab, near_w = unpack(place, [packed[0], *crossed])
    own = [slab] + [lax.ppermute(slab, "x", shift(d)) for d in range(1, 4)]
    swapped = [lax.ppermute(part, "c", FLIP) for part in own]
    first = first_partial(place, near_w, own, swapped)
    cot_all, first = lax.optimization_barrier((cot_all, first))
    piece, near, away = grad_piece(place, cot_all, near_w, own, swapped)

    beside = lax.ppermute(piece, "zl", FLIP)
    pieces = [piece] + [lax.ppermute(piece, "y", shift(d)) for d in range(1, 4)]
    pieces += [beside] + [lax.ppermute(beside, "y", shift(d)) for d in range(1, 4)]
    first, *_ = lax.optimization_barrier((first, beside, pieces[1], pieces[3]))
    first_parts = lax.all_to_all(first, ZAX, 0, 0, tiled=True)
    away, first, *pieces = lax.optimization_barrier((away, first, *pieces))
    far = lax.ppermute(away, "zl", FLIP)
    left_old = pltpu.with_memory_space_constraint(left_old[0, 0], pltpu.HBM)
    right_old = pltpu.with_memory_space_constraint(right_old[0, 0], pltpu.HBM)
    new_left, new_right, update, sent = solve(place, pieces, left_old, right_old)
    sent, first_parts = lax.optimization_barrier((sent, first_parts))
    update_cols = lax.all_to_all(sent, SOLVER, 0, 0, tiled=True)
    far, sent = lax.optimization_barrier((far, sent))
    far_swapped = lax.ppermute(far, "c", FLIP)
    first_out = lax.ppermute(add_up(place, first_parts), AXES, SWAP)

    second, spread = second_partial(place, update_cols, near_w, near, far, far_swapped)
    arrived = lax.all_to_all(second, "zh", 0, 0, tiled=True)
    second_out = lax.ppermute(add_up(place, arrived), AXES, SWAP)
    direction = update / spread[0, 0]
    return (first_out, new_left[None, None], new_right[None, None], direction, second_out)


def solution(mesh):
    fine = Mesh(mesh.devices.reshape(4, 2, 4, 2, 4), AXES)
    rows = ("zh", "zl", "y")
    in_specs = (
        P(BATCH, rows),
        P(rows, BATCH),
        P(rows, BATCH),
        P("zh", BATCH, None, None),
        P("zh", BATCH, None, None),
    )
    out_specs = (
        P(rows, BATCH),
        P("zh", BATCH, SOLVER, None),
        P("zh", BATCH, SOLVER, None),
        P(rows, BATCH),
        P(rows, BATCH),
    )
    return jax.shard_map(body, mesh=fine, in_specs=in_specs, out_specs=out_specs, check_vma=False)
```

```python
import jax
import jax.numpy as jnp
from jax import lax
from jax.experimental import pallas as pl
from jax.experimental.pallas import tpu as pltpu
from jax.sharding import Mesh
from jax.sharding import PartitionSpec as P

BLOCK = 1024
STAT_DECAY = 0.8
LEARN_RATE = 0.005
EPSILON = 1e-06

AXES = ("x", "c", "zh", "zl", "y")
BATCH = ("x", "c")
ZAX = ("zh", "zl")
SOLVER = ("zl", "y")
MIB = 1 << 20
SHAPE = jax.ShapeDtypeStruct
BF16 = jnp.bfloat16
F32 = jnp.float32


def device(x, c, zh, zl, y):
    return (((x * 2 + c) * 4 + zh) * 2 + zl) * 4 + y


EVERY = [
    (x, c, zh, zl, y)
    for x in range(4)
    for c in range(2)
    for zh in range(4)
    for zl in range(2)
    for y in range(4)
]
SWAP = [(device(*d), device(d[2], d[3], d[0], d[1], d[4])) for d in EVERY]
FLIP = [(0, 1), (1, 0)]


def shift(by):
    return [(i, (i + by) % 4) for i in range(4)]


def copies_to(shard, axis, count):
    copies = jnp.broadcast_to(shard, (count, *shard.shape))
    return lax.all_to_all(copies, axis, split_axis=0, concat_axis=0, tiled=True)


def dot(a, b):
    return jnp.dot(a, b, preferred_element_type=F32)


def dot_minor(a, b):
    return lax.dot_general(a, b, (((1,), (1,)), ((), ())), preferred_element_type=F32)


VMEM = pl.BlockSpec(memory_space=pltpu.VMEM)
HBM = pl.BlockSpec(memory_space=pltpu.HBM)


def call(body, in_specs, out_specs, out_shape, scratch=(), limit=24, name=None):
    return pl.pallas_call(
        body,
        out_shape=out_shape,
        in_specs=[pl.BlockSpec(memory_space=pltpu.SMEM), *in_specs],
        out_specs=out_specs,
        scratch_shapes=list(scratch),
        compiler_params=pltpu.CompilerParams(vmem_limit_bytes=limit * MIB),
        name=name,
    )


def in_hbm(value):
    return pltpu.with_memory_space_constraint(value, pltpu.HBM)


def wide(slab):
    return jnp.concatenate([slab[q] for q in range(4)], axis=1)


def pack_body(place, acts_hbm, weight_hbm, *refs):
    outs, (acts_ref, weight_ref, work, sems) = refs[:4], refs[4:]
    loads = [
        pltpu.make_async_copy(weight_hbm, weight_ref, sems.at[0]),
        pltpu.make_async_copy(acts_hbm, acts_ref, sems.at[1]),
    ]
    for load in loads:
        load.start()
    for load in loads:
        load.wait()
    for q in range(4):
        for half in range(2):
            at = q * 256 + half * 128
            work[q, half * 128 : (half + 1) * 128, :] = weight_ref[:, at : at + 128]
    acts = acts_ref[...]
    for d in range(4):
        outs[d][:256, :] = acts
        outs[d][256:, :] = work[(place[4] + d) & 3]


def pack(place, acts, weight):
    part = SHAPE((512, 128), BF16)
    return call(
        pack_body,
        [HBM] * 2,
        [VMEM] * 4,
        [part] * 4,
        scratch=[
            pltpu.VMEM((256, 128), BF16),
            pltpu.VMEM((128, 1024), BF16),
            pltpu.VMEM((4, 256, 128), BF16),
            pltpu.SemaphoreType.DMA((2,)),
        ],
        limit=8,
        name="pack",
    )(place, in_hbm(acts), in_hbm(weight))


def unpack_body(place, *refs):
    for d in range(4):
        at = (place[4] - d) & 3
        refs[4][at] = refs[d][:256, :]
        refs[5][at] = refs[d][256:, :]


def unpack(place, parts):
    shape = SHAPE((4, 256, 128), BF16)
    return call(unpack_body, [VMEM] * 4, [VMEM] * 2, [shape] * 2, limit=8, name="unpack")(
        place, *parts
    )


def weight_of(parts):
    rows = [jnp.concatenate([parts[q, :128, :], parts[q, 128:, :]], axis=1) for q in range(4)]
    return jnp.concatenate(rows, axis=0)


def grad_body(place, cot_ref, *refs):
    own, swapped = refs[:4], refs[4:8]
    piece_ref, kept_ref, sem = refs[8:]
    x, c = place[0], place[1]
    total = jnp.zeros((256, 512), F32)
    for d in range(4):
        at = (x - d) & 3
        total = total + dot(cot_ref[at * 2 + c], wide(own[d]))
        total = total + dot(cot_ref[at * 2 + 1 - c], wide(swapped[d]))
    piece_ref[...] = total.astype(BF16)
    keep = pltpu.make_async_copy(piece_ref, kept_ref, sem)
    keep.start()
    keep.wait()


def grad_piece(place, cot_all, own, swapped):
    return call(
        grad_body,
        [VMEM] * 9,
        [VMEM, HBM],
        [SHAPE((256, 512), BF16), pltpu.HBM((256, 512), BF16)],
        scratch=[pltpu.SemaphoreType.DMA],
        limit=10,
        name="grad_piece",
    )(place, cot_all, *own, *swapped)


def first_body(place, weight_ref, *refs):
    own, swapped = refs[:4], refs[4:8]
    out_ref, near_ref, away_ref, work, sems = refs[8:]
    x, c, zl = place[0], place[1], place[3]

    def slabs_move(step):
        step(pltpu.make_async_copy(weight_ref, away_ref.at[2], sems.at[16]))
        for mine, theirs, here in ((own, swapped, c == zl), (swapped, own, c != zl)):
            for d in range(4):
                at = (x - d) & 3

                @pl.when(here)
                def _(mine=mine, d=d, at=at):
                    step(pltpu.make_async_copy(mine[d], near_ref.at[at], sems.at[8 + d]))

                @pl.when(here & (at // 2 == c))
                def _(theirs=theirs, d=d, at=at):
                    step(pltpu.make_async_copy(theirs[d], away_ref.at[at & 1], sems.at[12 + d]))

    slabs_move(lambda copy: copy.start())
    weight_t = weight_of(weight_ref).T
    sends = []
    for d in range(4):
        at = ((x - d) & 3) * 2
        for i, (slab, group) in enumerate(((own[d], at + c), (swapped[d], at + 1 - c))):
            work[d * 2 + i] = dot_minor(weight_t, wide(slab)).astype(BF16)
            sends.append(
                pltpu.make_async_copy(work.at[d * 2 + i], out_ref.at[group], sems.at[d * 2 + i])
            )
            sends[-1].start()
    for send in sends:
        send.wait()
    slabs_move(lambda copy: copy.wait())


def first_partial(place, near_w, own, swapped):
    return call(
        first_body,
        [VMEM] * 9,
        [HBM] * 3,
        [
            pltpu.HBM((8, 256, 256), BF16),
            pltpu.HBM((4, 4, 256, 128), BF16),
            pltpu.HBM((3, 4, 256, 128), BF16),
        ],
        scratch=[pltpu.VMEM((8, 256, 256), BF16), pltpu.SemaphoreType.DMA((17,))],
        limit=12,
        name="first_partial",
    )(place, near_w, *own, *swapped)


def second_body(
    place,
    update_ref,
    near_w,
    near_hbm,
    far_hbm,
    swap_hbm,
    out_ref,
    spread_ref,
    near_ref,
    far_ref,
    swap_ref,
    work,
    sems,
):
    loads = [
        pltpu.make_async_copy(far_hbm, far_ref, sems.at[4]),
        pltpu.make_async_copy(near_hbm, near_ref, sems.at[5]),
        pltpu.make_async_copy(swap_hbm, swap_ref, sems.at[6]),
    ]
    for load in loads:
        load.start()
    squares = jnp.zeros((16, 128), F32)
    for s in range(8):
        squares = squares + update_ref[s, 128:144, :128].astype(F32)
    mean = jnp.sum(squares, axis=0, keepdims=True)[:, :1] / (BLOCK * BLOCK)
    spread = jnp.sqrt(mean + EPSILON)
    spread_ref[...] = jnp.broadcast_to(spread, (8, 128))
    rate = LEARN_RATE / spread
    c, zl = place[1], place[3]

    def changed(weight, first):
        update = jnp.concatenate([update_ref[first + q, :128, :] for q in range(4)], axis=0)
        return (weight_of(weight).astype(F32) - rate * update.astype(F32)).astype(BF16).T

    near_t = changed(near_w, zl * 4)
    loads[0].wait()
    far_t = changed(far_ref.at[2], 4 - zl * 4)
    sends = []
    for load in loads[1:]:
        load.wait()
    for i in range(2):
        for j in range(2):
            at = (c * 2 if i == 0 else 2 - c * 2) + j
            total = dot_minor(near_t, wide(near_ref.at[at]))
            total = total + dot_minor(far_t, wide((far_ref, swap_ref)[i].at[j]))
            work[i * 2 + j] = total.astype(BF16)
            sends.append(
                pltpu.make_async_copy(work.at[i * 2 + j], out_ref.at[at], sems.at[i * 2 + j])
            )
            sends[-1].start()
    for send in sends:
        send.wait()


def second_partial(place, update_cols, near_w, near, far, far_swapped):
    return call(
        second_body,
        [VMEM, VMEM, HBM, HBM, HBM],
        [HBM, VMEM],
        [pltpu.HBM((4, 256, 256), BF16), SHAPE((8, 128), F32)],
        scratch=[
            pltpu.VMEM((4, 4, 256, 128), BF16),
            pltpu.VMEM((3, 4, 256, 128), BF16),
            pltpu.VMEM((3, 4, 256, 128), BF16),
            pltpu.VMEM((4, 256, 256), BF16),
            pltpu.SemaphoreType.DMA((7,)),
        ],
        limit=14,
        name="second_partial",
    )(place, update_cols, near_w, in_hbm(near), in_hbm(far), in_hbm(far_swapped))


def add_body(place, parts_ref, out_ref):
    total = parts_ref[0].astype(F32)
    for i in range(1, parts_ref.shape[0]):
        total = total + parts_ref[i].astype(F32)
    out_ref[...] = total.astype(BF16)


def add_up(place, parts):
    return call(add_body, [VMEM], VMEM, SHAPE((256, 256), BF16), limit=8, name="add_up")(
        place, parts
    )


def statistics(lhs_ref, rhs_ref, old_ref, full_ref, off_ref):
    tile = 256
    sums = jnp.zeros((1, BLOCK), F32)
    diag = jnp.zeros((1, BLOCK), F32)
    for i in range(BLOCK // tile):
        rows = pl.ds(i * tile, tile)
        gram = dot(lhs_ref[rows, :], rhs_ref[...])
        new = STAT_DECAY * old_ref[rows, :] + (1.0 - STAT_DECAY) / BLOCK * gram
        full_ref[rows, :] = new
        sums = sums + jnp.sum(jnp.abs(new), axis=0, keepdims=True)
        row = lax.broadcasted_iota(jnp.int32, (tile, BLOCK), 0) + i * tile
        col = lax.broadcasted_iota(jnp.int32, (tile, BLOCK), 1)
        on_diag = row == col
        diag = diag + jnp.sum(jnp.where(on_diag, new, 0.0), axis=0, keepdims=True)
        off_ref[rows, :] = jnp.where(on_diag, 0.0, new).astype(BF16)
    scale = 2.5 / (jnp.max(sums, axis=1, keepdims=True) + EPSILON)
    return scale, diag


def times_factor(rows, off_ref, diag):
    return rows * diag + dot(rows.astype(BF16), off_ref[...])


def times_root(start, off_ref, diag, quarter):
    value = start
    for _ in range(4):
        value = 1.25 * value - quarter * times_factor(value, off_ref, diag)
    return 1.25 * start - quarter * times_factor(value, off_ref, diag)


def solver_body(
    place,
    near0,
    near1,
    near2,
    near3,
    far0,
    far1,
    far2,
    far3,
    left_old_ref,
    right_old_ref,
    new_left_ref,
    new_right_ref,
    update_ref,
    sent_ref,
    pieces_ref,
    left_buf,
    right_buf,
    grad_ref,
    grad_t_ref,
    full_ref,
    off_left_ref,
    off_right_ref,
    rows_buf,
    update_buf,
    sent_buf,
    sems,
):
    load_left = pltpu.make_async_copy(left_old_ref, left_buf, sems.at[0])
    load_right = pltpu.make_async_copy(right_old_ref, right_buf, sems.at[1])
    load_own = pltpu.make_async_copy(
        near0, pieces_ref.at[place[3] * 4 + place[4]], sems.at[7]
    )
    load_own.start()
    load_left.start()
    load_right.start()
    first = pl.multiple_of((place[3] * 4 + place[4]) * 128, 128)
    own = pl.ds(first, 128)
    for d, (near, far) in enumerate(((near0, far0), (near1, far1), (near2, far2), (near3, far3))):
        at = (place[4] - d) & 3
        if d > 0:
            pieces_ref[place[3] * 4 + at] = near[...]
        pieces_ref[4 - place[3] * 4 + at] = far[...]
    load_own.wait()
    for zl in range(2):
        for y in range(4):
            piece = pieces_ref[zl * 4 + y]
            grad_ref[pl.ds(y * 256, 256), pl.ds(zl * 512, 512)] = piece
            grad_t_ref[pl.ds(zl * 512, 512), pl.ds(y * 256, 256)] = piece.T
    load_left.wait()
    scale_left, diag_left = statistics(grad_t_ref, grad_ref, left_buf, full_ref, off_left_ref)
    left_rows = full_ref[own, :]
    rows_buf[...] = left_rows
    store_left = pltpu.make_async_copy(rows_buf, new_left_ref, sems.at[2])
    store_left.start()
    load_right.wait()
    scale_right, diag_right = statistics(
        grad_ref, grad_t_ref, right_buf, full_ref, off_right_ref
    )
    store_right = pltpu.make_async_copy(full_ref.at[own, :], new_right_ref, sems.at[3])
    store_right.start()
    quarter_left = scale_left * 0.25
    quarter_right = scale_right * 0.25
    row = lax.broadcasted_iota(jnp.int32, (128, BLOCK), 0) + first
    col = lax.broadcasted_iota(jnp.int32, (128, BLOCK), 1)
    start = jnp.where(row == col, 1.25, 0.0) - quarter_left * left_rows
    root = jnp.sqrt(jnp.sqrt(scale_left)) * times_root(start, off_left_ref, diag_left, quarter_left)
    high = root.astype(BF16)
    low = (root - high.astype(F32)).astype(BF16)
    both = dot(jnp.concatenate([high, low], axis=0), grad_t_ref[...])
    mixed = both[:128] + both[128:]
    turned = 1.25 * mixed - quarter_right * times_factor(mixed, off_right_ref, diag_right)
    update = jnp.sqrt(jnp.sqrt(scale_right)) * times_root(
        turned, off_right_ref, diag_right, quarter_right
    )
    squares = jnp.sum(jnp.sum(update * update, axis=0, keepdims=True), axis=1, keepdims=True)
    high = squares.astype(BF16).astype(F32)
    middle = (squares - high).astype(BF16).astype(F32)
    low = squares - high - middle
    row = lax.broadcasted_iota(jnp.int32, (16, 256), 0)
    tail = jnp.where(row == 0, high, jnp.where(row == 1, middle, jnp.where(row == 2, low, 0.0)))
    tail = tail.astype(BF16)
    for y in range(4):
        sent_buf[y, :128, :] = update[:, y * 256 : (y + 1) * 256].astype(BF16)
        sent_buf[y, 128:, :] = tail
    stores = [
        pltpu.make_async_copy(sent_buf, sent_ref.at[pl.ds(zl * 4, 4)], sems.at[4 + zl])
        for zl in range(2)
    ]
    for store in stores:
        store.start()
    update_buf[...] = update
    stores.append(pltpu.make_async_copy(update_buf, update_ref, sems.at[6]))
    stores[-1].start()
    for store in [store_left, store_right, *stores]:
        store.wait()


def solve(place, pieces, left_old, right_old):
    square = (BLOCK, BLOCK)
    rows = pltpu.HBM((128, BLOCK), F32)
    return call(
        solver_body,
        [HBM, *[VMEM] * 7, HBM, HBM],
        [HBM] * 4,
        [rows, rows, rows, pltpu.HBM((8, 144, 256), BF16)],
        scratch=[
            pltpu.VMEM((8, 256, 512), BF16),
            *[pltpu.VMEM(square, kind) for kind in (F32, F32, BF16, BF16, F32, BF16, BF16)],
            pltpu.VMEM((128, BLOCK), F32),
            pltpu.VMEM((128, BLOCK), F32),
            pltpu.VMEM((4, 144, 256), BF16),
            pltpu.SemaphoreType.DMA((8,)),
        ],
        limit=27,
        name="solve",
    )(place, *pieces, left_old, right_old)


def body(activations, cotangent, weight, left_old, right_old):
    place = jnp.stack([lax.axis_index(a).astype(jnp.int32) for a in AXES])
    cot_turned = lax.ppermute(cotangent, AXES, SWAP)
    packed = pack(place, activations, weight)
    crossed = [lax.ppermute(packed[d], "y", shift(d)) for d in range(1, 4)]
    cot_turned, crossed[0], crossed[2] = lax.optimization_barrier(
        (cot_turned, crossed[0], crossed[2])
    )
    cot_all = copies_to(cot_turned, ZAX, 8)
    slab, near_w = unpack(place, [packed[0], *crossed])
    own = [slab] + [lax.ppermute(slab, "x", shift(d)) for d in range(1, 4)]
    swapped = [lax.ppermute(part, "c", FLIP) for part in own]
    first, near, away = first_partial(place, near_w, own, swapped)
    cot_all, first = lax.optimization_barrier((cot_all, first))
    first_parts = lax.all_to_all(first, ZAX, 0, 0, tiled=True)
    piece, kept = grad_piece(place, cot_all, own, swapped)

    beside = lax.ppermute(piece, "zl", FLIP)
    pieces = [in_hbm(kept)] + [lax.ppermute(piece, "y", shift(d)) for d in range(1, 4)]
    pieces += [beside] + [lax.ppermute(beside, "y", shift(d)) for d in range(1, 4)]
    away, *pieces = lax.optimization_barrier((away, *pieces))
    far = lax.ppermute(away, "zl", FLIP)
    new_left, new_right, update, sent = solve(
        place, pieces, in_hbm(left_old[0, 0]), in_hbm(right_old[0, 0])
    )
    sent, first_parts = lax.optimization_barrier((sent, first_parts))
    update_cols = lax.all_to_all(sent, SOLVER, 0, 0, tiled=True)
    far, sent = lax.optimization_barrier((far, sent))
    far_swapped = lax.ppermute(far, "c", FLIP)
    first_sum = add_up(place, first_parts)
    near_w, first_out = lax.optimization_barrier((near_w, lax.ppermute(first_sum, AXES, SWAP)))

    second, spread = second_partial(place, update_cols, near_w, near, far, far_swapped)
    arrived = lax.all_to_all(second, "zh", 0, 0, tiled=True)
    second_out = lax.ppermute(add_up(place, arrived), AXES, SWAP)
    direction = update / spread[0, 0]
    return (first_out, new_left[None, None], new_right[None, None], direction, second_out)


def solution(mesh):
    fine = Mesh(mesh.devices.reshape(4, 2, 4, 2, 4), AXES)
    rows = ("zh", "zl", "y")
    in_specs = (
        P(BATCH, rows),
        P(rows, BATCH),
        P(rows, BATCH),
        P("zh", BATCH, None, None),
        P("zh", BATCH, None, None),
    )
    out_specs = (
        P(rows, BATCH),
        P("zh", BATCH, SOLVER, None),
        P("zh", BATCH, SOLVER, None),
        P(rows, BATCH),
        P(rows, BATCH),
    )
    return jax.shard_map(body, mesh=fine, in_specs=in_specs, out_specs=out_specs, check_vma=False)
```

```python
import jax
import jax.numpy as jnp
from jax import lax
from jax.experimental import pallas as pl
from jax.experimental.pallas import tpu as pltpu
from jax.sharding import Mesh
from jax.sharding import PartitionSpec as P

BLOCK = 1024
STAT_DECAY = 0.8
LEARN_RATE = 0.005
EPSILON = 1e-06

AXES = ("x", "c", "zh", "zl", "y")
BATCH = ("x", "c")
ZAX = ("zh", "zl")
SOLVER = ("zl", "y")
MIB = 1 << 20
SHAPE = jax.ShapeDtypeStruct
BF16 = jnp.bfloat16
F32 = jnp.float32


def device(x, c, zh, zl, y):
    return (((x * 2 + c) * 4 + zh) * 2 + zl) * 4 + y


EVERY = [
    (x, c, zh, zl, y)
    for x in range(4)
    for c in range(2)
    for zh in range(4)
    for zl in range(2)
    for y in range(4)
]
SWAP = [(device(*d), device(d[2], d[3], d[0], d[1], d[4])) for d in EVERY]
FLIP = [(0, 1), (1, 0)]


def shift(by):
    return [(i, (i + by) % 4) for i in range(4)]


def copies_to(shard, axis, count):
    copies = jnp.broadcast_to(shard, (count, *shard.shape))
    return lax.all_to_all(copies, axis, split_axis=0, concat_axis=0, tiled=True)


def dot(a, b):
    return jnp.dot(a, b, preferred_element_type=F32)


def dot_minor(a, b):
    return lax.dot_general(a, b, (((1,), (1,)), ((), ())), preferred_element_type=F32)


VMEM = pl.BlockSpec(memory_space=pltpu.VMEM)
HBM = pl.BlockSpec(memory_space=pltpu.HBM)


def call(body, in_specs, out_specs, out_shape, scratch=(), limit=24, name=None):
    return pl.pallas_call(
        body,
        out_shape=out_shape,
        in_specs=[pl.BlockSpec(memory_space=pltpu.SMEM), *in_specs],
        out_specs=out_specs,
        scratch_shapes=list(scratch),
        compiler_params=pltpu.CompilerParams(vmem_limit_bytes=limit * MIB),
        name=name,
    )


def in_hbm(value):
    return pltpu.with_memory_space_constraint(value, pltpu.HBM)


def wide(slab):
    return jnp.concatenate([slab[q] for q in range(4)], axis=1)


def pack_body(place, acts_hbm, weight_hbm, *refs):
    outs, (acts_ref, weight_ref, work, sems) = refs[:4], refs[4:]
    loads = [
        pltpu.make_async_copy(weight_hbm, weight_ref, sems.at[0]),
        pltpu.make_async_copy(acts_hbm, acts_ref, sems.at[1]),
    ]
    for load in loads:
        load.start()
    for load in loads:
        load.wait()
    for q in range(4):
        for half in range(2):
            at = q * 256 + half * 128
            work[q, half * 128 : (half + 1) * 128, :] = weight_ref[:, at : at + 128]
    acts = acts_ref[...]
    for d in range(4):
        outs[d][:256, :] = acts
        outs[d][256:, :] = work[(place[4] + d) & 3]


def pack(place, acts, weight):
    part = SHAPE((512, 128), BF16)
    return call(
        pack_body,
        [HBM] * 2,
        [VMEM] * 4,
        [part] * 4,
        scratch=[
            pltpu.VMEM((256, 128), BF16),
            pltpu.VMEM((128, 1024), BF16),
            pltpu.VMEM((4, 256, 128), BF16),
            pltpu.SemaphoreType.DMA((2,)),
        ],
        limit=8,
        name="pack",
    )(place, in_hbm(acts), in_hbm(weight))


def unpack_body(place, *refs):
    for d in range(4):
        at = (place[4] - d) & 3
        refs[4][at] = refs[d][:256, :]
        refs[5][at] = refs[d][256:, :]


def unpack(place, parts):
    shape = SHAPE((4, 256, 128), BF16)
    return call(unpack_body, [VMEM] * 4, [VMEM] * 2, [shape] * 2, limit=8, name="unpack")(
        place, *parts
    )


def weight_of(parts):
    rows = [jnp.concatenate([parts[q, :128, :], parts[q, 128:, :]], axis=1) for q in range(4)]
    return jnp.concatenate(rows, axis=0)


def grad_body(place, cot_ref, *refs):
    own, swapped = refs[:4], refs[4:8]
    copies_ref, acts_ref, piece_ref, sems = refs[8:]
    x, c = place[0], place[1]
    sends = []
    for d in range(4):
        at = ((x - d) & 3) * 2
        sends.append(pltpu.make_async_copy(own[d], acts_ref.at[at + c], sems.at[d]))
        sends.append(pltpu.make_async_copy(swapped[d], acts_ref.at[at + 1 - c], sems.at[4 + d]))
    for send in sends:
        send.start()
    total = jnp.zeros((256, 512), F32)
    for d in range(4):
        at = ((x - d) & 3) * 2
        total = total + dot(cot_ref[at + c], wide(own[d]))
        total = total + dot(cot_ref[at + 1 - c], wide(swapped[d]))
    piece_ref[...] = total.astype(BF16)
    for s in range(8):
        sends.append(pltpu.make_async_copy(piece_ref, copies_ref.at[s], sems.at[8 + s]))
        sends[-1].start()
    for send in sends:
        send.wait()


def grad_piece(place, cot_all, own, swapped):
    return call(
        grad_body,
        [VMEM] * 9,
        [HBM, HBM],
        [pltpu.HBM((8, 256, 512), BF16), pltpu.HBM((8, 4, 256, 128), BF16)],
        scratch=[pltpu.VMEM((256, 512), BF16), pltpu.SemaphoreType.DMA((16,))],
        limit=10,
        name="grad_piece",
    )(place, cot_all, *own, *swapped)


def first_body(place, weight_ref, acts_ref, out_ref, work, sems):
    weight_t = weight_of(weight_ref).T
    sends = []
    for group in range(8):
        work[group] = dot_minor(weight_t, wide(acts_ref.at[group])).astype(BF16)
        sends.append(pltpu.make_async_copy(work.at[group], out_ref.at[group], sems.at[group]))
        sends[-1].start()
    for send in sends:
        send.wait()


def first_partial(place, near_w, acts):
    return call(
        first_body,
        [VMEM] * 2,
        HBM,
        pltpu.HBM((8, 256, 256), BF16),
        scratch=[pltpu.VMEM((8, 256, 256), BF16), pltpu.SemaphoreType.DMA((8,))],
        limit=12,
        name="first_partial",
    )(place, near_w, acts)


def as_rows(value):
    high = value.astype(BF16).astype(F32)
    middle = (value - high).astype(BF16).astype(F32)
    low = value - high - middle
    row = lax.broadcasted_iota(jnp.int32, (16, 256), 0)
    rows = jnp.where(row == 0, high, jnp.where(row == 1, middle, jnp.where(row == 2, low, 0.0)))
    return rows.astype(BF16)


def from_rows(rows):
    return jnp.sum(rows.astype(F32), axis=0, keepdims=True)[:, :1]


def second_body(place, u0, u1, u2, u3, acts_ref, out_ref, squares_ref, update_ref, work, sems):
    squares = jnp.zeros((1, 1), F32)
    for d, piece in enumerate((u0, u1, u2, u3)):
        update_ref[(place[4] - d) & 3] = piece[:128, :]
        squares = squares + from_rows(piece[128:, :])
    squares_ref[...] = jnp.broadcast_to(squares, (8, 128))
    tail = as_rows(squares)
    update_t = update_ref[...].reshape(512, 256).T
    sends = []
    for group in range(8):
        work[group, :256, :] = dot_minor(update_t, wide(acts_ref.at[group])).astype(BF16)
        work[group, 256:, :] = tail
        sends.append(pltpu.make_async_copy(work.at[group], out_ref.at[group], sems.at[group]))
        sends[-1].start()
    for send in sends:
        send.wait()


def second_partial(place, update_parts, acts):
    return call(
        second_body,
        [VMEM] * 5,
        [HBM, VMEM],
        [pltpu.HBM((8, 272, 256), BF16), SHAPE((8, 128), F32)],
        scratch=[
            pltpu.VMEM((4, 128, 256), BF16),
            pltpu.VMEM((8, 272, 256), BF16),
            pltpu.SemaphoreType.DMA((8,)),
        ],
        limit=12,
        name="second_partial",
    )(place, *update_parts, acts)


def first_add_body(place, parts_ref, total_ref, out_ref):
    total = parts_ref[0].astype(F32)
    for i in range(1, 8):
        total = total + parts_ref[i].astype(F32)
    total_ref[...] = total
    out_ref[...] = total.astype(BF16)


def first_add(place, parts):
    shape = (256, 256)
    return call(
        first_add_body,
        [VMEM],
        [VMEM] * 2,
        [SHAPE(shape, F32), SHAPE(shape, BF16)],
        limit=8,
        name="first_add",
    )(place, parts)


def second_add_body(place, total_ref, parts_ref, out_ref):
    total = total_ref[...]
    for h in range(4):
        squares = from_rows(parts_ref[2 * h, 256:, :]) + from_rows(parts_ref[2 * h + 1, 256:, :])
        rate = LEARN_RATE / jnp.sqrt(squares / (BLOCK * BLOCK) + EPSILON)
        change = parts_ref[2 * h, :256, :].astype(F32) + parts_ref[2 * h + 1, :256, :].astype(F32)
        total = total - rate * change
    out_ref[...] = total.astype(BF16)


def second_add(place, total, parts):
    return call(
        second_add_body,
        [VMEM] * 2,
        VMEM,
        SHAPE((256, 256), BF16),
        limit=8,
        name="second_add",
    )(place, total, parts)


def statistics(lhs_ref, rhs_ref, old_ref, full_ref, off_ref):
    tile = 256
    sums = jnp.zeros((1, BLOCK), F32)
    diag = jnp.zeros((1, BLOCK), F32)
    for i in range(BLOCK // tile):
        rows = pl.ds(i * tile, tile)
        gram = dot(lhs_ref[rows, :], rhs_ref[...])
        new = STAT_DECAY * old_ref[rows, :] + (1.0 - STAT_DECAY) / BLOCK * gram
        full_ref[rows, :] = new
        sums = sums + jnp.sum(jnp.abs(new), axis=0, keepdims=True)
        row = lax.broadcasted_iota(jnp.int32, (tile, BLOCK), 0) + i * tile
        col = lax.broadcasted_iota(jnp.int32, (tile, BLOCK), 1)
        on_diag = row == col
        diag = diag + jnp.sum(jnp.where(on_diag, new, 0.0), axis=0, keepdims=True)
        off_ref[rows, :] = jnp.where(on_diag, 0.0, new).astype(BF16)
    scale = 2.5 / (jnp.max(sums, axis=1, keepdims=True) + EPSILON)
    return scale, diag


def times_factor(rows, off_ref, diag):
    return rows * diag + dot(rows.astype(BF16), off_ref[...])


def times_root(start, off_ref, diag, quarter):
    value = start
    for _ in range(4):
        value = 1.25 * value - quarter * times_factor(value, off_ref, diag)
    return 1.25 * start - quarter * times_factor(value, off_ref, diag)


def solver_body(
    place,
    pieces_ref,
    left_old_ref,
    right_old_ref,
    new_left_ref,
    new_right_ref,
    update_ref,
    sent0,
    sent1,
    sent2,
    sent3,
    left_buf,
    right_buf,
    grad_ref,
    grad_t_ref,
    full_ref,
    off_left_ref,
    off_right_ref,
    rows_buf,
    update_buf,
    sent_buf,
    sems,
):
    load_left = pltpu.make_async_copy(left_old_ref, left_buf, sems.at[0])
    load_right = pltpu.make_async_copy(right_old_ref, right_buf, sems.at[1])
    load_left.start()
    load_right.start()
    first = pl.multiple_of((place[3] * 4 + place[4]) * 128, 128)
    own = pl.ds(first, 128)
    for zl in range(2):
        for y in range(4):
            piece = pieces_ref[zl * 4 + y]
            grad_ref[pl.ds(y * 256, 256), pl.ds(zl * 512, 512)] = piece
            grad_t_ref[pl.ds(zl * 512, 512), pl.ds(y * 256, 256)] = piece.T
    load_left.wait()
    scale_left, diag_left = statistics(grad_t_ref, grad_ref, left_buf, full_ref, off_left_ref)
    left_rows = full_ref[own, :]
    rows_buf[...] = left_rows
    store_left = pltpu.make_async_copy(rows_buf, new_left_ref, sems.at[2])
    store_left.start()
    load_right.wait()
    scale_right, diag_right = statistics(
        grad_ref, grad_t_ref, right_buf, full_ref, off_right_ref
    )
    store_right = pltpu.make_async_copy(full_ref.at[own, :], new_right_ref, sems.at[3])
    store_right.start()
    quarter_left = scale_left * 0.25
    quarter_right = scale_right * 0.25
    row = lax.broadcasted_iota(jnp.int32, (128, BLOCK), 0) + first
    col = lax.broadcasted_iota(jnp.int32, (128, BLOCK), 1)
    start = jnp.where(row == col, 1.25, 0.0) - quarter_left * left_rows
    root = jnp.sqrt(jnp.sqrt(scale_left)) * times_root(start, off_left_ref, diag_left, quarter_left)
    high = root.astype(BF16)
    low = (root - high.astype(F32)).astype(BF16)
    both = dot(jnp.concatenate([high, low], axis=0), grad_t_ref[...])
    mixed = both[:128] + both[128:]
    turned = 1.25 * mixed - quarter_right * times_factor(mixed, off_right_ref, diag_right)
    update = jnp.sqrt(jnp.sqrt(scale_right)) * times_root(
        turned, off_right_ref, diag_right, quarter_right
    )
    squares = jnp.sum(jnp.sum(update * update, axis=0, keepdims=True), axis=1, keepdims=True)
    tail = as_rows(squares)
    for y in range(4):
        sent_buf[y, :128, :] = update[:, y * 256 : (y + 1) * 256].astype(BF16)
        sent_buf[y, 128:, :] = tail
    stores = [
        pltpu.make_async_copy(sent_buf.at[(place[4] + d) & 3], sent, sems.at[4 + d])
        for d, sent in enumerate((sent0, sent1, sent2, sent3))
    ]
    for store in stores:
        store.start()
    update_buf[...] = update
    stores.append(pltpu.make_async_copy(update_buf, update_ref, sems.at[8]))
    stores[-1].start()
    for store in [store_left, store_right, *stores]:
        store.wait()


def solve(place, pieces, left_old, right_old):
    square = (BLOCK, BLOCK)
    rows = pltpu.HBM((128, BLOCK), F32)
    return call(
        solver_body,
        [VMEM, HBM, HBM],
        [HBM] * 7,
        [rows, rows, rows, *[pltpu.HBM((144, 256), BF16)] * 4],
        scratch=[
            *[pltpu.VMEM(square, kind) for kind in (F32, F32, BF16, BF16, F32, BF16, BF16)],
            pltpu.VMEM((128, BLOCK), F32),
            pltpu.VMEM((128, BLOCK), F32),
            pltpu.VMEM((4, 144, 256), BF16),
            pltpu.SemaphoreType.DMA((9,)),
        ],
        limit=27,
        name="solve",
    )(place, pieces, left_old, right_old)


def body(activations, cotangent, weight, left_old, right_old):
    place = jnp.stack([lax.axis_index(a).astype(jnp.int32) for a in AXES])
    cot_turned = lax.ppermute(cotangent, AXES, SWAP)
    packed = pack(place, activations, weight)
    crossed = [lax.ppermute(packed[d], "y", shift(d)) for d in range(1, 4)]
    cot_turned, crossed[0], crossed[2] = lax.optimization_barrier(
        (cot_turned, crossed[0], crossed[2])
    )
    cot_all = copies_to(cot_turned, ZAX, 8)
    slab, near_w = unpack(place, [packed[0], *crossed])
    own = [slab] + [lax.ppermute(slab, "x", shift(d)) for d in range(1, 4)]
    swapped = [lax.ppermute(part, "c", FLIP) for part in own]
    copies, acts = grad_piece(place, cot_all, own, swapped)

    pieces = lax.all_to_all(copies, SOLVER, 0, 0, tiled=True)
    first = first_partial(place, near_w, acts)
    pieces, first = lax.optimization_barrier((pieces, first))
    first_parts = lax.all_to_all(first, ZAX, 0, 0, tiled=True)
    new_left, new_right, update, *sent = solve(
        place, pieces, in_hbm(left_old[0, 0]), in_hbm(right_old[0, 0])
    )
    update_parts = [sent[0]] + [lax.ppermute(sent[d], "y", shift(d)) for d in range(1, 4)]
    second, squares = second_partial(place, update_parts, acts)
    second, first_parts = lax.optimization_barrier((second, first_parts))
    arrived = lax.all_to_all(second, ZAX, 0, 0, tiled=True)
    first_total, first_sum = first_add(place, first_parts)
    first_out = lax.ppermute(first_sum, AXES, SWAP)
    second_out = lax.ppermute(second_add(place, first_total, arrived), AXES, SWAP)
    total = squares[0, 0] + lax.ppermute(squares, "zl", FLIP)[0, 0]
    direction = update / jnp.sqrt(total / (BLOCK * BLOCK) + EPSILON)
    return (first_out, new_left[None, None], new_right[None, None], direction, second_out)


def solution(mesh):
    fine = Mesh(mesh.devices.reshape(4, 2, 4, 2, 4), AXES)
    rows = ("zh", "zl", "y")
    in_specs = (
        P(BATCH, rows),
        P(rows, BATCH),
        P(rows, BATCH),
        P("zh", BATCH, None, None),
        P("zh", BATCH, None, None),
    )
    out_specs = (
        P(rows, BATCH),
        P("zh", BATCH, SOLVER, None),
        P("zh", BATCH, SOLVER, None),
        P(rows, BATCH),
        P(rows, BATCH),
    )
    return jax.shard_map(body, mesh=fine, in_specs=in_specs, out_specs=out_specs, check_vma=False)
```

```python
import jax
import jax.numpy as jnp
from jax import lax
from jax.experimental import pallas as pl
from jax.experimental.pallas import tpu as pltpu
from jax.sharding import Mesh
from jax.sharding import PartitionSpec as P

BLOCK = 1024
STAT_DECAY = 0.8
LEARN_RATE = 0.005
EPSILON = 1e-06

AXES = ("x", "c", "zh", "zl", "y")
BATCH = ("x", "c")
ZAX = ("zh", "zl")
SOLVER = ("zl", "y")
MIB = 1 << 20
SHAPE = jax.ShapeDtypeStruct
BF16 = jnp.bfloat16
F32 = jnp.float32


def device(x, c, zh, zl, y):
    return (((x * 2 + c) * 4 + zh) * 2 + zl) * 4 + y


EVERY = [
    (x, c, zh, zl, y)
    for x in range(4)
    for c in range(2)
    for zh in range(4)
    for zl in range(2)
    for y in range(4)
]
SWAP = [(device(*d), device(d[2], d[3], d[0], d[1], d[4])) for d in EVERY]
FLIP = [(0, 1), (1, 0)]


def shift(by):
    return [(i, (i + by) % 4) for i in range(4)]


def copies_to(shard, axis, count):
    copies = jnp.broadcast_to(shard, (count, *shard.shape))
    return lax.all_to_all(copies, axis, split_axis=0, concat_axis=0, tiled=True)


def dot(a, b):
    return jnp.dot(a, b, preferred_element_type=F32)


def dot_minor(a, b):
    return lax.dot_general(a, b, (((1,), (1,)), ((), ())), preferred_element_type=F32)


VMEM = pl.BlockSpec(memory_space=pltpu.VMEM)
HBM = pl.BlockSpec(memory_space=pltpu.HBM)


def call(body, in_specs, out_specs, out_shape, scratch=(), limit=24, name=None):
    return pl.pallas_call(
        body,
        out_shape=out_shape,
        in_specs=[pl.BlockSpec(memory_space=pltpu.SMEM), *in_specs],
        out_specs=out_specs,
        scratch_shapes=list(scratch),
        compiler_params=pltpu.CompilerParams(vmem_limit_bytes=limit * MIB),
        name=name,
    )


def in_hbm(value):
    return pltpu.with_memory_space_constraint(value, pltpu.HBM)


def wide(slab):
    return jnp.concatenate([slab[q] for q in range(4)], axis=1)


def pack_body(place, acts_hbm, weight_hbm, *refs):
    outs, (acts_ref, weight_ref, work, sems) = refs[:4], refs[4:]
    loads = [
        pltpu.make_async_copy(weight_hbm, weight_ref, sems.at[0]),
        pltpu.make_async_copy(acts_hbm, acts_ref, sems.at[1]),
    ]
    for load in loads:
        load.start()
    for load in loads:
        load.wait()
    for q in range(4):
        for half in range(2):
            at = q * 256 + half * 128
            work[q, half * 128 : (half + 1) * 128, :] = weight_ref[:, at : at + 128]
    acts = acts_ref[...]
    for d in range(4):
        outs[d][:256, :] = acts
        outs[d][256:, :] = work[(place[4] + d) & 3]


def pack(place, acts, weight):
    part = SHAPE((512, 128), BF16)
    return call(
        pack_body,
        [HBM] * 2,
        [VMEM] * 4,
        [part] * 4,
        scratch=[
            pltpu.VMEM((256, 128), BF16),
            pltpu.VMEM((128, 1024), BF16),
            pltpu.VMEM((4, 256, 128), BF16),
            pltpu.SemaphoreType.DMA((2,)),
        ],
        limit=8,
        name="pack",
    )(place, in_hbm(acts), in_hbm(weight))


def unpack_body(place, *refs):
    for d in range(4):
        at = (place[4] - d) & 3
        refs[4][at] = refs[d][:256, :]
        refs[5][at] = refs[d][256:, :]


def unpack(place, parts):
    shape = SHAPE((4, 256, 128), BF16)
    return call(unpack_body, [VMEM] * 4, [VMEM] * 2, [shape] * 2, limit=8, name="unpack")(
        place, *parts
    )


def weight_of(parts):
    rows = [jnp.concatenate([parts[q, :128, :], parts[q, 128:, :]], axis=1) for q in range(4)]
    return jnp.concatenate(rows, axis=0)


def grad_body(place, cot_ref, *refs):
    own, swapped = refs[:4], refs[4:8]
    copies_ref, acts_ref, piece_ref, sems = refs[8:]
    x, c = place[0], place[1]
    sends = []
    for d in range(4):
        at = ((x - d) & 3) * 2
        sends.append(pltpu.make_async_copy(own[d], acts_ref.at[at + c], sems.at[d]))
        sends.append(pltpu.make_async_copy(swapped[d], acts_ref.at[at + 1 - c], sems.at[4 + d]))
    for send in sends:
        send.start()
    total = jnp.zeros((256, 512), F32)
    for d in range(4):
        at = ((x - d) & 3) * 2
        total = total + dot(cot_ref[at + c], wide(own[d]))
        total = total + dot(cot_ref[at + 1 - c], wide(swapped[d]))
    piece_ref[...] = total.astype(BF16)
    for s in range(8):
        sends.append(pltpu.make_async_copy(piece_ref, copies_ref.at[s], sems.at[8 + s]))
        sends[-1].start()
    for send in sends:
        send.wait()


def grad_piece(place, cot_all, own, swapped):
    return call(
        grad_body,
        [VMEM] * 9,
        [HBM, HBM],
        [pltpu.HBM((8, 256, 512), BF16), pltpu.HBM((8, 4, 256, 128), BF16)],
        scratch=[pltpu.VMEM((256, 512), BF16), pltpu.SemaphoreType.DMA((16,))],
        limit=10,
        name="grad_piece",
    )(place, cot_all, *own, *swapped)


def first_body(place, weight_ref, acts_hbm, out_ref, acts_ref, work, sems):
    loads = [
        pltpu.make_async_copy(acts_hbm.at[group], acts_ref.at[group], sems.at[8 + group])
        for group in range(8)
    ]
    for load in loads:
        load.start()
    weight_t = weight_of(weight_ref).T
    sends = []
    for group in range(8):
        loads[group].wait()
        work[group] = dot_minor(weight_t, wide(acts_ref.at[group])).astype(BF16)
        sends.append(pltpu.make_async_copy(work.at[group], out_ref.at[group], sems.at[group]))
        sends[-1].start()
    for send in sends:
        send.wait()


def first_partial(place, near_w, acts):
    return call(
        first_body,
        [VMEM, HBM],
        HBM,
        pltpu.HBM((8, 256, 256), BF16),
        scratch=[
            pltpu.VMEM((8, 4, 256, 128), BF16),
            pltpu.VMEM((8, 256, 256), BF16),
            pltpu.SemaphoreType.DMA((16,)),
        ],
        limit=12,
        name="first_partial",
    )(place, near_w, in_hbm(acts))


def as_rows(value):
    high = value.astype(BF16).astype(F32)
    middle = (value - high).astype(BF16).astype(F32)
    low = value - high - middle
    row = lax.broadcasted_iota(jnp.int32, (16, 256), 0)
    rows = jnp.where(row == 0, high, jnp.where(row == 1, middle, jnp.where(row == 2, low, 0.0)))
    return rows.astype(BF16)


def from_rows(rows):
    return jnp.sum(rows.astype(F32), axis=0, keepdims=True)[:, :1]


def second_body(place, own_hbm, u1, u2, u3, acts_ref, out_ref, own_ref, update_ref, work, sems):
    load = pltpu.make_async_copy(own_hbm, own_ref, sems.at[8])
    load.start()
    squares = jnp.zeros((1, 1), F32)
    for d, piece in ((1, u1), (2, u2), (3, u3), (0, own_ref)):
        if d == 0:
            load.wait()
        update_ref[(place[4] - d) & 3] = piece[:128, :]
        squares = squares + from_rows(piece[128:, :])
    tail = as_rows(squares)
    update_t = update_ref[...].reshape(512, 256).T
    sends = []
    for group in range(8):
        work[group, :256, :] = dot_minor(update_t, wide(acts_ref.at[group])).astype(BF16)
        work[group, 256:, :] = tail
        sends.append(pltpu.make_async_copy(work.at[group], out_ref.at[group], sems.at[group]))
        sends[-1].start()
    for send in sends:
        send.wait()


def second_partial(place, update_parts, acts):
    return call(
        second_body,
        [HBM, *[VMEM] * 4],
        HBM,
        pltpu.HBM((8, 272, 256), BF16),
        scratch=[
            pltpu.VMEM((144, 256), BF16),
            pltpu.VMEM((4, 128, 256), BF16),
            pltpu.VMEM((8, 272, 256), BF16),
            pltpu.SemaphoreType.DMA((9,)),
        ],
        limit=12,
        name="second_partial",
    )(place, *update_parts, acts)


def first_add_body(place, parts_ref, total_ref, out_ref):
    total = parts_ref[0].astype(F32)
    for i in range(1, 8):
        total = total + parts_ref[i].astype(F32)
    total_ref[...] = total
    out_ref[...] = total.astype(BF16)


def first_add(place, parts):
    shape = (256, 256)
    return call(
        first_add_body,
        [VMEM],
        [VMEM] * 2,
        [SHAPE(shape, F32), SHAPE(shape, BF16)],
        limit=8,
        name="first_add",
    )(place, parts)


def second_add_body(place, total_ref, parts_ref, out_ref, spread_ref):
    total = total_ref[...]
    own = jnp.zeros((1, 1), F32)
    for h in range(4):
        squares = from_rows(parts_ref[2 * h, 256:, :]) + from_rows(parts_ref[2 * h + 1, 256:, :])
        spread = jnp.sqrt(squares / (BLOCK * BLOCK) + EPSILON)
        own = jnp.where(place[2] == h, spread, own)
        rate = LEARN_RATE / spread
        change = parts_ref[2 * h, :256, :].astype(F32) + parts_ref[2 * h + 1, :256, :].astype(F32)
        total = total - rate * change
    out_ref[...] = total.astype(BF16)
    spread_ref[...] = jnp.broadcast_to(own, (8, 128))


def second_add(place, total, parts):
    return call(
        second_add_body,
        [VMEM] * 2,
        [VMEM] * 2,
        [SHAPE((256, 256), BF16), SHAPE((8, 128), F32)],
        limit=8,
        name="second_add",
    )(place, total, parts)


def statistics(lhs_ref, rhs_ref, old_ref, full_ref, off_ref):
    tile = 256
    sums = jnp.zeros((1, BLOCK), F32)
    diag = jnp.zeros((1, BLOCK), F32)
    for i in range(BLOCK // tile):
        rows = pl.ds(i * tile, tile)
        gram = dot(lhs_ref[rows, :], rhs_ref[...])
        new = STAT_DECAY * old_ref[rows, :] + (1.0 - STAT_DECAY) / BLOCK * gram
        full_ref[rows, :] = new
        sums = sums + jnp.sum(jnp.abs(new), axis=0, keepdims=True)
        row = lax.broadcasted_iota(jnp.int32, (tile, BLOCK), 0) + i * tile
        col = lax.broadcasted_iota(jnp.int32, (tile, BLOCK), 1)
        on_diag = row == col
        diag = diag + jnp.sum(jnp.where(on_diag, new, 0.0), axis=0, keepdims=True)
        off_ref[rows, :] = jnp.where(on_diag, 0.0, new).astype(BF16)
    scale = 2.5 / (jnp.max(sums, axis=1, keepdims=True) + EPSILON)
    return scale, diag


def times_factor(rows, off_ref, diag):
    return rows * diag + dot(rows.astype(BF16), off_ref[...])


def times_root(start, off_ref, diag, quarter):
    value = start
    for _ in range(4):
        value = 1.25 * value - quarter * times_factor(value, off_ref, diag)
    return 1.25 * start - quarter * times_factor(value, off_ref, diag)


def solver_body(
    place,
    pieces_ref,
    left_old_ref,
    right_old_ref,
    new_left_ref,
    new_right_ref,
    update_ref,
    sent0,
    sent1,
    sent2,
    sent3,
    pieces_buf,
    left_buf,
    right_buf,
    grad_ref,
    grad_t_ref,
    full_ref,
    off_left_ref,
    off_right_ref,
    rows_buf,
    update_buf,
    sent_buf,
    sems,
):
    load_left = pltpu.make_async_copy(left_old_ref, left_buf, sems.at[0])
    load_right = pltpu.make_async_copy(right_old_ref, right_buf, sems.at[1])
    loads = [
        pltpu.make_async_copy(pieces_ref.at[s], pieces_buf.at[s], sems.at[9 + s]) for s in range(8)
    ]
    for load in loads:
        load.start()
    load_left.start()
    load_right.start()
    first = pl.multiple_of((place[3] * 4 + place[4]) * 128, 128)
    own = pl.ds(first, 128)
    for zl in range(2):
        for y in range(4):
            loads[zl * 4 + y].wait()
            piece = pieces_buf[zl * 4 + y]
            grad_ref[pl.ds(y * 256, 256), pl.ds(zl * 512, 512)] = piece
            grad_t_ref[pl.ds(zl * 512, 512), pl.ds(y * 256, 256)] = piece.T
    load_left.wait()
    scale_left, diag_left = statistics(grad_t_ref, grad_ref, left_buf, full_ref, off_left_ref)
    left_rows = full_ref[own, :]
    rows_buf[...] = left_rows
    store_left = pltpu.make_async_copy(rows_buf, new_left_ref, sems.at[2])
    store_left.start()
    load_right.wait()
    scale_right, diag_right = statistics(
        grad_ref, grad_t_ref, right_buf, full_ref, off_right_ref
    )
    store_right = pltpu.make_async_copy(full_ref.at[own, :], new_right_ref, sems.at[3])
    store_right.start()
    quarter_left = scale_left * 0.25
    quarter_right = scale_right * 0.25
    row = lax.broadcasted_iota(jnp.int32, (128, BLOCK), 0) + first
    col = lax.broadcasted_iota(jnp.int32, (128, BLOCK), 1)
    start = jnp.where(row == col, 1.25, 0.0) - quarter_left * left_rows
    root = jnp.sqrt(jnp.sqrt(scale_left)) * times_root(start, off_left_ref, diag_left, quarter_left)
    high = root.astype(BF16)
    low = (root - high.astype(F32)).astype(BF16)
    both = dot(jnp.concatenate([high, low], axis=0), grad_t_ref[...])
    mixed = both[:128] + both[128:]
    turned = 1.25 * mixed - quarter_right * times_factor(mixed, off_right_ref, diag_right)
    update = jnp.sqrt(jnp.sqrt(scale_right)) * times_root(
        turned, off_right_ref, diag_right, quarter_right
    )
    squares = jnp.sum(jnp.sum(update * update, axis=0, keepdims=True), axis=1, keepdims=True)
    tail = as_rows(squares)
    for y in range(4):
        sent_buf[y, :128, :] = update[:, y * 256 : (y + 1) * 256].astype(BF16)
        sent_buf[y, 128:, :] = tail
    stores = [
        pltpu.make_async_copy(sent_buf.at[(place[4] + d) & 3], sent, sems.at[4 + d])
        for d, sent in enumerate((sent0, sent1, sent2, sent3))
    ]
    for store in stores:
        store.start()
    update_buf[...] = update
    stores.append(pltpu.make_async_copy(update_buf, update_ref, sems.at[8]))
    stores[-1].start()
    for store in [store_left, store_right, *stores]:
        store.wait()


def solve(place, pieces, left_old, right_old):
    square = (BLOCK, BLOCK)
    rows = pltpu.HBM((128, BLOCK), F32)
    return call(
        solver_body,
        [HBM] * 3,
        [HBM] * 7,
        [rows, rows, rows, *[pltpu.HBM((144, 256), BF16)] * 4],
        scratch=[
            pltpu.VMEM((8, 256, 512), BF16),
            *[pltpu.VMEM(square, kind) for kind in (F32, F32, BF16, BF16, F32, BF16, BF16)],
            pltpu.VMEM((128, BLOCK), F32),
            pltpu.VMEM((128, BLOCK), F32),
            pltpu.VMEM((4, 144, 256), BF16),
            pltpu.SemaphoreType.DMA((17,)),
        ],
        limit=28,
        name="solve",
    )(place, pieces, left_old, right_old)


def body(activations, cotangent, weight, left_old, right_old):
    place = jnp.stack([lax.axis_index(a).astype(jnp.int32) for a in AXES])
    cot_turned = lax.ppermute(cotangent, AXES, SWAP)
    packed = pack(place, activations, weight)
    crossed = [lax.ppermute(packed[d], "y", shift(d)) for d in range(1, 4)]
    cot_turned, crossed[0], crossed[2] = lax.optimization_barrier(
        (cot_turned, crossed[0], crossed[2])
    )
    cot_all = copies_to(cot_turned, ZAX, 8)
    slab, near_w = unpack(place, [packed[0], *crossed])
    own = [slab] + [lax.ppermute(slab, "x", shift(d)) for d in range(1, 4)]
    swapped = [lax.ppermute(part, "c", FLIP) for part in own]
    copies, acts = grad_piece(place, cot_all, own, swapped)

    pieces = lax.all_to_all(copies, SOLVER, 0, 0, tiled=True)
    pieces, near_w = lax.optimization_barrier((pieces, near_w))
    first = first_partial(place, near_w, acts)
    first_parts = lax.all_to_all(first, ZAX, 0, 0, tiled=True)
    new_left, new_right, update, *sent = solve(
        place, in_hbm(pieces), in_hbm(left_old[0, 0]), in_hbm(right_old[0, 0])
    )
    update_parts = [in_hbm(sent[0])] + [lax.ppermute(sent[d], "y", shift(d)) for d in range(1, 4)]
    second = second_partial(place, update_parts, acts)
    second, first_parts = lax.optimization_barrier((second, first_parts))
    arrived = lax.all_to_all(second, ZAX, 0, 0, tiled=True)
    first_total, first_sum = first_add(place, first_parts)
    first_out = lax.ppermute(first_sum, AXES, SWAP)
    second_sum, spread = second_add(place, first_total, arrived)
    second_out = lax.ppermute(second_sum, AXES, SWAP)
    direction = update / spread[0, 0]
    return (first_out, new_left[None, None], new_right[None, None], direction, second_out)


def solution(mesh):
    fine = Mesh(mesh.devices.reshape(4, 2, 4, 2, 4), AXES)
    rows = ("zh", "zl", "y")
    in_specs = (
        P(BATCH, rows),
        P(rows, BATCH),
        P(rows, BATCH),
        P("zh", BATCH, None, None),
        P("zh", BATCH, None, None),
    )
    out_specs = (
        P(rows, BATCH),
        P("zh", BATCH, SOLVER, None),
        P("zh", BATCH, SOLVER, None),
        P(rows, BATCH),
        P(rows, BATCH),
    )
    return jax.shard_map(body, mesh=fine, in_specs=in_specs, out_specs=out_specs, check_vma=False)
```

```python
import jax
import jax.numpy as jnp
from jax import lax
from jax.experimental import pallas as pl
from jax.experimental.pallas import tpu as pltpu
from jax.sharding import Mesh
from jax.sharding import PartitionSpec as P

BLOCK = 1024
STAT_DECAY = 0.8
LEARN_RATE = 0.005
EPSILON = 1e-06

AXES = ("x", "c", "zh", "zl", "y")
BATCH = ("x", "c")
ZAX = ("zh", "zl")
SOLVER = ("zl", "y")
MIB = 1 << 20
SHAPE = jax.ShapeDtypeStruct
BF16 = jnp.bfloat16
F32 = jnp.float32


def device(x, c, zh, zl, y):
    return (((x * 2 + c) * 4 + zh) * 2 + zl) * 4 + y


EVERY = [
    (x, c, zh, zl, y)
    for x in range(4)
    for c in range(2)
    for zh in range(4)
    for zl in range(2)
    for y in range(4)
]
SWAP = [(device(*d), device(d[2], d[3], d[0], d[1], d[4])) for d in EVERY]
HOME = [
    (b * 32 + z * 4 + y, (z - b) % 8 * 32 + b * 4 + y)
    for b in range(8)
    for z in range(8)
    for y in range(4)
]
FLIP = [(0, 1), (1, 0)]


def shift(by):
    return [(i, (i + by) % 4) for i in range(4)]


def copies_to(shard, axis, count):
    copies = jnp.broadcast_to(shard, (count, *shard.shape))
    return lax.all_to_all(copies, axis, split_axis=0, concat_axis=0, tiled=True)


def dot(a, b):
    return jnp.dot(a, b, preferred_element_type=F32)


def dot_minor(a, b):
    return lax.dot_general(a, b, (((1,), (1,)), ((), ())), preferred_element_type=F32)


VMEM = pl.BlockSpec(memory_space=pltpu.VMEM)
HBM = pl.BlockSpec(memory_space=pltpu.HBM)


def call(body, in_specs, out_specs, out_shape, scratch=(), limit=24, name=None):
    return pl.pallas_call(
        body,
        out_shape=out_shape,
        in_specs=[pl.BlockSpec(memory_space=pltpu.SMEM), *in_specs],
        out_specs=out_specs,
        scratch_shapes=list(scratch),
        compiler_params=pltpu.CompilerParams(vmem_limit_bytes=limit * MIB),
        name=name,
    )


def in_hbm(value):
    return pltpu.with_memory_space_constraint(value, pltpu.HBM)


def wide(slab):
    return jnp.concatenate([slab[q] for q in range(4)], axis=1)


def pack_body(place, acts_hbm, weight_hbm, *refs):
    outs, (acts_ref, weight_ref, work, sems) = refs[:4], refs[4:]
    loads = [
        pltpu.make_async_copy(weight_hbm, weight_ref, sems.at[0]),
        pltpu.make_async_copy(acts_hbm, acts_ref, sems.at[1]),
    ]
    for load in loads:
        load.start()
    for load in loads:
        load.wait()
    for q in range(4):
        for half in range(2):
            at = q * 256 + half * 128
            work[q, half * 128 : (half + 1) * 128, :] = weight_ref[:, at : at + 128]
    acts = acts_ref[...]
    for d in range(4):
        outs[d][:256, :] = acts
        outs[d][256:, :] = work[(place[4] + d) & 3]


def pack(place, acts, weight):
    part = SHAPE((512, 128), BF16)
    return call(
        pack_body,
        [HBM] * 2,
        [VMEM] * 4,
        [part] * 4,
        scratch=[
            pltpu.VMEM((256, 128), BF16),
            pltpu.VMEM((128, 1024), BF16),
            pltpu.VMEM((4, 256, 128), BF16),
            pltpu.SemaphoreType.DMA((2,)),
        ],
        limit=8,
        name="pack",
    )(place, in_hbm(acts), in_hbm(weight))


def unpack_body(place, *refs):
    for d in range(4):
        at = (place[4] - d) & 3
        refs[4][at] = refs[d][:256, :]
        refs[5][at] = refs[d][256:, :]


def unpack(place, parts):
    shape = SHAPE((4, 256, 128), BF16)
    return call(unpack_body, [VMEM] * 4, [VMEM] * 2, [shape] * 2, limit=8, name="unpack")(
        place, *parts
    )


def weight_of(parts):
    rows = [jnp.concatenate([parts[q, :128, :], parts[q, 128:, :]], axis=1) for q in range(4)]
    return jnp.concatenate(rows, axis=0)


def grad_body(place, cot_ref, *refs):
    own, swapped = refs[:4], refs[4:8]
    copies_ref, acts_ref, piece_ref, sems = refs[8:]
    x, c = place[0], place[1]
    sends = []
    for d in range(4):
        at = ((x - d) & 3) * 2
        sends.append(pltpu.make_async_copy(own[d], acts_ref.at[at + c], sems.at[d]))
        sends.append(pltpu.make_async_copy(swapped[d], acts_ref.at[at + 1 - c], sems.at[4 + d]))
    for send in sends:
        send.start()
    total = jnp.zeros((256, 512), F32)
    for d in range(4):
        at = ((x - d) & 3) * 2
        total = total + dot(cot_ref[at + c], wide(own[d]))
        total = total + dot(cot_ref[at + 1 - c], wide(swapped[d]))
    piece_ref[...] = total.astype(BF16)
    for s in range(8):
        sends.append(pltpu.make_async_copy(piece_ref, copies_ref.at[s], sems.at[8 + s]))
        sends[-1].start()
    for send in sends:
        send.wait()


def grad_piece(place, cot_all, own, swapped):
    return call(
        grad_body,
        [VMEM] * 9,
        [HBM, HBM],
        [pltpu.HBM((8, 256, 512), BF16), pltpu.HBM((8, 4, 256, 128), BF16)],
        scratch=[pltpu.VMEM((256, 512), BF16), pltpu.SemaphoreType.DMA((16,))],
        limit=10,
        name="grad_piece",
    )(place, cot_all, *own, *swapped)


def first_body(place, weight_ref, *refs):
    own, swapped = refs[:4], refs[4:8]
    out_ref, work, sems = refs[8:]
    x, c = place[0], place[1]
    weight_t = weight_of(weight_ref).T
    sends = []
    for d in range(4):
        at = ((x - d) & 3) * 2
        for i, (slab, group) in enumerate(((own[d], at + c), (swapped[d], at + 1 - c))):
            n = d * 2 + i
            work[n] = dot_minor(weight_t, wide(slab)).astype(BF16)
            to = (group + 2 * x + c) & 7
            sends.append(pltpu.make_async_copy(work.at[n], out_ref.at[to], sems.at[n]))
            sends[-1].start()
    for send in sends:
        send.wait()


def first_partial(place, near_w, own, swapped):
    return call(
        first_body,
        [VMEM] * 9,
        HBM,
        pltpu.HBM((8, 256, 256), BF16),
        scratch=[pltpu.VMEM((8, 256, 256), BF16), pltpu.SemaphoreType.DMA((8,))],
        limit=12,
        name="first_partial",
    )(place, near_w, *own, *swapped)


def as_rows(value):
    high = value.astype(BF16).astype(F32)
    middle = (value - high).astype(BF16).astype(F32)
    low = value - high - middle
    row = lax.broadcasted_iota(jnp.int32, (16, 256), 0)
    rows = jnp.where(row == 0, high, jnp.where(row == 1, middle, jnp.where(row == 2, low, 0.0)))
    return rows.astype(BF16)


def from_rows(rows):
    return jnp.sum(rows.astype(F32), axis=0, keepdims=True)[:, :1]


def second_body(place, own_hbm, u1, u2, u3, acts_ref, out_ref, own_ref, update_ref, work, sems):
    load = pltpu.make_async_copy(own_hbm, own_ref, sems.at[8])
    load.start()
    squares = jnp.zeros((1, 1), F32)
    for d, piece in ((1, u1), (2, u2), (3, u3), (0, own_ref)):
        if d == 0:
            load.wait()
        update_ref[(place[4] - d) & 3] = piece[:128, :]
        squares = squares + from_rows(piece[128:, :])
    tail = as_rows(squares)
    update_t = update_ref[...].reshape(512, 256).T
    sends = []
    for group in range(8):
        work[group, :256, :] = dot_minor(update_t, wide(acts_ref.at[group])).astype(BF16)
        work[group, 256:, :] = tail
        to = (group + 2 * place[0] + place[1]) & 7
        sends.append(pltpu.make_async_copy(work.at[group], out_ref.at[to], sems.at[group]))
        sends[-1].start()
    for send in sends:
        send.wait()


def second_partial(place, update_parts, acts):
    return call(
        second_body,
        [HBM, *[VMEM] * 4],
        HBM,
        pltpu.HBM((8, 272, 256), BF16),
        scratch=[
            pltpu.VMEM((144, 256), BF16),
            pltpu.VMEM((4, 128, 256), BF16),
            pltpu.VMEM((8, 272, 256), BF16),
            pltpu.SemaphoreType.DMA((9,)),
        ],
        limit=12,
        name="second_partial",
    )(place, *update_parts, acts)


def first_add_body(place, parts_ref, total_ref):
    total = parts_ref[0].astype(F32)
    for i in range(1, 8):
        total = total + parts_ref[i].astype(F32)
    total_ref[...] = total


def first_add(place, parts):
    return call(
        first_add_body,
        [VMEM],
        VMEM,
        SHAPE((256, 256), F32),
        limit=8,
        name="first_add",
    )(place, parts)


def second_add_body(place, total_ref, parts_ref, out_ref, spread_ref):
    total = total_ref[...]
    out_ref[0] = total.astype(BF16)
    own = jnp.zeros((1, 1), F32)
    for h in range(4):
        squares = from_rows(parts_ref[2 * h, 256:, :]) + from_rows(parts_ref[2 * h + 1, 256:, :])
        spread = jnp.sqrt(squares / (BLOCK * BLOCK) + EPSILON)
        own = jnp.where(place[2] == h, spread, own)
        rate = LEARN_RATE / spread
        change = parts_ref[2 * h, :256, :].astype(F32) + parts_ref[2 * h + 1, :256, :].astype(F32)
        total = total - rate * change
    out_ref[1] = total.astype(BF16)
    spread_ref[...] = jnp.broadcast_to(own, (8, 128))


def second_add(place, total, parts):
    return call(
        second_add_body,
        [VMEM] * 2,
        [VMEM] * 2,
        [SHAPE((2, 256, 256), BF16), SHAPE((8, 128), F32)],
        limit=8,
        name="second_add",
    )(place, total, parts)


def statistics(lhs_ref, rhs_ref, old_ref, full_ref, off_ref):
    tile = 256
    sums = jnp.zeros((1, BLOCK), F32)
    diag = jnp.zeros((1, BLOCK), F32)
    for i in range(BLOCK // tile):
        rows = pl.ds(i * tile, tile)
        gram = dot(lhs_ref[rows, :], rhs_ref[...])
        new = STAT_DECAY * old_ref[rows, :] + (1.0 - STAT_DECAY) / BLOCK * gram
        full_ref[rows, :] = new
        sums = sums + jnp.sum(jnp.abs(new), axis=0, keepdims=True)
        row = lax.broadcasted_iota(jnp.int32, (tile, BLOCK), 0) + i * tile
        col = lax.broadcasted_iota(jnp.int32, (tile, BLOCK), 1)
        on_diag = row == col
        diag = diag + jnp.sum(jnp.where(on_diag, new, 0.0), axis=0, keepdims=True)
        off_ref[rows, :] = jnp.where(on_diag, 0.0, new).astype(BF16)
    scale = 2.5 / (jnp.max(sums, axis=1, keepdims=True) + EPSILON)
    return scale, diag


def times_factor(rows, off_ref, diag):
    return rows * diag + dot(rows.astype(BF16), off_ref[...])


def times_root(start, off_ref, diag, quarter):
    value = start
    for _ in range(4):
        value = 1.25 * value - quarter * times_factor(value, off_ref, diag)
    return 1.25 * start - quarter * times_factor(value, off_ref, diag)


def solver_body(
    place,
    pieces_ref,
    left_old_ref,
    right_old_ref,
    new_left_ref,
    new_right_ref,
    update_ref,
    sent0,
    sent1,
    sent2,
    sent3,
    left_buf,
    right_buf,
    grad_ref,
    grad_t_ref,
    full_ref,
    off_left_ref,
    off_right_ref,
    rows_buf,
    update_buf,
    sent_buf,
    sems,
):
    load_left = pltpu.make_async_copy(left_old_ref, left_buf, sems.at[0])
    load_right = pltpu.make_async_copy(right_old_ref, right_buf, sems.at[1])
    load_left.start()
    load_right.start()
    first = pl.multiple_of((place[3] * 4 + place[4]) * 128, 128)
    own = pl.ds(first, 128)
    for zl in range(2):
        for y in range(4):
            piece = pieces_ref[zl * 4 + y]
            grad_ref[pl.ds(y * 256, 256), pl.ds(zl * 512, 512)] = piece
            grad_t_ref[pl.ds(zl * 512, 512), pl.ds(y * 256, 256)] = piece.T
    load_left.wait()
    scale_left, diag_left = statistics(grad_t_ref, grad_ref, left_buf, full_ref, off_left_ref)
    left_rows = full_ref[own, :]
    rows_buf[...] = left_rows
    store_left = pltpu.make_async_copy(rows_buf, new_left_ref, sems.at[2])
    store_left.start()
    load_right.wait()
    scale_right, diag_right = statistics(
        grad_ref, grad_t_ref, right_buf, full_ref, off_right_ref
    )
    store_right = pltpu.make_async_copy(full_ref.at[own, :], new_right_ref, sems.at[3])
    store_right.start()
    quarter_left = scale_left * 0.25
    quarter_right = scale_right * 0.25
    row = lax.broadcasted_iota(jnp.int32, (128, BLOCK), 0) + first
    col = lax.broadcasted_iota(jnp.int32, (128, BLOCK), 1)
    start = jnp.where(row == col, 1.25, 0.0) - quarter_left * left_rows
    root = jnp.sqrt(jnp.sqrt(scale_left)) * times_root(start, off_left_ref, diag_left, quarter_left)
    high = root.astype(BF16)
    low = (root - high.astype(F32)).astype(BF16)
    both = dot(jnp.concatenate([high, low], axis=0), grad_t_ref[...])
    mixed = both[:128] + both[128:]
    turned = 1.25 * mixed - quarter_right * times_factor(mixed, off_right_ref, diag_right)
    update = jnp.sqrt(jnp.sqrt(scale_right)) * times_root(
        turned, off_right_ref, diag_right, quarter_right
    )
    squares = jnp.sum(jnp.sum(update * update, axis=0, keepdims=True), axis=1, keepdims=True)
    tail = as_rows(squares)
    for y in range(4):
        sent_buf[y, :128, :] = update[:, y * 256 : (y + 1) * 256].astype(BF16)
        sent_buf[y, 128:, :] = tail
    stores = [
        pltpu.make_async_copy(sent_buf.at[(place[4] + d) & 3], sent, sems.at[4 + d])
        for d, sent in enumerate((sent0, sent1, sent2, sent3))
    ]
    for store in stores:
        store.start()
    update_buf[...] = update
    stores.append(pltpu.make_async_copy(update_buf, update_ref, sems.at[8]))
    stores[-1].start()
    for store in [store_left, store_right, *stores]:
        store.wait()


def solve(place, pieces, left_old, right_old):
    square = (BLOCK, BLOCK)
    rows = pltpu.HBM((128, BLOCK), F32)
    return call(
        solver_body,
        [VMEM, HBM, HBM],
        [HBM] * 7,
        [rows, rows, rows, *[pltpu.HBM((144, 256), BF16)] * 4],
        scratch=[
            *[pltpu.VMEM(square, kind) for kind in (F32, F32, BF16, BF16, F32, BF16, BF16)],
            pltpu.VMEM((128, BLOCK), F32),
            pltpu.VMEM((128, BLOCK), F32),
            pltpu.VMEM((4, 144, 256), BF16),
            pltpu.SemaphoreType.DMA((9,)),
        ],
        limit=27,
        name="solve",
    )(place, pieces, left_old, right_old)


def body(activations, cotangent, weight, left_old, right_old):
    place = jnp.stack([lax.axis_index(a).astype(jnp.int32) for a in AXES])
    cot_turned = lax.ppermute(cotangent, AXES, SWAP)
    packed = pack(place, activations, weight)
    crossed = [lax.ppermute(packed[d], "y", shift(d)) for d in range(1, 4)]
    cot_turned, *crossed = lax.optimization_barrier((cot_turned, *crossed))
    cot_all = copies_to(cot_turned, ZAX, 8)
    slab, near_w = unpack(place, [packed[0], *crossed])
    own = [slab] + [lax.ppermute(slab, "x", shift(d)) for d in range(1, 4)]
    swapped = [lax.ppermute(part, "c", FLIP) for part in own]
    first = first_partial(place, near_w, own, swapped)
    cot_all, first = lax.optimization_barrier((cot_all, first))
    copies, acts = grad_piece(place, cot_all, own, swapped)

    pieces = lax.all_to_all(copies, SOLVER, 0, 0, tiled=True)
    pieces, first = lax.optimization_barrier((pieces, first))
    first_parts = lax.all_to_all(first, ZAX, 0, 0, tiled=True)
    new_left, new_right, update, *sent = solve(
        place, pieces, in_hbm(left_old[0, 0]), in_hbm(right_old[0, 0])
    )
    update_parts = [in_hbm(sent[0])] + [lax.ppermute(sent[d], "y", shift(d)) for d in range(1, 4)]
    second = second_partial(place, update_parts, acts)
    second, first_parts = lax.optimization_barrier((second, first_parts))
    arrived = lax.all_to_all(second, ZAX, 0, 0, tiled=True)
    outs, spread = second_add(place, first_add(place, first_parts), arrived)
    outs = lax.ppermute(outs, AXES, HOME)
    first_out, second_out = outs[0], outs[1]
    direction = update / spread[0, 0]
    return (first_out, new_left[None, None], new_right[None, None], direction, second_out)


def solution(mesh):
    fine = Mesh(mesh.devices.reshape(4, 2, 4, 2, 4), AXES)
    rows = ("zh", "zl", "y")
    in_specs = (
        P(BATCH, rows),
        P(rows, BATCH),
        P(rows, BATCH),
        P("zh", BATCH, None, None),
        P("zh", BATCH, None, None),
    )
    out_specs = (
        P(rows, BATCH),
        P("zh", BATCH, SOLVER, None),
        P("zh", BATCH, SOLVER, None),
        P(rows, BATCH),
        P(rows, BATCH),
    )
    return jax.shard_map(body, mesh=fine, in_specs=in_specs, out_specs=out_specs, check_vma=False)
```

```python
import jax
import jax.numpy as jnp
from jax import lax
from jax.experimental import pallas as pl
from jax.experimental.pallas import tpu as pltpu
from jax.sharding import Mesh
from jax.sharding import PartitionSpec as P

BLOCK = 1024
STAT_DECAY = 0.8
LEARN_RATE = 0.005
EPSILON = 1e-06

AXES = ("x", "c", "zh", "zl", "y")
BATCH = ("x", "c")
ZAX = ("zh", "zl")
SOLVER = ("zl", "y")
MIB = 1 << 20
SHAPE = jax.ShapeDtypeStruct
BF16 = jnp.bfloat16
F32 = jnp.float32


def device(x, c, zh, zl, y):
    return (((x * 2 + c) * 4 + zh) * 2 + zl) * 4 + y


EVERY = [
    (x, c, zh, zl, y)
    for x in range(4)
    for c in range(2)
    for zh in range(4)
    for zl in range(2)
    for y in range(4)
]
SWAP = [(device(*d), device(d[2], d[3], d[0], d[1], d[4])) for d in EVERY]
FLIP = [(0, 1), (1, 0)]


def shift(by):
    return [(i, (i + by) % 4) for i in range(4)]


def copies_to(shard, axis, count):
    copies = jnp.broadcast_to(shard, (count, *shard.shape))
    return lax.all_to_all(copies, axis, split_axis=0, concat_axis=0, tiled=True)


def dot(a, b):
    return jnp.dot(a, b, preferred_element_type=F32)


def dot_minor(a, b):
    return lax.dot_general(a, b, (((1,), (1,)), ((), ())), preferred_element_type=F32)


VMEM = pl.BlockSpec(memory_space=pltpu.VMEM)
HBM = pl.BlockSpec(memory_space=pltpu.HBM)


def call(body, in_specs, out_specs, out_shape, scratch=(), limit=24, name=None):
    return pl.pallas_call(
        body,
        out_shape=out_shape,
        in_specs=[pl.BlockSpec(memory_space=pltpu.SMEM), *in_specs],
        out_specs=out_specs,
        scratch_shapes=list(scratch),
        compiler_params=pltpu.CompilerParams(vmem_limit_bytes=limit * MIB),
        name=name,
    )


def in_hbm(value):
    return pltpu.with_memory_space_constraint(value, pltpu.HBM)


def wide(slab):
    return jnp.concatenate([slab[q] for q in range(4)], axis=1)


def pack_body(place, acts_hbm, weight_hbm, *refs):
    outs, (acts_ref, weight_ref, work, sems) = refs[:4], refs[4:]
    loads = [
        pltpu.make_async_copy(weight_hbm, weight_ref, sems.at[0]),
        pltpu.make_async_copy(acts_hbm, acts_ref, sems.at[1]),
    ]
    for load in loads:
        load.start()
    for load in loads:
        load.wait()
    for q in range(4):
        for half in range(2):
            at = q * 256 + half * 128
            work[q, half * 128 : (half + 1) * 128, :] = weight_ref[:, at : at + 128]
    acts = acts_ref[...]
    for d in range(4):
        outs[d][:256, :] = acts
        outs[d][256:, :] = work[(place[4] + d) & 3]


def pack(place, acts, weight):
    part = SHAPE((512, 128), BF16)
    return call(
        pack_body,
        [HBM] * 2,
        [VMEM] * 4,
        [part] * 4,
        scratch=[
            pltpu.VMEM((256, 128), BF16),
            pltpu.VMEM((128, 1024), BF16),
            pltpu.VMEM((4, 256, 128), BF16),
            pltpu.SemaphoreType.DMA((2,)),
        ],
        limit=8,
        name="pack",
    )(place, in_hbm(acts), in_hbm(weight))


def unpack_body(place, *refs):
    for d in range(4):
        at = (place[4] - d) & 3
        refs[4][at] = refs[d][:256, :]
        refs[5][at] = refs[d][256:, :]


def unpack(place, parts):
    shape = SHAPE((4, 256, 128), BF16)
    return call(unpack_body, [VMEM] * 4, [VMEM] * 2, [shape] * 2, limit=8, name="unpack")(
        place, *parts
    )


def weight_of(parts):
    rows = [jnp.concatenate([parts[q, :128, :], parts[q, 128:, :]], axis=1) for q in range(4)]
    return jnp.concatenate(rows, axis=0)


def grad_body(place, cot_ref, *refs):
    own, swapped = refs[:4], refs[4:8]
    piece_ref, kept_ref, acts_ref, sems = refs[8:]
    x, c = place[0], place[1]
    sends = []
    for d in range(4):
        at = ((x - d) & 3) * 2
        sends.append(pltpu.make_async_copy(own[d], acts_ref.at[at + c], sems.at[d]))
        sends.append(pltpu.make_async_copy(swapped[d], acts_ref.at[at + 1 - c], sems.at[4 + d]))
    for send in sends:
        send.start()
    total = jnp.zeros((256, 512), F32)
    for d in range(4):
        at = ((x - d) & 3) * 2
        total = total + dot(cot_ref[at + c], wide(own[d]))
        total = total + dot(cot_ref[at + 1 - c], wide(swapped[d]))
    piece_ref[...] = total.astype(BF16)
    sends.append(pltpu.make_async_copy(piece_ref, kept_ref, sems.at[8]))
    sends[-1].start()
    for send in sends:
        send.wait()


def grad_piece(place, cot_all, own, swapped):
    return call(
        grad_body,
        [VMEM] * 9,
        [VMEM, HBM, HBM],
        [
            SHAPE((256, 512), BF16),
            pltpu.HBM((256, 512), BF16),
            pltpu.HBM((8, 4, 256, 128), BF16),
        ],
        scratch=[pltpu.SemaphoreType.DMA((9,))],
        limit=10,
        name="grad_piece",
    )(place, cot_all, *own, *swapped)


def first_body(place, weight_ref, *refs):
    own, swapped = refs[:4], refs[4:8]
    out_ref, work, sems = refs[8:]
    x, c = place[0], place[1]
    weight_t = weight_of(weight_ref).T
    sends = []
    for d in range(4):
        at = ((x - d) & 3) * 2
        for i, (slab, group) in enumerate(((own[d], at + c), (swapped[d], at + 1 - c))):
            n = d * 2 + i
            work[n] = dot_minor(weight_t, wide(slab)).astype(BF16)
            sends.append(pltpu.make_async_copy(work.at[n], out_ref.at[group], sems.at[n]))
            sends[-1].start()
    for send in sends:
        send.wait()


def first_partial(place, near_w, own, swapped):
    return call(
        first_body,
        [VMEM] * 9,
        HBM,
        pltpu.HBM((8, 256, 256), BF16),
        scratch=[pltpu.VMEM((8, 256, 256), BF16), pltpu.SemaphoreType.DMA((8,))],
        limit=12,
        name="first_partial",
    )(place, near_w, *own, *swapped)


def as_rows(value):
    high = value.astype(BF16).astype(F32)
    middle = (value - high).astype(BF16).astype(F32)
    low = value - high - middle
    row = lax.broadcasted_iota(jnp.int32, (16, 256), 0)
    rows = jnp.where(row == 0, high, jnp.where(row == 1, middle, jnp.where(row == 2, low, 0.0)))
    return rows.astype(BF16)


def from_rows(rows):
    return jnp.sum(rows.astype(F32), axis=0, keepdims=True)[:, :1]


def order_body(place, *refs):
    for d in range(4):
        refs[4][(place[4] - d) & 3] = refs[d][...]


def in_order(place, parts):
    shape = SHAPE((4, 144, 256), BF16)
    return call(order_body, [VMEM] * 4, VMEM, shape, limit=8, name="in_order")(place, *parts)


def second_body(
    place,
    near_u,
    far_u,
    acts_hbm,
    far_hbm,
    swap_hbm,
    out_ref,
    spread_ref,
    near_ref,
    far_ref,
    swap_ref,
    work,
    sems,
):
    c, zl = place[1], place[3]
    loads = [
        pltpu.make_async_copy(acts_hbm.at[2 * i + zl], near_ref.at[i], sems.at[i])
        for i in range(4)
    ]
    loads.append(pltpu.make_async_copy(far_hbm, far_ref, sems.at[4]))
    loads.append(pltpu.make_async_copy(swap_hbm, swap_ref, sems.at[5]))
    for load in loads:
        load.start()
    squares = jnp.zeros((1, 1), F32)
    for q in range(4):
        squares = squares + from_rows(near_u[q, 128:, :]) + from_rows(far_u[q, 128:, :])
    spread = jnp.sqrt(squares / (BLOCK * BLOCK) + EPSILON)
    spread_ref[...] = jnp.broadcast_to(spread, (8, 128))
    rate = LEARN_RATE / spread
    near_t = jnp.concatenate([near_u[q, :128, :] for q in range(4)], axis=0).T
    far_t = jnp.concatenate([far_u[q, :128, :] for q in range(4)], axis=0).T
    for load in loads:
        load.wait()
    sends = []
    for i in range(2):
        for j in range(2):
            at = (c * 2 if i == 0 else 2 - c * 2) + j
            total = dot_minor(near_t, wide(near_ref.at[at]))
            total = total + dot_minor(far_t, wide((far_ref, swap_ref)[i].at[j]))
            n = i * 2 + j
            work[n] = (rate * total).astype(BF16)
            sends.append(pltpu.make_async_copy(work.at[n], out_ref.at[at], sems.at[6 + n]))
            sends[-1].start()
    for send in sends:
        send.wait()


def second_partial(place, near_u, far_u, acts, far, far_swapped):
    return call(
        second_body,
        [VMEM, VMEM, HBM, HBM, HBM],
        [HBM, VMEM],
        [pltpu.HBM((4, 256, 256), BF16), SHAPE((8, 128), F32)],
        scratch=[
            pltpu.VMEM((4, 4, 256, 128), BF16),
            pltpu.VMEM((2, 4, 256, 128), BF16),
            pltpu.VMEM((2, 4, 256, 128), BF16),
            pltpu.VMEM((4, 256, 256), BF16),
            pltpu.SemaphoreType.DMA((10,)),
        ],
        limit=14,
        name="second_partial",
    )(place, near_u, far_u, in_hbm(acts), in_hbm(far), in_hbm(far_swapped))


def first_add_body(place, parts_ref, total_ref, out_ref):
    total = parts_ref[0].astype(F32)
    for i in range(1, 8):
        total = total + parts_ref[i].astype(F32)
    total_ref[...] = total
    out_ref[...] = total.astype(BF16)


def first_add(place, parts):
    shape = (256, 256)
    return call(
        first_add_body,
        [VMEM],
        [VMEM] * 2,
        [SHAPE(shape, F32), SHAPE(shape, BF16)],
        limit=8,
        name="first_add",
    )(place, parts)


def second_add_body(place, total_ref, parts_ref, out_ref):
    change = parts_ref[0].astype(F32)
    for i in range(1, 4):
        change = change + parts_ref[i].astype(F32)
    out_ref[...] = (total_ref[...] - change).astype(BF16)


def second_add(place, total, parts):
    return call(
        second_add_body,
        [VMEM] * 2,
        VMEM,
        SHAPE((256, 256), BF16),
        limit=8,
        name="second_add",
    )(place, total, parts)


def statistics(lhs_ref, rhs_ref, old_ref, full_ref, off_ref):
    tile = 256
    sums = jnp.zeros((1, BLOCK), F32)
    diag = jnp.zeros((1, BLOCK), F32)
    for i in range(BLOCK // tile):
        rows = pl.ds(i * tile, tile)
        gram = dot(lhs_ref[rows, :], rhs_ref[...])
        new = STAT_DECAY * old_ref[rows, :] + (1.0 - STAT_DECAY) / BLOCK * gram
        full_ref[rows, :] = new
        sums = sums + jnp.sum(jnp.abs(new), axis=0, keepdims=True)
        row = lax.broadcasted_iota(jnp.int32, (tile, BLOCK), 0) + i * tile
        col = lax.broadcasted_iota(jnp.int32, (tile, BLOCK), 1)
        on_diag = row == col
        diag = diag + jnp.sum(jnp.where(on_diag, new, 0.0), axis=0, keepdims=True)
        off_ref[rows, :] = jnp.where(on_diag, 0.0, new).astype(BF16)
    scale = 2.5 / (jnp.max(sums, axis=1, keepdims=True) + EPSILON)
    return scale, diag


def times_factor(rows, off_ref, diag):
    return rows * diag + dot(rows.astype(BF16), off_ref[...])


def times_root(start, off_ref, diag, quarter):
    value = start
    for _ in range(4):
        value = 1.25 * value - quarter * times_factor(value, off_ref, diag)
    return 1.25 * start - quarter * times_factor(value, off_ref, diag)


def solver_body(
    place,
    near0,
    near1,
    near2,
    near3,
    far0,
    far1,
    far2,
    far3,
    left_old_ref,
    right_old_ref,
    new_left_ref,
    new_right_ref,
    update_ref,
    sent0,
    sent1,
    sent2,
    sent3,
    pieces_ref,
    left_buf,
    right_buf,
    grad_ref,
    grad_t_ref,
    full_ref,
    off_left_ref,
    off_right_ref,
    rows_buf,
    update_buf,
    sent_buf,
    sems,
):
    load_left = pltpu.make_async_copy(left_old_ref, left_buf, sems.at[0])
    load_right = pltpu.make_async_copy(right_old_ref, right_buf, sems.at[1])
    load_own = pltpu.make_async_copy(
        near0, pieces_ref.at[place[3] * 4 + place[4]], sems.at[9]
    )
    load_own.start()
    load_left.start()
    load_right.start()
    first = pl.multiple_of((place[3] * 4 + place[4]) * 128, 128)
    own = pl.ds(first, 128)
    for d, (near, far) in enumerate(((near0, far0), (near1, far1), (near2, far2), (near3, far3))):
        at = (place[4] - d) & 3
        if d > 0:
            pieces_ref[place[3] * 4 + at] = near[...]
        pieces_ref[4 - place[3] * 4 + at] = far[...]
    load_own.wait()
    for zl in range(2):
        for y in range(4):
            piece = pieces_ref[zl * 4 + y]
            grad_ref[pl.ds(y * 256, 256), pl.ds(zl * 512, 512)] = piece
            grad_t_ref[pl.ds(zl * 512, 512), pl.ds(y * 256, 256)] = piece.T
    load_left.wait()
    scale_left, diag_left = statistics(grad_t_ref, grad_ref, left_buf, full_ref, off_left_ref)
    left_rows = full_ref[own, :]
    rows_buf[...] = left_rows
    store_left = pltpu.make_async_copy(rows_buf, new_left_ref, sems.at[2])
    store_left.start()
    load_right.wait()
    scale_right, diag_right = statistics(
        grad_ref, grad_t_ref, right_buf, full_ref, off_right_ref
    )
    store_right = pltpu.make_async_copy(full_ref.at[own, :], new_right_ref, sems.at[3])
    store_right.start()
    quarter_left = scale_left * 0.25
    quarter_right = scale_right * 0.25
    row = lax.broadcasted_iota(jnp.int32, (128, BLOCK), 0) + first
    col = lax.broadcasted_iota(jnp.int32, (128, BLOCK), 1)
    start = jnp.where(row == col, 1.25, 0.0) - quarter_left * left_rows
    root = jnp.sqrt(jnp.sqrt(scale_left)) * times_root(start, off_left_ref, diag_left, quarter_left)
    high = root.astype(BF16)
    low = (root - high.astype(F32)).astype(BF16)
    both = dot(jnp.concatenate([high, low], axis=0), grad_t_ref[...])
    mixed = both[:128] + both[128:]
    turned = 1.25 * mixed - quarter_right * times_factor(mixed, off_right_ref, diag_right)
    update = jnp.sqrt(jnp.sqrt(scale_right)) * times_root(
        turned, off_right_ref, diag_right, quarter_right
    )
    squares = jnp.sum(jnp.sum(update * update, axis=0, keepdims=True), axis=1, keepdims=True)
    tail = as_rows(squares)
    for y in range(4):
        sent_buf[y, :128, :] = update[:, y * 256 : (y + 1) * 256].astype(BF16)
        sent_buf[y, 128:, :] = tail
    stores = [
        pltpu.make_async_copy(sent_buf.at[(place[4] + d) & 3], sent, sems.at[4 + d])
        for d, sent in enumerate((sent0, sent1, sent2, sent3))
    ]
    for store in stores:
        store.start()
    update_buf[...] = update
    stores.append(pltpu.make_async_copy(update_buf, update_ref, sems.at[8]))
    stores[-1].start()
    for store in [store_left, store_right, *stores]:
        store.wait()


def solve(place, pieces, left_old, right_old):
    square = (BLOCK, BLOCK)
    rows = pltpu.HBM((128, BLOCK), F32)
    return call(
        solver_body,
        [HBM, *[VMEM] * 7, HBM, HBM],
        [HBM] * 7,
        [rows, rows, rows, *[pltpu.HBM((144, 256), BF16)] * 4],
        scratch=[
            pltpu.VMEM((8, 256, 512), BF16),
            *[pltpu.VMEM(square, kind) for kind in (F32, F32, BF16, BF16, F32, BF16, BF16)],
            pltpu.VMEM((128, BLOCK), F32),
            pltpu.VMEM((128, BLOCK), F32),
            pltpu.VMEM((4, 144, 256), BF16),
            pltpu.SemaphoreType.DMA((10,)),
        ],
        limit=28,
        name="solve",
    )(place, *pieces, left_old, right_old)


def body(activations, cotangent, weight, left_old, right_old):
    place = jnp.stack([lax.axis_index(a).astype(jnp.int32) for a in AXES])
    cot_turned = lax.ppermute(cotangent, AXES, SWAP)
    packed = pack(place, activations, weight)
    crossed = [lax.ppermute(packed[d], "y", shift(d)) for d in range(1, 4)]
    cot_turned, *crossed = lax.optimization_barrier((cot_turned, *crossed))
    cot_all = copies_to(cot_turned, ZAX, 8)
    slab, near_w = unpack(place, [packed[0], *crossed])
    own = [slab] + [lax.ppermute(slab, "x", shift(d)) for d in range(1, 4)]
    swapped = [lax.ppermute(part, "c", FLIP) for part in own]
    first = first_partial(place, near_w, own, swapped)
    cot_all, first = lax.optimization_barrier((cot_all, first))
    piece, kept, acts = grad_piece(place, cot_all, own, swapped)

    beside = lax.ppermute(piece, "zl", FLIP)
    pieces = [in_hbm(kept)] + [lax.ppermute(piece, "y", shift(d)) for d in range(1, 4)]
    pieces += [beside, lax.ppermute(beside, "y", shift(1)), lax.ppermute(pieces[2], "zl", FLIP)]
    pieces += [lax.ppermute(beside, "y", shift(3))]
    first, *pieces[1:] = lax.optimization_barrier((first, *pieces[1:]))
    first_parts = lax.all_to_all(first, ZAX, 0, 0, tiled=True)
    halves = acts.reshape(2, 2, 2, 4, 256, 128)
    away = lax.dynamic_index_in_dim(halves, place[1], 0, keepdims=False)
    away = lax.dynamic_index_in_dim(away, 1 - place[3], 1, keepdims=False)
    away, *pieces = lax.optimization_barrier((away, *pieces))
    far = lax.ppermute(away, "zl", FLIP)
    new_left, new_right, update, *sent = solve(
        place, pieces, in_hbm(left_old[0, 0]), in_hbm(right_old[0, 0])
    )
    far, *sent = lax.optimization_barrier((far, *sent))
    near_u = in_order(
        place, [sent[0]] + [lax.ppermute(sent[d], "y", shift(d)) for d in range(1, 4)]
    )
    far_u = lax.ppermute(near_u, "zl", FLIP)
    far_swapped = lax.ppermute(far, "c", FLIP)
    first_total, first_sum = first_add(place, first_parts)
    acts, first_sum = lax.optimization_barrier((acts, first_sum))
    first_out = lax.ppermute(first_sum, AXES, SWAP)

    second, spread = second_partial(place, near_u, far_u, acts, far, far_swapped)
    arrived = lax.all_to_all(second, "zh", 0, 0, tiled=True)
    second_out = lax.ppermute(second_add(place, first_total, arrived), AXES, SWAP)
    direction = update / spread[0, 0]
    return (first_out, new_left[None, None], new_right[None, None], direction, second_out)


def solution(mesh):
    fine = Mesh(mesh.devices.reshape(4, 2, 4, 2, 4), AXES)
    rows = ("zh", "zl", "y")
    in_specs = (
        P(BATCH, rows),
        P(rows, BATCH),
        P(rows, BATCH),
        P("zh", BATCH, None, None),
        P("zh", BATCH, None, None),
    )
    out_specs = (
        P(rows, BATCH),
        P("zh", BATCH, SOLVER, None),
        P("zh", BATCH, SOLVER, None),
        P(rows, BATCH),
        P(rows, BATCH),
    )
    return jax.shard_map(body, mesh=fine, in_specs=in_specs, out_specs=out_specs, check_vma=False)
```

```python
import jax
import jax.numpy as jnp
from jax import lax
from jax.experimental import pallas as pl
from jax.experimental.pallas import tpu as pltpu
from jax.sharding import Mesh
from jax.sharding import PartitionSpec as P

BLOCK = 1024
STAT_DECAY = 0.8
LEARN_RATE = 0.005
EPSILON = 1e-06

AXES = ("x", "c", "zh", "zl", "y")
BATCH = ("x", "c")
ZAX = ("zh", "zl")
SOLVER = ("zl", "y")
MIB = 1 << 20
SHAPE = jax.ShapeDtypeStruct
BF16 = jnp.bfloat16
F32 = jnp.float32


def device(x, c, zh, zl, y):
    return (((x * 2 + c) * 4 + zh) * 2 + zl) * 4 + y


EVERY = [
    (x, c, zh, zl, y)
    for x in range(4)
    for c in range(2)
    for zh in range(4)
    for zl in range(2)
    for y in range(4)
]
SWAP = [(device(*d), device(d[2], d[3], d[0], d[1], d[4])) for d in EVERY]
HOME = [
    (b * 32 + z * 4 + y, (z - b) % 8 * 32 + b * 4 + y)
    for b in range(8)
    for z in range(8)
    for y in range(4)
]
FLIP = [(0, 1), (1, 0)]


def shift(by):
    return [(i, (i + by) % 4) for i in range(4)]


def copies_to(shard, axis, count):
    copies = jnp.broadcast_to(shard, (count, *shard.shape))
    return lax.all_to_all(copies, axis, split_axis=0, concat_axis=0, tiled=True)


def dot(a, b):
    return jnp.dot(a, b, preferred_element_type=F32)


def dot_minor(a, b):
    return lax.dot_general(a, b, (((1,), (1,)), ((), ())), preferred_element_type=F32)


VMEM = pl.BlockSpec(memory_space=pltpu.VMEM)
HBM = pl.BlockSpec(memory_space=pltpu.HBM)


def call(body, in_specs, out_specs, out_shape, scratch=(), limit=24, name=None):
    return pl.pallas_call(
        body,
        out_shape=out_shape,
        in_specs=[pl.BlockSpec(memory_space=pltpu.SMEM), *in_specs],
        out_specs=out_specs,
        scratch_shapes=list(scratch),
        compiler_params=pltpu.CompilerParams(vmem_limit_bytes=limit * MIB),
        name=name,
    )


def in_hbm(value):
    return pltpu.with_memory_space_constraint(value, pltpu.HBM)


def wide(slab):
    return jnp.concatenate([slab[q] for q in range(4)], axis=1)


def pack_body(place, acts_hbm, weight_hbm, *refs):
    outs, (acts_ref, weight_ref, work, sems) = refs[:4], refs[4:]
    loads = [
        pltpu.make_async_copy(weight_hbm, weight_ref, sems.at[0]),
        pltpu.make_async_copy(acts_hbm, acts_ref, sems.at[1]),
    ]
    for load in loads:
        load.start()
    for load in loads:
        load.wait()
    for q in range(4):
        for half in range(2):
            at = q * 256 + half * 128
            work[q, half * 128 : (half + 1) * 128, :] = weight_ref[:, at : at + 128]
    acts = acts_ref[...]
    for d in range(4):
        outs[d][:256, :] = acts
        outs[d][256:, :] = work[(place[4] + d) & 3]


def pack(place, acts, weight):
    part = SHAPE((512, 128), BF16)
    return call(
        pack_body,
        [HBM] * 2,
        [VMEM] * 4,
        [part] * 4,
        scratch=[
            pltpu.VMEM((256, 128), BF16),
            pltpu.VMEM((128, 1024), BF16),
            pltpu.VMEM((4, 256, 128), BF16),
            pltpu.SemaphoreType.DMA((2,)),
        ],
        limit=8,
        name="pack",
    )(place, in_hbm(acts), in_hbm(weight))


def unpack_body(place, *refs):
    for d in range(4):
        at = (place[4] - d) & 3
        refs[4][at] = refs[d][:256, :]
        refs[5][at] = refs[d][256:, :]


def unpack(place, parts):
    shape = SHAPE((4, 256, 128), BF16)
    return call(unpack_body, [VMEM] * 4, [VMEM] * 2, [shape] * 2, limit=8, name="unpack")(
        place, *parts
    )


def weight_of(parts):
    rows = [jnp.concatenate([parts[q, :128, :], parts[q, 128:, :]], axis=1) for q in range(4)]
    return jnp.concatenate(rows, axis=0)


def grad_body(place, cot_ref, *refs):
    own, swapped = refs[:4], refs[4:8]
    piece_ref, kept_ref, acts_ref, sems = refs[8:]
    x, c = place[0], place[1]
    sends = []
    for d in range(4):
        at = ((x - d) & 3) * 2
        sends.append(pltpu.make_async_copy(own[d], acts_ref.at[at + c], sems.at[d]))
        sends.append(pltpu.make_async_copy(swapped[d], acts_ref.at[at + 1 - c], sems.at[4 + d]))
    for send in sends:
        send.start()
    total = jnp.zeros((256, 512), F32)
    for d in range(4):
        at = ((x - d) & 3) * 2
        total = total + dot(cot_ref[at + c], wide(own[d]))
        total = total + dot(cot_ref[at + 1 - c], wide(swapped[d]))
    piece_ref[...] = total.astype(BF16)
    sends.append(pltpu.make_async_copy(piece_ref, kept_ref, sems.at[8]))
    sends[-1].start()
    for send in sends:
        send.wait()


def grad_piece(place, cot_all, own, swapped):
    return call(
        grad_body,
        [VMEM] * 9,
        [VMEM, HBM, HBM],
        [
            SHAPE((256, 512), BF16),
            pltpu.HBM((256, 512), BF16),
            pltpu.HBM((8, 4, 256, 128), BF16),
        ],
        scratch=[pltpu.SemaphoreType.DMA((9,))],
        limit=10,
        name="grad_piece",
    )(place, cot_all, *own, *swapped)


def first_body(place, weight_ref, *refs):
    own, swapped = refs[:4], refs[4:8]
    out_ref, work, sems = refs[8:]
    x, c = place[0], place[1]
    weight_t = weight_of(weight_ref).T
    sends = []
    for d in range(4):
        at = ((x - d) & 3) * 2
        for i, (slab, group) in enumerate(((own[d], at + c), (swapped[d], at + 1 - c))):
            n = d * 2 + i
            work[n] = dot_minor(weight_t, wide(slab)).astype(BF16)
            to = (group + 2 * x + c) & 7
            sends.append(pltpu.make_async_copy(work.at[n], out_ref.at[to], sems.at[n]))
            sends[-1].start()
    for send in sends:
        send.wait()


def first_partial(place, near_w, own, swapped):
    return call(
        first_body,
        [VMEM] * 9,
        HBM,
        pltpu.HBM((8, 256, 256), BF16),
        scratch=[pltpu.VMEM((8, 256, 256), BF16), pltpu.SemaphoreType.DMA((8,))],
        limit=12,
        name="first_partial",
    )(place, near_w, *own, *swapped)


def as_rows(value):
    high = value.astype(BF16).astype(F32)
    middle = (value - high).astype(BF16).astype(F32)
    low = value - high - middle
    row = lax.broadcasted_iota(jnp.int32, (16, 256), 0)
    rows = jnp.where(row == 0, high, jnp.where(row == 1, middle, jnp.where(row == 2, low, 0.0)))
    return rows.astype(BF16)


def from_rows(rows):
    return jnp.sum(rows.astype(F32), axis=0, keepdims=True)[:, :1]


def second_body(place, own_hbm, u1, u2, u3, acts_ref, out_ref, own_ref, update_ref, work, sems):
    load = pltpu.make_async_copy(own_hbm, own_ref, sems.at[8])
    load.start()
    squares = jnp.zeros((1, 1), F32)
    for d, piece in ((1, u1), (2, u2), (3, u3), (0, own_ref)):
        if d == 0:
            load.wait()
        update_ref[(place[4] - d) & 3] = piece[:128, :]
        squares = squares + from_rows(piece[128:, :])
    tail = as_rows(squares)
    update_t = update_ref[...].reshape(512, 256).T
    sends = []
    for group in range(8):
        work[group, :256, :] = dot_minor(update_t, wide(acts_ref.at[group])).astype(BF16)
        work[group, 256:, :] = tail
        to = (group + 2 * place[0] + place[1]) & 7
        sends.append(pltpu.make_async_copy(work.at[group], out_ref.at[to], sems.at[group]))
        sends[-1].start()
    for send in sends:
        send.wait()


def second_partial(place, update_parts, acts):
    return call(
        second_body,
        [HBM, *[VMEM] * 4],
        HBM,
        pltpu.HBM((8, 272, 256), BF16),
        scratch=[
            pltpu.VMEM((144, 256), BF16),
            pltpu.VMEM((4, 128, 256), BF16),
            pltpu.VMEM((8, 272, 256), BF16),
            pltpu.SemaphoreType.DMA((9,)),
        ],
        limit=12,
        name="second_partial",
    )(place, *update_parts, acts)


def first_add_body(place, parts_ref, total_ref):
    total = parts_ref[0].astype(F32)
    for i in range(1, 8):
        total = total + parts_ref[i].astype(F32)
    total_ref[...] = total


def first_add(place, parts):
    return call(
        first_add_body,
        [VMEM],
        VMEM,
        SHAPE((256, 256), F32),
        limit=8,
        name="first_add",
    )(place, parts)


def second_add_body(place, total_ref, parts_ref, out_ref, spread_ref):
    total = total_ref[...]
    out_ref[0] = total.astype(BF16)
    own = jnp.zeros((1, 1), F32)
    for h in range(4):
        squares = from_rows(parts_ref[2 * h, 256:, :]) + from_rows(parts_ref[2 * h + 1, 256:, :])
        spread = jnp.sqrt(squares / (BLOCK * BLOCK) + EPSILON)
        own = jnp.where(place[2] == h, spread, own)
        rate = LEARN_RATE / spread
        change = parts_ref[2 * h, :256, :].astype(F32) + parts_ref[2 * h + 1, :256, :].astype(F32)
        total = total - rate * change
    out_ref[1] = total.astype(BF16)
    spread_ref[...] = jnp.broadcast_to(own, (8, 128))


def second_add(place, total, parts):
    return call(
        second_add_body,
        [VMEM] * 2,
        [VMEM] * 2,
        [SHAPE((2, 256, 256), BF16), SHAPE((8, 128), F32)],
        limit=8,
        name="second_add",
    )(place, total, parts)


def statistics(lhs_ref, rhs_ref, old_ref, full_ref, off_ref):
    tile = 256
    sums = jnp.zeros((1, BLOCK), F32)
    diag = jnp.zeros((1, BLOCK), F32)
    for i in range(BLOCK // tile):
        rows = pl.ds(i * tile, tile)
        gram = dot(lhs_ref[rows, :], rhs_ref[...])
        new = STAT_DECAY * old_ref[rows, :] + (1.0 - STAT_DECAY) / BLOCK * gram
        full_ref[rows, :] = new
        sums = sums + jnp.sum(jnp.abs(new), axis=0, keepdims=True)
        row = lax.broadcasted_iota(jnp.int32, (tile, BLOCK), 0) + i * tile
        col = lax.broadcasted_iota(jnp.int32, (tile, BLOCK), 1)
        on_diag = row == col
        diag = diag + jnp.sum(jnp.where(on_diag, new, 0.0), axis=0, keepdims=True)
        off_ref[rows, :] = jnp.where(on_diag, 0.0, new).astype(BF16)
    scale = 2.5 / (jnp.max(sums, axis=1, keepdims=True) + EPSILON)
    return scale, diag


def times_factor(rows, off_ref, diag):
    return rows * diag + dot(rows.astype(BF16), off_ref[...])


def times_root(start, off_ref, diag, quarter):
    value = start
    for _ in range(4):
        value = 1.25 * value - quarter * times_factor(value, off_ref, diag)
    return 1.25 * start - quarter * times_factor(value, off_ref, diag)


def solver_body(
    place,
    near0,
    near1,
    near2,
    near3,
    far0,
    far1,
    far2,
    far3,
    left_old_ref,
    right_old_ref,
    new_left_ref,
    new_right_ref,
    update_ref,
    sent0,
    sent1,
    sent2,
    sent3,
    pieces_ref,
    left_buf,
    right_buf,
    grad_ref,
    grad_t_ref,
    full_ref,
    off_left_ref,
    off_right_ref,
    rows_buf,
    update_buf,
    sent_buf,
    sems,
):
    load_left = pltpu.make_async_copy(left_old_ref, left_buf, sems.at[0])
    load_right = pltpu.make_async_copy(right_old_ref, right_buf, sems.at[1])
    load_own = pltpu.make_async_copy(
        near0, pieces_ref.at[place[3] * 4 + place[4]], sems.at[9]
    )
    load_own.start()
    load_left.start()
    load_right.start()
    first = pl.multiple_of((place[3] * 4 + place[4]) * 128, 128)
    own = pl.ds(first, 128)
    for d, (near, far) in enumerate(((near0, far0), (near1, far1), (near2, far2), (near3, far3))):
        at = (place[4] - d) & 3
        if d > 0:
            pieces_ref[place[3] * 4 + at] = near[...]
        pieces_ref[4 - place[3] * 4 + at] = far[...]
    load_own.wait()
    for zl in range(2):
        for y in range(4):
            piece = pieces_ref[zl * 4 + y]
            grad_ref[pl.ds(y * 256, 256), pl.ds(zl * 512, 512)] = piece
            grad_t_ref[pl.ds(zl * 512, 512), pl.ds(y * 256, 256)] = piece.T
    load_left.wait()
    scale_left, diag_left = statistics(grad_t_ref, grad_ref, left_buf, full_ref, off_left_ref)
    left_rows = full_ref[own, :]
    rows_buf[...] = left_rows
    store_left = pltpu.make_async_copy(rows_buf, new_left_ref, sems.at[2])
    store_left.start()
    load_right.wait()
    scale_right, diag_right = statistics(
        grad_ref, grad_t_ref, right_buf, full_ref, off_right_ref
    )
    store_right = pltpu.make_async_copy(full_ref.at[own, :], new_right_ref, sems.at[3])
    store_right.start()
    quarter_left = scale_left * 0.25
    quarter_right = scale_right * 0.25
    row = lax.broadcasted_iota(jnp.int32, (128, BLOCK), 0) + first
    col = lax.broadcasted_iota(jnp.int32, (128, BLOCK), 1)
    start = jnp.where(row == col, 1.25, 0.0) - quarter_left * left_rows
    root = jnp.sqrt(jnp.sqrt(scale_left)) * times_root(start, off_left_ref, diag_left, quarter_left)
    high = root.astype(BF16)
    low = (root - high.astype(F32)).astype(BF16)
    both = dot(jnp.concatenate([high, low], axis=0), grad_t_ref[...])
    mixed = both[:128] + both[128:]
    turned = 1.25 * mixed - quarter_right * times_factor(mixed, off_right_ref, diag_right)
    update = jnp.sqrt(jnp.sqrt(scale_right)) * times_root(
        turned, off_right_ref, diag_right, quarter_right
    )
    squares = jnp.sum(jnp.sum(update * update, axis=0, keepdims=True), axis=1, keepdims=True)
    tail = as_rows(squares)
    for y in range(4):
        sent_buf[y, :128, :] = update[:, y * 256 : (y + 1) * 256].astype(BF16)
        sent_buf[y, 128:, :] = tail
    stores = [
        pltpu.make_async_copy(sent_buf.at[(place[4] + d) & 3], sent, sems.at[4 + d])
        for d, sent in enumerate((sent0, sent1, sent2, sent3))
    ]
    for store in stores:
        store.start()
    update_buf[...] = update
    stores.append(pltpu.make_async_copy(update_buf, update_ref, sems.at[8]))
    stores[-1].start()
    for store in [store_left, store_right, *stores]:
        store.wait()


def solve(place, pieces, left_old, right_old):
    square = (BLOCK, BLOCK)
    rows = pltpu.HBM((128, BLOCK), F32)
    return call(
        solver_body,
        [HBM, *[VMEM] * 7, HBM, HBM],
        [HBM] * 7,
        [rows, rows, rows, *[pltpu.HBM((144, 256), BF16)] * 4],
        scratch=[
            pltpu.VMEM((8, 256, 512), BF16),
            *[pltpu.VMEM(square, kind) for kind in (F32, F32, BF16, BF16, F32, BF16, BF16)],
            pltpu.VMEM((128, BLOCK), F32),
            pltpu.VMEM((128, BLOCK), F32),
            pltpu.VMEM((4, 144, 256), BF16),
            pltpu.SemaphoreType.DMA((10,)),
        ],
        limit=28,
        name="solve",
    )(place, *pieces, left_old, right_old)


def body(activations, cotangent, weight, left_old, right_old):
    place = jnp.stack([lax.axis_index(a).astype(jnp.int32) for a in AXES])
    cot_turned = lax.ppermute(cotangent, AXES, SWAP)
    packed = pack(place, activations, weight)
    crossed = [lax.ppermute(packed[d], "y", shift(d)) for d in range(1, 4)]
    cot_turned, *crossed = lax.optimization_barrier((cot_turned, *crossed))
    cot_all = copies_to(cot_turned, ZAX, 8)
    slab, near_w = unpack(place, [packed[0], *crossed])
    own = [slab] + [lax.ppermute(slab, "x", shift(d)) for d in range(1, 4)]
    swapped = [lax.ppermute(part, "c", FLIP) for part in own]
    first = first_partial(place, near_w, own, swapped)
    cot_all, first = lax.optimization_barrier((cot_all, first))
    piece, kept, acts = grad_piece(place, cot_all, own, swapped)

    beside = lax.ppermute(piece, "zl", FLIP)
    pieces = [in_hbm(kept)] + [lax.ppermute(piece, "y", shift(d)) for d in range(1, 4)]
    pieces += [beside, lax.ppermute(beside, "y", shift(1)), lax.ppermute(pieces[2], "zl", FLIP)]
    pieces += [lax.ppermute(beside, "y", shift(3))]
    first, *pieces[1:] = lax.optimization_barrier((first, *pieces[1:]))
    first_parts = lax.all_to_all(first, ZAX, 0, 0, tiled=True)
    new_left, new_right, update, *sent = solve(
        place, pieces, in_hbm(left_old[0, 0]), in_hbm(right_old[0, 0])
    )
    update_parts = [in_hbm(sent[0])] + [lax.ppermute(sent[d], "y", shift(d)) for d in range(1, 4)]
    second = second_partial(place, update_parts, acts)
    second, first_parts = lax.optimization_barrier((second, first_parts))
    arrived = lax.all_to_all(second, ZAX, 0, 0, tiled=True)
    outs, spread = second_add(place, first_add(place, first_parts), arrived)
    outs = lax.ppermute(outs, AXES, HOME)
    first_out, second_out = outs[0], outs[1]
    direction = update / spread[0, 0]
    return (first_out, new_left[None, None], new_right[None, None], direction, second_out)


def solution(mesh):
    fine = Mesh(mesh.devices.reshape(4, 2, 4, 2, 4), AXES)
    rows = ("zh", "zl", "y")
    in_specs = (
        P(BATCH, rows),
        P(rows, BATCH),
        P(rows, BATCH),
        P("zh", BATCH, None, None),
        P("zh", BATCH, None, None),
    )
    out_specs = (
        P(rows, BATCH),
        P("zh", BATCH, SOLVER, None),
        P("zh", BATCH, SOLVER, None),
        P(rows, BATCH),
        P(rows, BATCH),
    )
    return jax.shard_map(body, mesh=fine, in_specs=in_specs, out_specs=out_specs, check_vma=False)
```

```python
import jax
import jax.numpy as jnp
from jax import lax
from jax.experimental import pallas as pl
from jax.experimental.pallas import tpu as pltpu
from jax.sharding import Mesh
from jax.sharding import PartitionSpec as P

BLOCK = 1024
STAT_DECAY = 0.8
LEARN_RATE = 0.005
EPSILON = 1e-06

AXES = ("x", "c", "zh", "zl", "y")
BATCH = ("x", "c")
ZAX = ("zh", "zl")
SOLVER = ("zl", "y")
MIB = 1 << 20
SHAPE = jax.ShapeDtypeStruct
BF16 = jnp.bfloat16
F32 = jnp.float32


def device(x, c, zh, zl, y):
    return (((x * 2 + c) * 4 + zh) * 2 + zl) * 4 + y


EVERY = [
    (x, c, zh, zl, y)
    for x in range(4)
    for c in range(2)
    for zh in range(4)
    for zl in range(2)
    for y in range(4)
]
SWAP = [(device(*d), device(d[2], d[3], d[0], d[1], d[4])) for d in EVERY]
HOME = [
    (b * 32 + z * 4 + y, (z - b) % 8 * 32 + b * 4 + y)
    for b in range(8)
    for z in range(8)
    for y in range(4)
]
FLIP = [(0, 1), (1, 0)]


def shift(by):
    return [(i, (i + by) % 4) for i in range(4)]


def copies_to(shard, axis, count):
    copies = jnp.broadcast_to(shard, (count, *shard.shape))
    return lax.all_to_all(copies, axis, split_axis=0, concat_axis=0, tiled=True)


def dot(a, b):
    return jnp.dot(a, b, preferred_element_type=F32)


def dot_minor(a, b):
    return lax.dot_general(a, b, (((1,), (1,)), ((), ())), preferred_element_type=F32)


VMEM = pl.BlockSpec(memory_space=pltpu.VMEM)
HBM = pl.BlockSpec(memory_space=pltpu.HBM)


def call(body, in_specs, out_specs, out_shape, scratch=(), limit=24, name=None):
    return pl.pallas_call(
        body,
        out_shape=out_shape,
        in_specs=[pl.BlockSpec(memory_space=pltpu.SMEM), *in_specs],
        out_specs=out_specs,
        scratch_shapes=list(scratch),
        compiler_params=pltpu.CompilerParams(vmem_limit_bytes=limit * MIB),
        name=name,
    )


def in_hbm(value):
    return pltpu.with_memory_space_constraint(value, pltpu.HBM)


def wide(slab):
    return jnp.concatenate([slab[q] for q in range(4)], axis=1)


def pack_body(place, acts_hbm, weight_hbm, *refs):
    outs, (acts_ref, weight_ref, work, sems) = refs[:4], refs[4:]
    loads = [
        pltpu.make_async_copy(weight_hbm, weight_ref, sems.at[0]),
        pltpu.make_async_copy(acts_hbm, acts_ref, sems.at[1]),
    ]
    for load in loads:
        load.start()
    for load in loads:
        load.wait()
    for q in range(4):
        for half in range(2):
            at = q * 256 + half * 128
            work[q, half * 128 : (half + 1) * 128, :] = weight_ref[:, at : at + 128]
    acts = acts_ref[...]
    for d in range(4):
        outs[d][:256, :] = acts
        outs[d][256:, :] = work[(place[4] + d) & 3]


def pack(place, acts, weight):
    part = SHAPE((512, 128), BF16)
    return call(
        pack_body,
        [HBM] * 2,
        [VMEM] * 4,
        [part] * 4,
        scratch=[
            pltpu.VMEM((256, 128), BF16),
            pltpu.VMEM((128, 1024), BF16),
            pltpu.VMEM((4, 256, 128), BF16),
            pltpu.SemaphoreType.DMA((2,)),
        ],
        limit=8,
        name="pack",
    )(place, in_hbm(acts), in_hbm(weight))


def unpack_body(place, *refs):
    for d in range(4):
        at = (place[4] - d) & 3
        refs[4][at] = refs[d][:256, :]
        refs[5][at] = refs[d][256:, :]


def unpack(place, parts):
    shape = SHAPE((4, 256, 128), BF16)
    return call(unpack_body, [VMEM] * 4, [VMEM] * 2, [shape] * 2, limit=8, name="unpack")(
        place, *parts
    )


def weight_of(parts):
    rows = [jnp.concatenate([parts[q, :128, :], parts[q, 128:, :]], axis=1) for q in range(4)]
    return jnp.concatenate(rows, axis=0)


def grad_body(place, cot_ref, *refs):
    own, swapped = refs[:4], refs[4:8]
    piece_ref, kept_ref, acts_ref, sems = refs[8:]
    x, c = place[0], place[1]
    sends = []
    for d in range(4):
        at = ((x - d) & 3) * 2
        sends.append(pltpu.make_async_copy(own[d], acts_ref.at[at + c], sems.at[d]))
        sends.append(pltpu.make_async_copy(swapped[d], acts_ref.at[at + 1 - c], sems.at[4 + d]))
    for send in sends:
        send.start()
    total = jnp.zeros((256, 512), F32)
    for d in range(4):
        at = ((x - d) & 3) * 2
        total = total + dot(cot_ref[at + c], wide(own[d]))
        total = total + dot(cot_ref[at + 1 - c], wide(swapped[d]))
    piece_ref[...] = total.astype(BF16)
    sends.append(pltpu.make_async_copy(piece_ref, kept_ref, sems.at[8]))
    sends[-1].start()
    for send in sends:
        send.wait()


def grad_piece(place, cot_all, own, swapped):
    return call(
        grad_body,
        [VMEM] * 9,
        [VMEM, HBM, HBM],
        [
            SHAPE((256, 512), BF16),
            pltpu.HBM((256, 512), BF16),
            pltpu.HBM((8, 4, 256, 128), BF16),
        ],
        scratch=[pltpu.SemaphoreType.DMA((9,))],
        limit=10,
        name="grad_piece",
    )(place, cot_all, *own, *swapped)


def first_body(place, weight_ref, *refs):
    own, swapped = refs[:4], refs[4:8]
    out_ref, work, sems = refs[8:]
    x, c = place[0], place[1]
    weight_t = weight_of(weight_ref).T
    sends = []
    for d in range(4):
        at = ((x - d) & 3) * 2
        for i, (slab, group) in enumerate(((own[d], at + c), (swapped[d], at + 1 - c))):
            n = d * 2 + i
            work[n] = dot_minor(weight_t, wide(slab)).astype(BF16)
            to = (group + 2 * x + c) & 7
            sends.append(pltpu.make_async_copy(work.at[n], out_ref.at[to], sems.at[n]))
            sends[-1].start()
    for send in sends:
        send.wait()


def first_partial(place, near_w, own, swapped):
    return call(
        first_body,
        [VMEM] * 9,
        HBM,
        pltpu.HBM((8, 256, 256), BF16),
        scratch=[pltpu.VMEM((8, 256, 256), BF16), pltpu.SemaphoreType.DMA((8,))],
        limit=12,
        name="first_partial",
    )(place, near_w, *own, *swapped)


def as_rows(value):
    high = value.astype(BF16).astype(F32)
    middle = (value - high).astype(BF16).astype(F32)
    low = value - high - middle
    row = lax.broadcasted_iota(jnp.int32, (16, 256), 0)
    rows = jnp.where(row == 0, high, jnp.where(row == 1, middle, jnp.where(row == 2, low, 0.0)))
    return rows.astype(BF16)


def from_rows(rows):
    return jnp.sum(rows.astype(F32), axis=0, keepdims=True)[:, :1]


def second_body(place, own_hbm, u1, u2, u3, acts_ref, out_ref, own_ref, update_ref, work, sems):
    load = pltpu.make_async_copy(own_hbm, own_ref, sems.at[8])
    load.start()
    squares = jnp.zeros((1, 1), F32)
    for d, piece in ((1, u1), (2, u2), (3, u3), (0, own_ref)):
        if d == 0:
            load.wait()
        update_ref[(place[4] - d) & 3] = piece[:128, :]
        squares = squares + from_rows(piece[128:, :])
    tail = as_rows(squares)
    update_t = update_ref[...].reshape(512, 256).T
    sends = []
    for group in range(8):
        work[group, :256, :] = dot_minor(update_t, wide(acts_ref.at[group])).astype(BF16)
        work[group, 256:, :] = tail
        to = (group + 2 * place[0] + place[1]) & 7
        sends.append(pltpu.make_async_copy(work.at[group], out_ref.at[to], sems.at[group]))
        sends[-1].start()
    for send in sends:
        send.wait()


def second_partial(place, update_parts, acts):
    return call(
        second_body,
        [HBM, *[VMEM] * 4],
        HBM,
        pltpu.HBM((8, 272, 256), BF16),
        scratch=[
            pltpu.VMEM((144, 256), BF16),
            pltpu.VMEM((4, 128, 256), BF16),
            pltpu.VMEM((8, 272, 256), BF16),
            pltpu.SemaphoreType.DMA((9,)),
        ],
        limit=12,
        name="second_partial",
    )(place, *update_parts, acts)


def first_add_body(place, parts_ref, total_ref):
    total = parts_ref[0].astype(F32)
    for i in range(1, 8):
        total = total + parts_ref[i].astype(F32)
    total_ref[...] = total


def first_add(place, parts):
    return call(
        first_add_body,
        [VMEM],
        VMEM,
        SHAPE((256, 256), F32),
        limit=8,
        name="first_add",
    )(place, parts)


def second_add_body(place, total_ref, parts_ref, out_ref, spread_ref):
    total = total_ref[...]
    out_ref[0] = total.astype(BF16)
    own = jnp.zeros((1, 1), F32)
    for h in range(4):
        squares = from_rows(parts_ref[2 * h, 256:, :]) + from_rows(parts_ref[2 * h + 1, 256:, :])
        spread = jnp.sqrt(squares / (BLOCK * BLOCK) + EPSILON)
        own = jnp.where(place[2] == h, spread, own)
        rate = LEARN_RATE / spread
        change = parts_ref[2 * h, :256, :].astype(F32) + parts_ref[2 * h + 1, :256, :].astype(F32)
        total = total - rate * change
    out_ref[1] = total.astype(BF16)
    spread_ref[...] = jnp.broadcast_to(own, (8, 128))


def second_add(place, total, parts):
    return call(
        second_add_body,
        [VMEM] * 2,
        [VMEM] * 2,
        [SHAPE((2, 256, 256), BF16), SHAPE((8, 128), F32)],
        limit=8,
        name="second_add",
    )(place, total, parts)


def statistics(lhs_ref, rhs_ref, old_ref, full_ref, off_ref):
    tile = 256
    sums = jnp.zeros((1, BLOCK), F32)
    diag = jnp.zeros((1, BLOCK), F32)
    for i in range(BLOCK // tile):
        rows = pl.ds(i * tile, tile)
        gram = dot(lhs_ref[rows, :], rhs_ref[...])
        new = STAT_DECAY * old_ref[rows, :] + (1.0 - STAT_DECAY) / BLOCK * gram
        full_ref[rows, :] = new
        sums = sums + jnp.sum(jnp.abs(new), axis=0, keepdims=True)
        row = lax.broadcasted_iota(jnp.int32, (tile, BLOCK), 0) + i * tile
        col = lax.broadcasted_iota(jnp.int32, (tile, BLOCK), 1)
        on_diag = row == col
        diag = diag + jnp.sum(jnp.where(on_diag, new, 0.0), axis=0, keepdims=True)
        off_ref[rows, :] = jnp.where(on_diag, 0.0, new).astype(BF16)
    scale = 2.5 / (jnp.max(sums, axis=1, keepdims=True) + EPSILON)
    return scale, diag


def times_factor(rows, off_ref, diag):
    return rows * diag + dot(rows.astype(BF16), off_ref[...])


def times_root(start, off_ref, diag, quarter):
    value = start
    for _ in range(4):
        value = 1.25 * value - quarter * times_factor(value, off_ref, diag)
    return 1.25 * start - quarter * times_factor(value, off_ref, diag)


def solver_body(
    place,
    near0,
    near1,
    near2,
    near3,
    far0,
    far1,
    far2,
    far3,
    left_old_ref,
    right_old_ref,
    new_left_ref,
    new_right_ref,
    update_ref,
    sent0,
    sent1,
    sent2,
    sent3,
    pieces_ref,
    left_buf,
    right_buf,
    grad_ref,
    grad_t_ref,
    full_ref,
    off_left_ref,
    off_right_ref,
    rows_buf,
    update_buf,
    sent_buf,
    sems,
):
    load_left = pltpu.make_async_copy(left_old_ref, left_buf, sems.at[0])
    load_right = pltpu.make_async_copy(right_old_ref, right_buf, sems.at[1])
    load_own = pltpu.make_async_copy(
        near0, pieces_ref.at[place[3] * 4 + place[4]], sems.at[9]
    )
    load_own.start()
    load_left.start()
    load_right.start()
    first = pl.multiple_of((place[3] * 4 + place[4]) * 128, 128)
    own = pl.ds(first, 128)
    for d, (near, far) in enumerate(((near0, far0), (near1, far1), (near2, far2), (near3, far3))):
        at = (place[4] - d) & 3
        if d > 0:
            pieces_ref[place[3] * 4 + at] = near[...]
        pieces_ref[4 - place[3] * 4 + at] = far[...]
    load_own.wait()
    for zl in range(2):
        for y in range(4):
            piece = pieces_ref[zl * 4 + y]
            grad_ref[pl.ds(y * 256, 256), pl.ds(zl * 512, 512)] = piece
            grad_t_ref[pl.ds(zl * 512, 512), pl.ds(y * 256, 256)] = piece.T
    load_left.wait()
    scale_left, diag_left = statistics(grad_t_ref, grad_ref, left_buf, full_ref, off_left_ref)
    left_rows = full_ref[own, :]
    rows_buf[...] = left_rows
    store_left = pltpu.make_async_copy(rows_buf, new_left_ref, sems.at[2])
    store_left.start()
    load_right.wait()
    scale_right, diag_right = statistics(
        grad_ref, grad_t_ref, right_buf, full_ref, off_right_ref
    )
    store_right = pltpu.make_async_copy(full_ref.at[own, :], new_right_ref, sems.at[3])
    store_right.start()
    quarter_left = scale_left * 0.25
    quarter_right = scale_right * 0.25
    row = lax.broadcasted_iota(jnp.int32, (128, BLOCK), 0) + first
    col = lax.broadcasted_iota(jnp.int32, (128, BLOCK), 1)
    start = jnp.where(row == col, 1.25, 0.0) - quarter_left * left_rows
    root = jnp.sqrt(jnp.sqrt(scale_left)) * times_root(start, off_left_ref, diag_left, quarter_left)
    high = root.astype(BF16)
    low = (root - high.astype(F32)).astype(BF16)
    both = dot(jnp.concatenate([high, low], axis=0), grad_t_ref[...])
    mixed = both[:128] + both[128:]
    turned = 1.25 * mixed - quarter_right * times_factor(mixed, off_right_ref, diag_right)
    update = jnp.sqrt(jnp.sqrt(scale_right)) * times_root(
        turned, off_right_ref, diag_right, quarter_right
    )
    squares = jnp.sum(jnp.sum(update * update, axis=0, keepdims=True), axis=1, keepdims=True)
    tail = as_rows(squares)
    for y in range(4):
        sent_buf[y, :128, :] = update[:, y * 256 : (y + 1) * 256].astype(BF16)
        sent_buf[y, 128:, :] = tail
    stores = [
        pltpu.make_async_copy(sent_buf.at[(place[4] + d) & 3], sent, sems.at[4 + d])
        for d, sent in enumerate((sent0, sent1, sent2, sent3))
    ]
    for store in stores:
        store.start()
    update_buf[...] = update
    stores.append(pltpu.make_async_copy(update_buf, update_ref, sems.at[8]))
    stores[-1].start()
    for store in [store_left, store_right, *stores]:
        store.wait()


def solve(place, pieces, left_old, right_old):
    square = (BLOCK, BLOCK)
    rows = pltpu.HBM((128, BLOCK), F32)
    return call(
        solver_body,
        [HBM, *[VMEM] * 7, HBM, HBM],
        [HBM] * 7,
        [rows, rows, rows, *[pltpu.HBM((144, 256), BF16)] * 4],
        scratch=[
            pltpu.VMEM((8, 256, 512), BF16),
            *[pltpu.VMEM(square, kind) for kind in (F32, F32, BF16, BF16, F32, BF16, BF16)],
            pltpu.VMEM((128, BLOCK), F32),
            pltpu.VMEM((128, BLOCK), F32),
            pltpu.VMEM((4, 144, 256), BF16),
            pltpu.SemaphoreType.DMA((10,)),
        ],
        limit=28,
        name="solve",
    )(place, *pieces, left_old, right_old)


def body(activations, cotangent, weight, left_old, right_old):
    place = jnp.stack([lax.axis_index(a).astype(jnp.int32) for a in AXES])
    cot_turned = lax.ppermute(cotangent, AXES, SWAP)
    packed = pack(place, activations, weight)
    crossed = [lax.ppermute(packed[d], "y", shift(d)) for d in range(1, 4)]
    cot_turned, crossed[0], crossed[2] = lax.optimization_barrier(
        (cot_turned, crossed[0], crossed[2])
    )
    cot_all = copies_to(cot_turned, ZAX, 8)
    slab, near_w = unpack(place, [packed[0], *crossed])
    own = [slab] + [lax.ppermute(slab, "x", shift(d)) for d in range(1, 4)]
    swapped = [lax.ppermute(part, "c", FLIP) for part in own]
    first = first_partial(place, near_w, own, swapped)
    cot_all, first = lax.optimization_barrier((cot_all, first))
    piece, kept, acts = grad_piece(place, cot_all, own, swapped)

    beside = lax.ppermute(piece, "zl", FLIP)
    pieces = [in_hbm(kept)] + [lax.ppermute(piece, "y", shift(d)) for d in range(1, 4)]
    pieces += [beside, lax.ppermute(beside, "y", shift(1)), lax.ppermute(pieces[2], "zl", FLIP)]
    pieces += [lax.ppermute(beside, "y", shift(3))]
    first, *pieces[1:] = lax.optimization_barrier((first, *pieces[1:]))
    first_parts = lax.all_to_all(first, ZAX, 0, 0, tiled=True)
    new_left, new_right, update, *sent = solve(
        place, pieces, in_hbm(left_old[0, 0]), in_hbm(right_old[0, 0])
    )
    update_parts = [in_hbm(sent[0])] + [lax.ppermute(sent[d], "y", shift(d)) for d in range(1, 4)]
    second = second_partial(place, update_parts, acts)
    second, first_parts = lax.optimization_barrier((second, first_parts))
    arrived = lax.all_to_all(second, ZAX, 0, 0, tiled=True)
    outs, spread = second_add(place, first_add(place, first_parts), arrived)
    outs = lax.ppermute(outs, AXES, HOME)
    first_out, second_out = outs[0], outs[1]
    direction = update / spread[0, 0]
    return (first_out, new_left[None, None], new_right[None, None], direction, second_out)


def solution(mesh):
    fine = Mesh(mesh.devices.reshape(4, 2, 4, 2, 4), AXES)
    rows = ("zh", "zl", "y")
    in_specs = (
        P(BATCH, rows),
        P(rows, BATCH),
        P(rows, BATCH),
        P("zh", BATCH, None, None),
        P("zh", BATCH, None, None),
    )
    out_specs = (
        P(rows, BATCH),
        P("zh", BATCH, SOLVER, None),
        P("zh", BATCH, SOLVER, None),
        P(rows, BATCH),
        P(rows, BATCH),
    )
    return jax.shard_map(body, mesh=fine, in_specs=in_specs, out_specs=out_specs, check_vma=False)
```
